32 devices in a mesh: dp: 8 (over z, y), head: 4 (over x, core).
Axes of the slice: x: 2, y: 2, z: 4, core: 2. Of those that a mesh axis runs over, the one named last changes fastest.
Arguments:
- tokens: float32 [64, 512, 768], P('dp', 'head'), may hold values from -6 to 6
- segment: int32 [64, 512], P('dp'), may hold values from 0 to 3, never falling along the last dimension, each value on 1 to 256 neighbouring positions
- modality: int32 [64, 512], P('dp', 'head'), may hold values from 0 to 1, as said below
- first_gain: float32 [2, 768], replicated, may hold values from 0.1 to 1.9
- first_shift: float32 [2, 768], replicated, may hold values from -1 to 1
- project_in: bfloat16 [768, 2304], replicated, may hold values from -0.21875 to 0.21875
- project_out: bfloat16 [768, 768], replicated, may hold values from -1.75 to 1.75
- second_gain: float32 [2, 768], replicated, may hold values from 0.1 to 1.9
- second_shift: float32 [2, 768], replicated, may hold values from -1 to 1
- up_weight: bfloat16 [2, 768, 3072], replicated, may hold values from -0.21875 to 0.21875
- down_weight: bfloat16 [2, 3072, 768], replicated, may hold values from -0.109375 to 0.109375
- cotangent: float32 [64, 512, 768], P('dp', 'head'), may hold values from -6 to 6
Outputs:
- output: float32 [64, 512, 768], P('dp', 'head')
- input_grad: float32 [64, 512, 768], P('dp', 'head')
- first_gain_grad: float32 [2, 768], P(None, 'dp')
- first_shift_grad: float32 [2, 768], P(None, 'dp')
- project_in_grad: float32 [768, 2304], P('dp')
- project_out_grad: float32 [768, 768], P('dp')
- second_gain_grad: float32 [2, 768], P(None, 'dp')
- second_shift_grad: float32 [2, 768], P(None, 'dp')
- up_weight_grad: float32 [2, 768, 3072], P(None, 'dp')
- down_weight_grad: float32 [2, 3072, 768], P(None, 'dp')
The draws below stay inside these ranges and needn't reach their ends.
Inputs may be any that keep to these rules, and one draw needn't show every extreme that they name: Along each row segment numbers never fall; each segment is a run of 1 to 256 positions, and some run has exactly that many. On every device exactly 640 of its 1024 tokens have one modality and the others have the other one; which one is the larger varies by device.
All inputs are finite; a program needn't handle non-finite values.
Results may differ from the reference program's by a relative error of at most 0.015.
Values may be sent and summed in bfloat16 or wider, within the bound.
A program may use at most 320 MiB of HBM per device.

```python
import math
import jax
import jax.numpy as jnp
import numpy as np
from jax import lax

D = 768
HEADS = 12
HEAD_DIM = 64
FF = 3072
EXPERTS = 2
SEQ = 512
ROWS_GRP = 8
ROWS = 64
TOK_ROW = 128


def draw_modality(key, part):
    group_count = ROWS // ROWS_GRP
    cell_count = SEQ // TOK_ROW
    larger = jax.random.randint(jax.random.fold_in(key, 11), (group_count, cell_count), 0, 2)
    heavy = 5 * TOK_ROW // 8
    language = jnp.where(larger == 0, heavy, TOK_ROW - heavy)
    language = jnp.repeat(language, ROWS_GRP, axis=0)
    scores = jax.random.randint(jax.random.fold_in(key, 12), (ROWS, cell_count, TOK_ROW), 0, 1 << 20)
    scores = scores * TOK_ROW + jnp.arange(TOK_ROW, dtype=jnp.int32)
    ranks = jnp.argsort(jnp.argsort(scores, axis=-1), axis=-1)
    chosen = jnp.where(ranks < language[:, :, None], 0, 1)
    return chosen.astype(jnp.int32).reshape(ROWS, SEQ)


def block_scale(own_key, extent, shards, low, top_value):
    factor_of, own = 1.0, jax.random.fold_in(own_key, 6)
    for dim, blocks in shards:
        heights = jnp.exp(jax.random.uniform(jax.random.fold_in(own, dim), (blocks,), jnp.float32, low / len(shards), top_value / len(shards)))
        factor_of = factor_of * jnp.repeat(heights, extent[dim] // blocks).reshape([-1 if axis == dim else 1 for axis in range(len(extent))])
    return factor_of


def profile(amount, total, most, slope):
    weights = [(1 << 20) // math.isqrt(grade ** slope) + 1 for grade in range(2, amount + 1)]
    rest, given = total - most - (amount - 1), [1] * (amount - 1)
    while rest > 0:
        free = [i for i in range(amount - 1) if given[i] < most]
        mass, remaining = sum([weights[i] for i in free]), rest
        for i in free:
            more = min(most - given[i], max(1, remaining * weights[i] // mass), rest)
            given[i] = given[i] + more
            rest = rest - more
    return np.array([most] + given)


def uneven_parts(rng, count, total, most, slope):
    if count == 2:
        one = jax.random.randint(rng, (), max(1, total - most), min(most, total - 1) + 1)
        return jnp.stack([one, total - one])
    lengths = jnp.asarray(profile(count, total, most, slope), jnp.int32)
    twos = (count - 1) // 2
    source_of, sink = lengths[1:1 + 2 * twos:2], lengths[2:2 + 2 * twos:2]
    margin = jnp.minimum(source_of - 1, most - sink)
    shifted = jax.random.randint(jax.random.fold_in(rng, 1), (twos,), 0, 1 << 20) % (margin + 1)
    lengths = lengths.at[1:1 + 2 * twos:2].set(source_of - shifted).at[2:2 + 2 * twos:2].set(sink + shifted)
    return lengths[jax.random.permutation(jax.random.fold_in(rng, 2), count)]


def centred(key, extent, scale, reach, shards=(), kind=jnp.bfloat16):
    result = scale * jax.random.normal(key, extent, jnp.float32)
    if shards:
        result = result * block_scale(key, extent, shards, -0.22, 0.18)
    return jnp.clip(result, -reach, reach).astype(kind)


def setup_inputs(seed: int = 0) -> dict:
    arg_keys = jax.random.split(jax.random.key(seed), 13)
    return {
        "tokens": centred(arg_keys[0], (ROWS, SEQ, D), 1.0, 6.0, ((0, 8), (1, 4)), jnp.float32),
        "segment": jax.vmap(lambda own: jnp.searchsorted(jnp.cumsum(uneven_parts(own, 4, SEQ, SEQ // 2, 0)), jnp.arange(SEQ), side="right"))(jax.random.split(arg_keys[1], ROWS)).reshape((ROWS, SEQ)).astype(jnp.int32),
        "modality": draw_modality(jax.random.fold_in(arg_keys[12], 71), 0),
        "first_gain": jnp.clip(1.0 + 0.18 * jax.random.normal(arg_keys[3], (EXPERTS, D), jnp.float32), 0.1, 1.9),
        "first_shift": centred(arg_keys[4], (EXPERTS, D), 0.2, 1.0, (), jnp.float32),
        "project_in": centred(arg_keys[5], (D, 3 * D), D ** -0.5, 0.21875),
        "project_out": centred(arg_keys[6], (D, D), (D // 64) ** -0.5, 1.75),
        "second_gain": jnp.clip(1.0 + 0.18 * jax.random.normal(arg_keys[7], (EXPERTS, D), jnp.float32), 0.1, 1.9),
        "second_shift": centred(arg_keys[8], (EXPERTS, D), 0.2, 1.0, (), jnp.float32),
        "up_weight": centred(arg_keys[9], (EXPERTS, D, FF), D ** -0.5, 0.21875),
        "down_weight": centred(arg_keys[10], (EXPERTS, FF, D), FF ** -0.5, 0.109375),
        "cotangent": centred(arg_keys[11], (ROWS, SEQ, D), 1.0, 6.0, ((0, 8), (1, 4)), jnp.float32),
    }


@jax.custom_vjp
def low(v):
    return lax.optimization_barrier(v.astype(jnp.bfloat16)).astype(jnp.float32)

@jax.custom_vjp
def low_back(v):
    return v

def low_keep(v):
    return (low(v), None)

def low_pass(kept, grad):
    return (grad,)

def back_keep(v):
    return (v, None)

def back_low(kept, grad):
    return (low(grad),)
low.defvjp(low_keep, low_pass)
low_back.defvjp(back_keep, back_low)
highest = lax.Precision.HIGHEST
epsilon = 1e-05

def layer_norm(inputs, gains, shifts):
    centered = inputs - lax.optimization_barrier(jnp.mean(inputs, axis=-1, keepdims=True))
    variance = lax.optimization_barrier(jnp.mean(centered * centered, axis=-1, keepdims=True))
    return centered * lax.rsqrt(variance + epsilon) * gains + shifts

def pick(expert_table, modality):
    return jnp.where(modality[..., None] == 0, expert_table[0], expert_table[1])

def forward_rows(tokens, segment, modality, first_gain, first_shift, project_in, project_out, second_gain, second_shift, up_weight, down_weight):
    row_count = tokens.shape[0]
    first_normed = low(layer_norm(tokens, pick(first_gain, modality), pick(first_shift, modality)))
    projected = low(low_back(jnp.einsum('rsd,df->rsf', first_normed, project_in, precision=highest)))
    query = projected[:, :, :D].reshape(row_count, SEQ, HEADS, HEAD_DIM) * HEAD_DIM ** (-0.5)
    keys = projected[:, :, D:2 * D].reshape(row_count, SEQ, HEADS, HEAD_DIM)
    values = projected[:, :, 2 * D:].reshape(row_count, SEQ, HEADS, HEAD_DIM)
    scores = low_back(jnp.einsum('rqhc,rkhc->rhqk', query, keys, precision=highest))
    same_segment = (segment[:, :, None] == segment[:, None, :])[:, None]
    masked = jnp.where(same_segment, scores, -1000000000.0)
    probs = jax.nn.softmax(masked, axis=-1)
    context = jnp.einsum('rhqk,rkhc->rqhc', low(probs), values, precision=highest).reshape(row_count, SEQ, D)
    context = low(low_back(context))
    attention = low_back(jnp.einsum('rsd,de->rse', context, project_out, precision=highest))
    residual = tokens + attention
    second_normed = low(layer_norm(residual, pick(second_gain, modality), pick(second_shift, modality)))
    branch_sum = jnp.zeros_like(residual)
    for expert in range(EXPERTS):
        hidden = low_back(jnp.einsum('rsd,df->rsf', second_normed, up_weight[expert], precision=highest))
        activated = low(jax.nn.gelu(hidden, approximate=False))
        branch = low_back(jnp.einsum('rsf,fd->rsd', activated, down_weight[expert], precision=highest))
        branch_sum = branch_sum + jnp.where(modality[..., None] == expert, branch, 0.0)
    return residual + branch_sum

def reference(tokens, segment, modality, first_gain, first_shift, project_in, project_out, second_gain, second_shift, up_weight, down_weight, cotangent):
    block_count = ROWS // ROWS_GRP

    def whole(tokens, first_gain, first_shift, project_in, project_out, second_gain, second_shift, up_weight, down_weight):

        def one_block(items):
            return forward_rows(items[0], items[1], items[2], first_gain, first_shift, project_in, project_out, second_gain, second_shift, up_weight, down_weight)
        stacked = (tokens.reshape(block_count, ROWS_GRP, SEQ, D), segment.reshape(block_count, ROWS_GRP, SEQ), modality.reshape(block_count, ROWS_GRP, SEQ))
        return lax.map(jax.checkpoint(one_block), stacked).reshape(ROWS, SEQ, D)
    output, pullback = jax.vjp(whole, tokens, first_gain, first_shift, project_in.astype(jnp.float32), project_out.astype(jnp.float32), second_gain, second_shift, up_weight.astype(jnp.float32), down_weight.astype(jnp.float32))
    grads = pullback(cotangent)
    return (output, grads[0], grads[1], grads[2], grads[3], grads[4], grads[5], grads[6], grads[7], grads[8])
```

```python
import functools

import jax
import jax.numpy as jnp
from jax import lax
from jax.experimental import pallas as pl
from jax.experimental.pallas import tpu as pltpu
from jax.sharding import PartitionSpec as P

HEAD_DIM = 64
EXPERTS = 2
EPS = 1e-05
NEG = -1000000000.0
BLK = 128
CALLS = 2
VMEM_BYTES = 60 * 1024 * 1024
BF = jnp.bfloat16
F32 = jnp.float32
NT = (((1,), (1,)), ((), ()))
TN = (((0,), (0,)), ((), ()))


def mm(a, b):
    return jnp.dot(a, b, preferred_element_type=F32)


def mm_nt(a, b):
    return lax.dot_general(a, b, NT, preferred_element_type=F32)


def mm_tn(a, b):
    return lax.dot_general(a, b, TN, preferred_element_type=F32)


def bias_of(segc_ref, segr_ref, bias_ref):
    same = segc_ref[0] == segr_ref[0]
    bias_ref[...] = jnp.where(same, 0.0, NEG)


def attn_fwd_kernel(segc_ref, segr_ref, q_ref, k_ref, v_ref, o_ref, bias_ref):
    sub, _, length, width = q_ref.shape
    seq = sub * length

    @pl.when(pl.program_id(1) == 0)
    def _():
        bias_of(segc_ref, segr_ref, bias_ref)

    q = q_ref[...].reshape(seq, width) * jnp.asarray(HEAD_DIM**-0.5, BF)
    k = k_ref[...].reshape(seq, width)
    v = v_ref[...].reshape(seq, width)
    lane = lax.broadcasted_iota(jnp.int32, (1, width), 1) // HEAD_DIM
    zero = jnp.zeros((), BF)
    per = width // HEAD_DIM
    ks = [jnp.where(lane == h, k, zero) for h in range(per)]
    vs = [jnp.where(lane == h, v, zero) for h in range(per)]
    for b in range(sub):
        rows = slice(b * length, (b + 1) * length)
        total = None
        for h in range(per):
            s = mm_nt(q[rows], ks[h]) + bias_ref[rows, :]
            e = jnp.exp(s - jnp.max(s, axis=-1, keepdims=True))
            inv = 1.0 / jnp.sum(e, axis=-1, keepdims=True)
            o = mm(e.astype(BF), vs[h]) * inv
            total = o if total is None else total + o
        o_ref[b, 0] = total.astype(BF)


def attn_bwd_kernel(segc_ref, segr_ref, q_ref, k_ref, v_ref, do_ref, out_ref, bias_ref):
    sub, _, length, width = q_ref.shape
    seq = sub * length
    model = out_ref.shape[-1] // 3
    j = pl.program_id(1)

    @pl.when(j == 0)
    def _():
        bias_of(segc_ref, segr_ref, bias_ref)

    scale = HEAD_DIM**-0.5
    q = q_ref[...].reshape(seq, width) * jnp.asarray(scale, BF)
    k = k_ref[...].reshape(seq, width)
    v = v_ref[...].reshape(seq, width)
    do = do_ref[...].reshape(seq, width)
    lane = lax.broadcasted_iota(jnp.int32, (1, width), 1) // HEAD_DIM
    zero = jnp.zeros((), BF)
    per = width // HEAD_DIM
    step = 2 * length
    dk = jnp.zeros((seq, width), F32)
    dv = jnp.zeros((seq, width), F32)
    dqs = [jnp.zeros((step, width), F32) for _ in range(seq // step)]
    for h in range(per):
        kh = jnp.where(lane == h, k, zero)
        vh = jnp.where(lane == h, v, zero)
        qh = jnp.where(lane == h, q, zero)
        doh = jnp.where(lane == h, do, zero)
        for b in range(seq // step):
            cols = slice(b * step, (b + 1) * step)
            s = mm_nt(kh, q[cols]) + bias_ref[:, cols]
            e = jnp.exp(s - jnp.max(s, axis=0, keepdims=True))
            p = e * (1.0 / jnp.sum(e, axis=0, keepdims=True))
            dp = mm_nt(vh, do[cols])
            ds = (p * (dp - jnp.sum(p * dp, axis=0, keepdims=True))).astype(BF)
            dv = dv + mm(p.astype(BF), doh[cols])
            dk = dk + mm(ds, qh[cols])
            dqs[b] = dqs[b] + mm_tn(ds, kh)
    dq = jnp.concatenate([d * scale for d in dqs], axis=0)
    for i, g in enumerate((dq, dk, dv)):
        at = pl.multiple_of(i * model + j * width, width)
        out_ref[:, :, :, pl.ds(at, width)] = g.astype(BF).reshape(sub, 1, length, width)


def attn_specs(sub, length, pairs):
    def part(i):
        return pl.BlockSpec((sub, 1, length, 128), lambda r, j, i=i: (0, r, 0, i * pairs + j))

    return part


def attention_forward(segment, qkv):
    sub, rows, length, wide = qkv.shape
    seq = sub * length
    model = wide // 3
    pairs = model // 128
    part = attn_specs(sub, length, pairs)
    return pl.pallas_call(
        attn_fwd_kernel,
        grid=(rows, pairs),
        in_specs=[
            pl.BlockSpec((1, seq, 1), lambda r, j: (r, 0, 0)),
            pl.BlockSpec((1, 1, seq), lambda r, j: (r, 0, 0)),
            part(0),
            part(1),
            part(2),
        ],
        out_specs=part(0),
        out_shape=jax.ShapeDtypeStruct((sub, rows, length, model), BF),
        scratch_shapes=[pltpu.VMEM((seq, seq), F32)],
        compiler_params=pltpu.CompilerParams(vmem_limit_bytes=VMEM_BYTES),
        cost_estimate=pl.CostEstimate(
            flops=8 * rows * seq * seq * model, bytes_accessed=8 * rows * seq * model,
            transcendentals=rows * seq * seq * model // HEAD_DIM,
        ),
        name="attn_fwd",
    )(segment[:, :, None], segment[:, None, :], qkv, qkv, qkv)


def attention_backward(segment, qkv, grad):
    sub, rows, length, wide = qkv.shape
    seq = sub * length
    model = wide // 3
    pairs = model // 128
    part = attn_specs(sub, length, pairs)
    return pl.pallas_call(
        attn_bwd_kernel,
        grid=(rows, pairs),
        in_specs=[
            pl.BlockSpec((1, seq, 1), lambda r, j: (r, 0, 0)),
            pl.BlockSpec((1, 1, seq), lambda r, j: (r, 0, 0)),
            part(0),
            part(1),
            part(2),
            part(0),
        ],
        out_specs=pl.BlockSpec((sub, 1, length, wide), lambda r, j: (0, r, 0, 0)),
        out_shape=jax.ShapeDtypeStruct(qkv.shape, BF),
        scratch_shapes=[pltpu.VMEM((seq, seq), F32)],
        compiler_params=pltpu.CompilerParams(vmem_limit_bytes=VMEM_BYTES),
        cost_estimate=pl.CostEstimate(
            flops=20 * rows * seq * seq * model, bytes_accessed=14 * rows * seq * model,
            transcendentals=rows * seq * seq * model // HEAD_DIM,
        ),
        name="attn_bwd",
    )(segment[:, :, None], segment[:, None, :], qkv, qkv, qkv, grad)


def ffn_kernel(first, info_ref, xm_ref, xo_ref, gm_ref, go_ref, u_ref, d_ref, *refs):
    if first:
        prev = (None,) * 4
        outs, (ga_ref, gb_ref) = refs[:4], refs[4:6]
    else:
        prev, outs, (ga_ref, gb_ref) = refs[:4], refs[4:8], refs[8:10]
    du_ref, dd_ref, act_ref, dh_ref = refs[-4:]
    e = pl.program_id(0)
    slots, model = xm_ref.shape
    cols = u_ref.shape[-1]
    tile = 256
    down = d_ref[...].reshape(cols, model)

    @pl.when(e == 0)
    def _():
        for out in outs:
            out[slots - BLK :, :] = jnp.zeros((BLK, model), BF)

    du_ref[...] = jnp.zeros_like(du_ref)
    dd_ref[...] = jnp.zeros_like(dd_ref)

    def chunk(which, block, count):
        size = count * BLK
        rows = pl.ds(pl.multiple_of(block * BLK, BLK), size)
        x = (xm_ref, xo_ref)[which][rows, :]
        g = (gm_ref, go_ref)[which][rows, :]
        for n in range(cols // tile):
            part = slice(n * tile, (n + 1) * tile)
            h = mm(x, u_ref[0, :, part])
            da = mm_nt(g, down[part, :])
            cdf = 0.5 + 0.5 * lax.erf(h * 0.7071067811865476)
            pdf = 0.3989422804014327 * jnp.exp(-0.5 * h * h)
            act_ref[:size, part] = (h * cdf).astype(BF)
            dh_ref[:size, part] = (da * (cdf + h * pdf)).astype(BF)
        act = act_ref[:size, :]
        dh = dh_ref[:size, :]
        for slot, value in ((which, mm(act, down)), (2 + which, mm_nt(dh, u_ref[0]))):
            if prev[slot] is not None:
                value = value + prev[slot][rows, :].astype(F32)
            outs[slot][rows, :] = value.astype(BF)
        du_ref[...] += mm_tn(x, dh)
        dd_ref[...] += mm_tn(act, g)

    for which in range(2):
        n0 = info_ref[2 * which]
        n1 = info_ref[2 * which + 1]
        start = jnp.where(e == 0, 0, n0)
        count = jnp.where(e == 0, n0, n1)

        def four(i, carry, which=which, start=start):
            chunk(which, start + 4 * i, 4)
            return carry

        lax.fori_loop(0, count // 4, four, 0)
        at2 = start + (count // 4) * 4

        @pl.when((count // 2) % 2 == 1)
        def _(which=which, at2=at2):
            chunk(which, at2, 2)

        at1 = start + (count // 2) * 2

        @pl.when(count % 2 == 1)
        def _(which=which, at1=at1):
            chunk(which, at1, 1)

    xbit = info_ref[4]
    ybit = info_ref[5]
    quarter = gb_ref.shape[3]

    @pl.when(e == 0)
    def _():
        ga_ref[xbit] = du_ref[...].astype(BF)
        ga_ref[1 - xbit] = dd_ref[...].astype(BF)

    @pl.when(e == 1)
    def _():
        for w, ref in enumerate((du_ref, dd_ref)):
            for z in range(gb_ref.shape[2]):
                for y in range(2):
                    at = (2 * z + y) * quarter
                    value = ref[at : at + quarter, :].astype(BF)
                    gb_ref[y ^ ybit, w, z] = value


def ffn(call, core, info, x_mine, x_other, g_mine, g_other, up, down, partial, groups):
    slots, model = x_mine.shape
    cols = up.shape[-1]
    per = cols // groups
    whole = pl.BlockSpec((slots, model), lambda e, i: (0, 0), pipeline_mode=pl.Buffered(1))
    first = partial is None
    extra = () if first else tuple(partial)
    return pl.pallas_call(
        functools.partial(ffn_kernel, first),
        grid_spec=pltpu.PrefetchScalarGridSpec(
            num_scalar_prefetch=1,
            grid=(EXPERTS,),
            in_specs=[whole] * 4
            + [
                pl.BlockSpec((1, model, cols), lambda e, i: (e, 0, 0)),
                pl.BlockSpec(
                    (1, groups, 1, 1, per, model), lambda e, i: (e, 0, i[6], call, 0, 0)
                ),
            ]
            + [whole] * len(extra),
            out_specs=[pl.BlockSpec((slots, model), lambda e, i: (0, 0))] * 4
            + [
                pl.BlockSpec((2, model, cols), lambda e, i: (0, 0, 0)),
                pl.BlockSpec((2, 2, groups // 2, per, model), lambda e, i: (0, 0, 0, 0, 0)),
            ],
            scratch_shapes=[
                pltpu.VMEM((model, cols), F32),
                pltpu.VMEM((cols, model), F32),
                pltpu.VMEM((4 * BLK, cols), BF),
                pltpu.VMEM((4 * BLK, cols), BF),
            ],
        ),
        out_shape=[jax.ShapeDtypeStruct((slots, model), BF)] * 4
        + [
            jax.ShapeDtypeStruct((2, model, cols), BF),
            jax.ShapeDtypeStruct((2, 2, groups // 2, per, model), BF),
        ],
        compiler_params=pltpu.CompilerParams(vmem_limit_bytes=VMEM_BYTES),
        cost_estimate=pl.CostEstimate(
            flops=12 * 2 * slots * model * cols, bytes_accessed=40 * 1024 * 1024,
            transcendentals=2 * 2 * slots * cols,
        ),
        name="ffn",
    )(info, x_mine, x_other, g_mine, g_other, up, down, *extra)


def norm(values):
    mean = jnp.mean(values, axis=-1, keepdims=True)
    centered = values - mean
    rstd = lax.rsqrt(jnp.mean(centered * centered, axis=-1, keepdims=True) + EPS)
    return centered * rstd, rstd


def pick(table, kind):
    return jnp.where(kind == 0, table[0], table[1])


def norm_back(grad, gains, z, rstd):
    q = grad * gains
    return rstd * (
        q
        - jnp.mean(q, axis=-1, keepdims=True)
        - z * jnp.mean(q * z, axis=-1, keepdims=True)
    )


def by_expert(values, kind):
    first = jnp.sum(jnp.where(kind == 0, values, 0.0), axis=0)
    second = jnp.sum(jnp.where(kind == 0, 0.0, values), axis=0)
    return jnp.stack([first, second])


def flip(axis, size, bit):
    return functools.partial(
        lax.ppermute, axis_name=axis, perm=[(i, i ^ (1 << bit)) for i in range(size)]
    )


def take(values, dim, index):
    return lax.dynamic_index_in_dim(values, index, dim, keepdims=False)


def body(sizes, tokens, segment, modality, first_gain, first_shift, project_in, project_out,
         second_gain, second_shift, up_weight, down_weight, cotangent):
    heads, groups = sizes["head"], sizes["dp"]
    row_count, length, model = tokens.shape
    rows = row_count // heads
    count = row_count * length
    hidden = up_weight.shape[-1]
    me_h, me_d = lax.axis_index("head"), lax.axis_index("dp")
    core = me_h % 2
    head_bits = heads.bit_length() - 1
    dp_bits = groups.bit_length() - 1
    assert heads == 1 << head_bits and groups == 1 << dp_bits and head_bits >= 2
    hflip = [flip("head", heads, b) for b in range(head_bits)]
    dflip = [flip("dp", groups, b) for b in range(dp_bits)]

    def exchange(values):
        return lax.all_to_all(values, "head", split_axis=0, concat_axis=0, tiled=True)

    grid = (heads, rows, length)
    tok = exchange(tokens.astype(BF).reshape(*grid, model))
    kind = exchange(modality.reshape(grid)).reshape(count)
    cot = exchange(cotangent.astype(BF).reshape(*grid, model)).reshape(count, model)
    seg = lax.dynamic_slice_in_dim(segment, me_h * rows, rows, 0)
    kcol = kind[:, None]

    per = hidden // (groups * 2 * CALLS)
    up_own = take(up_weight.reshape(EXPERTS, model, groups, 2, CALLS, per), 3, core)
    up_own = up_own.transpose(3, 0, 1, 2, 4).reshape(CALLS, EXPERTS, model, groups * per)
    down_view = down_weight.reshape(EXPERTS, groups, 2, CALLS, per, model)

    flat = tok.astype(F32).reshape(count, model)
    z1, rstd1 = norm(flat)
    gain1 = pick(first_gain, kcol)
    low1 = (z1 * gain1 + pick(first_shift, kcol)).astype(BF)
    qkv = mm(low1, project_in).astype(BF).reshape(*grid, 3 * model)
    context = attention_forward(seg, qkv)
    ctx = context.reshape(count, model)
    attention = mm(ctx, project_out)
    residual = flat + attention
    z2, rstd2 = norm(residual)
    gain2 = pick(second_gain, kcol)
    low2 = (z2 * gain2 + pick(second_shift, kcol)).astype(BF)

    slots = count + BLK
    is0 = (kind == 0).astype(F32).reshape(count // BLK, BLK)
    tri = jnp.triu(jnp.ones((BLK, BLK), F32))
    inner = mm(is0, tri)
    ends = jnp.cumsum(inner[:, -1])
    before = (inner + (ends - inner[:, -1])[:, None]).reshape(count).astype(jnp.int32)
    n0 = ends[-1].astype(jnp.int32)
    blocks0 = (n0 + BLK - 1) // BLK
    blocks1 = (count - n0 + BLK - 1) // BLK
    rank1 = jnp.arange(count, dtype=jnp.int32) - before
    slot = jnp.where(kind == 0, before - 1, blocks0 * BLK + rank1)
    place = (slot[None, :] == jnp.arange(slots, dtype=jnp.int32)[:, None]).astype(BF)

    near = hflip[0]
    g_mine = mm(place, cot).astype(BF)
    g_other = near(g_mine)
    blocks = jnp.stack([blocks0, blocks1])
    blocks_other = near(blocks)
    xbit = (me_h // 2) % 2
    ybit = me_d % 2
    info = jnp.concatenate([blocks, blocks_other, jnp.stack([xbit, ybit, core])]).astype(jnp.int32)
    x_mine = mm(place, low2).astype(BF)
    x_other = near(x_mine)

    def split(values, bit, index):
        tail = values[0].shape
        shaped = [v.reshape(*tail[:1], -1, 2, *tail[2:]) if False else v for v in values]
        del tail, shaped
        keep = sum(take(v, bit, index).astype(F32) for v in values).astype(BF)
        send = sum(take(v, bit, 1 - index).astype(F32) for v in values).astype(BF)
        return keep, send

    dbit = [(me_d >> b) % 2 for b in range(dp_bits)]
    hbit = [(me_h >> b) % 2 for b in range(head_bits)]

    def reduce_dp(values, done):
        live = [b for b in range(dp_bits) if b not in done]
        for i, b in enumerate(live):
            dim = 1 + (len(live) - 1 - i)
            keep, send = split(values, dim, dbit[b])
            values = (keep, dflip[b](send))
        return sum(v.astype(F32) for v in values).astype(BF)

    def bits(n):
        return (2,) * n

    partial, pieces = None, []
    for call in range(CALLS):
        *partial, ga, gb = ffn(
            call, core, info, x_mine, x_other, g_mine, g_other, up_own[call], down_view, partial,
            groups,
        )
        keep, got = ga[0], hflip[1](ga[1])
        shape = (1, *bits(dp_bits), per, model)
        mine_a = reduce_dp((keep.reshape(shape), got.reshape(shape)), ())[0]
        keep, got = gb[0], dflip[0](gb[1])
        keep, send = split((keep, got), 0, xbit)
        got = hflip[1](send)
        shape = (1, *bits(dp_bits - 1), per, model)
        mine_b = reduce_dp((keep.reshape(shape), got.reshape(shape)), (0,))[0]
        pieces.append(jnp.stack([mine_a, mine_b]))

    sums = jnp.stack(pieces)
    sums_x = hflip[1](sums)
    both = jnp.where(xbit == 0, jnp.stack([sums, sums_x]), jnp.stack([sums_x, sums]))
    both_c = near(both)
    full = jnp.where(core == 0, jnp.stack([both, both_c]), jnp.stack([both_c, both]))
    up_grad = full[:, 0].reshape(2, CALLS, EXPERTS, model // groups, groups, per)
    up_grad = up_grad.transpose(2, 3, 4, 0, 1, 5).reshape(EXPERTS, model // groups, hidden)
    up_grad = up_grad.astype(F32)
    down_grad = full[:, 1].transpose(2, 0, 1, 3, 4).reshape(EXPERTS, hidden // groups, model)
    down_grad = down_grad.astype(F32)

    branch_mine, branch_other, dx_mine, dx_other = partial
    dx = dx_mine + near(dx_other)
    second_grad = mm_tn(place, dx)
    branch = mm_tn(place, branch_mine + near(branch_other))
    back = exchange((attention + branch).astype(BF).reshape(*grid, model))
    output = tokens + back.reshape(row_count, length, model).astype(F32)

    cot32 = cot.astype(F32)
    gain2_term = by_expert(second_grad * z2, kcol)
    shift2_term = by_expert(second_grad, kcol)
    extra = norm_back(second_grad, gain2, z2, rstd2)
    attention_low = (cot32 + extra).astype(BF)
    out_term = mm_tn(ctx, attention_low)
    context_grad = mm_nt(attention_low, project_out).astype(BF)
    dqkv = attention_backward(seg, qkv, context_grad.reshape(context.shape)).reshape(count, 3 * model)
    first_grad = mm_nt(dqkv, project_in)
    in_term = mm_tn(low1, dqkv)
    gain1_term = by_expert(first_grad * z1, kcol)
    shift1_term = by_expert(first_grad, kcol)
    tail = (extra + norm_back(first_grad, gain1, z1, rstd1)).astype(BF)
    home = exchange(tail.reshape(*grid, model))
    input_grad = cotangent + home.reshape(row_count, length, model).astype(F32)

    small = jnp.stack([gain1_term, shift1_term, gain2_term, shift2_term]).reshape(8, groups, model // groups)
    small = jnp.pad(small.transpose(1, 2, 0), ((0, 0), (0, 0), (0, 120)))
    low = jnp.concatenate(
        [t.reshape(groups, model // groups, -1).astype(BF) for t in (in_term, out_term, small)],
        axis=-1,
    )
    wide = low.shape[-1]
    lanes = low.reshape(groups, 2, 2, model // groups // 4, wide)
    keep, send = split((lanes,), 1, core)
    keep, send = split((keep, near(send)), 1, xbit)
    got = hflip[1](send)
    shape = (1, *bits(dp_bits), model // groups // 4, wide)
    part = reduce_dp((keep.reshape(shape), got.reshape(shape)), ())[0]
    part_x = hflip[1](part)
    pair = jnp.where(xbit == 0, jnp.stack([part, part_x]), jnp.stack([part_x, part]))
    pair_c = near(pair)
    whole = jnp.where(core == 0, jnp.stack([pair, pair_c]), jnp.stack([pair_c, pair]))
    whole = whole.reshape(model // groups, wide).astype(F32)
    in_grad = whole[:, : 3 * model]
    out_grad = whole[:, 3 * model : 4 * model]
    tables = whole[:, 4 * model : 4 * model + 8].T.reshape(4, EXPERTS, model // groups)
    return (
        output, input_grad, tables[0], tables[1], in_grad, out_grad, tables[2], tables[3],
        up_grad, down_grad,
    )


def solution(mesh):
    return jax.shard_map(
        functools.partial(body, dict(mesh.shape)),
        mesh=mesh,
        in_specs=(
            P("dp", "head", None),
            P("dp", None),
            P("dp", "head"),
            P(),
            P(),
            P(),
            P(),
            P(),
            P(),
            P(),
            P(),
            P("dp", "head", None),
        ),
        out_specs=(
            P("dp", "head", None),
            P("dp", "head", None),
            P(None, "dp"),
            P(None, "dp"),
            P("dp", None),
            P("dp", None),
            P(None, "dp"),
            P(None, "dp"),
            P(None, "dp", None),
            P(None, "dp", None),
        ),
        check_vma=False,
    )
```

```python
import functools

import jax
import jax.numpy as jnp
from jax import lax
from jax.experimental import pallas as pl
from jax.experimental.pallas import tpu as pltpu
from jax.sharding import PartitionSpec as P

HEAD_DIM = 64
EXPERTS = 2
EPS = 1e-05
NEG = -1000000000.0
BLK = 128
CALLS = 2
VMEM_BYTES = 60 * 1024 * 1024
BF = jnp.bfloat16
F32 = jnp.float32
NT = (((1,), (1,)), ((), ()))
TN = (((0,), (0,)), ((), ()))


def mm(a, b):
    return jnp.dot(a, b, preferred_element_type=F32)


def mm_nt(a, b):
    return lax.dot_general(a, b, NT, preferred_element_type=F32)


def mm_tn(a, b):
    return lax.dot_general(a, b, TN, preferred_element_type=F32)


def bias_of(segc_ref, segr_ref, bias_ref):
    same = segc_ref[0] == segr_ref[0]
    bias_ref[...] = jnp.where(same, 0.0, NEG)


def attn_fwd_kernel(segc_ref, segr_ref, q_ref, k_ref, v_ref, o_ref, bias_ref):
    sub, _, length, width = q_ref.shape
    seq = sub * length

    @pl.when(pl.program_id(1) == 0)
    def _():
        bias_of(segc_ref, segr_ref, bias_ref)

    q = q_ref[...].reshape(seq, width) * jnp.asarray(HEAD_DIM**-0.5, BF)
    k = k_ref[...].reshape(seq, width)
    v = v_ref[...].reshape(seq, width)
    lane = lax.broadcasted_iota(jnp.int32, (1, width), 1) // HEAD_DIM
    zero = jnp.zeros((), BF)
    per = width // HEAD_DIM
    ks = [jnp.where(lane == h, k, zero) for h in range(per)]
    vs = [jnp.where(lane == h, v, zero) for h in range(per)]
    for b in range(sub):
        rows = slice(b * length, (b + 1) * length)
        total = None
        for h in range(per):
            s = mm_nt(q[rows], ks[h]) + bias_ref[rows, :]
            e = jnp.exp(s - jnp.max(s, axis=-1, keepdims=True))
            inv = 1.0 / jnp.sum(e, axis=-1, keepdims=True)
            o = mm(e.astype(BF), vs[h]) * inv
            total = o if total is None else total + o
        o_ref[b, 0] = total.astype(BF)


def attn_bwd_kernel(segc_ref, segr_ref, q_ref, k_ref, v_ref, do_ref, out_ref, bias_ref):
    sub, _, length, width = q_ref.shape
    seq = sub * length
    model = out_ref.shape[-1] // 3
    j = pl.program_id(1)

    @pl.when(j == 0)
    def _():
        bias_of(segc_ref, segr_ref, bias_ref)

    scale = HEAD_DIM**-0.5
    q = q_ref[...].reshape(seq, width) * jnp.asarray(scale, BF)
    k = k_ref[...].reshape(seq, width)
    v = v_ref[...].reshape(seq, width)
    do = do_ref[...].reshape(seq, width)
    lane = lax.broadcasted_iota(jnp.int32, (1, width), 1) // HEAD_DIM
    zero = jnp.zeros((), BF)
    per = width // HEAD_DIM
    step = 2 * length
    dk = jnp.zeros((seq, width), F32)
    dv = jnp.zeros((seq, width), F32)
    dqs = [jnp.zeros((step, width), F32) for _ in range(seq // step)]
    for h in range(per):
        kh = jnp.where(lane == h, k, zero)
        vh = jnp.where(lane == h, v, zero)
        qh = jnp.where(lane == h, q, zero)
        doh = jnp.where(lane == h, do, zero)
        for b in range(seq // step):
            cols = slice(b * step, (b + 1) * step)
            s = mm_nt(kh, q[cols]) + bias_ref[:, cols]
            e = jnp.exp(s - jnp.max(s, axis=0, keepdims=True))
            p = e * (1.0 / jnp.sum(e, axis=0, keepdims=True))
            dp = mm_nt(vh, do[cols])
            ds = (p * (dp - jnp.sum(p * dp, axis=0, keepdims=True))).astype(BF)
            dv = dv + mm(p.astype(BF), doh[cols])
            dk = dk + mm(ds, qh[cols])
            dqs[b] = dqs[b] + mm_tn(ds, kh)
    dq = jnp.concatenate([d * scale for d in dqs], axis=0)
    for i, g in enumerate((dq, dk, dv)):
        at = pl.multiple_of(i * model + j * width, width)
        out_ref[:, :, :, pl.ds(at, width)] = g.astype(BF).reshape(sub, 1, length, width)


def attn_specs(sub, length, pairs):
    def part(i):
        return pl.BlockSpec((sub, 1, length, 128), lambda r, j, i=i: (0, r, 0, i * pairs + j))

    return part


def attention_forward(segment, qkv):
    sub, rows, length, wide = qkv.shape
    seq = sub * length
    model = wide // 3
    pairs = model // 128
    part = attn_specs(sub, length, pairs)
    return pl.pallas_call(
        attn_fwd_kernel,
        grid=(rows, pairs),
        in_specs=[
            pl.BlockSpec((1, seq, 1), lambda r, j: (r, 0, 0)),
            pl.BlockSpec((1, 1, seq), lambda r, j: (r, 0, 0)),
            part(0),
            part(1),
            part(2),
        ],
        out_specs=part(0),
        out_shape=jax.ShapeDtypeStruct((sub, rows, length, model), BF),
        scratch_shapes=[pltpu.VMEM((seq, seq), F32)],
        compiler_params=pltpu.CompilerParams(vmem_limit_bytes=VMEM_BYTES),
        cost_estimate=pl.CostEstimate(
            flops=8 * rows * seq * seq * model, bytes_accessed=8 * rows * seq * model,
            transcendentals=rows * seq * seq * model // HEAD_DIM,
        ),
        name="attn_fwd",
    )(segment[:, :, None], segment[:, None, :], qkv, qkv, qkv)


def attention_backward(segment, qkv, grad):
    sub, rows, length, wide = qkv.shape
    seq = sub * length
    model = wide // 3
    pairs = model // 128
    part = attn_specs(sub, length, pairs)
    return pl.pallas_call(
        attn_bwd_kernel,
        grid=(rows, pairs),
        in_specs=[
            pl.BlockSpec((1, seq, 1), lambda r, j: (r, 0, 0)),
            pl.BlockSpec((1, 1, seq), lambda r, j: (r, 0, 0)),
            part(0),
            part(1),
            part(2),
            part(0),
        ],
        out_specs=pl.BlockSpec((sub, 1, length, wide), lambda r, j: (0, r, 0, 0)),
        out_shape=jax.ShapeDtypeStruct(qkv.shape, BF),
        scratch_shapes=[pltpu.VMEM((seq, seq), F32)],
        compiler_params=pltpu.CompilerParams(vmem_limit_bytes=VMEM_BYTES),
        cost_estimate=pl.CostEstimate(
            flops=20 * rows * seq * seq * model, bytes_accessed=14 * rows * seq * model,
            transcendentals=rows * seq * seq * model // HEAD_DIM,
        ),
        name="attn_bwd",
    )(segment[:, :, None], segment[:, None, :], qkv, qkv, qkv, grad)


def ffn_kernel(first, info_ref, xm_ref, xo_ref, gm_ref, go_ref, u_ref, d_ref, *refs):
    if first:
        prev = (None,) * 4
        outs, (ga_ref, gb_ref) = refs[:4], refs[4:6]
    else:
        prev, outs, (ga_ref, gb_ref) = refs[:4], refs[4:8], refs[8:10]
    du_ref, dd_ref, act_ref, dh_ref = refs[-4:]
    e = pl.program_id(0)
    slots, model = xm_ref.shape
    cols = u_ref.shape[-1]
    tile = 256
    down = d_ref[...].reshape(cols, model)

    @pl.when(e == 0)
    def _():
        for out in outs:
            out[slots - BLK :, :] = jnp.zeros((BLK, model), BF)

    du_ref[...] = jnp.zeros_like(du_ref)
    dd_ref[...] = jnp.zeros_like(dd_ref)

    def chunk(which, block, count):
        size = count * BLK
        rows = pl.ds(pl.multiple_of(block * BLK, BLK), size)
        x = (xm_ref, xo_ref)[which][rows, :]
        g = (gm_ref, go_ref)[which][rows, :]
        for n in range(cols // tile):
            part = slice(n * tile, (n + 1) * tile)
            h = mm(x, u_ref[0, :, part])
            da = mm_nt(g, down[part, :])
            cdf = 0.5 + 0.5 * lax.erf(h * 0.7071067811865476)
            pdf = 0.3989422804014327 * jnp.exp(-0.5 * h * h)
            act_ref[:size, part] = (h * cdf).astype(BF)
            dh_ref[:size, part] = (da * (cdf + h * pdf)).astype(BF)
        act = act_ref[:size, :]
        dh = dh_ref[:size, :]
        for slot, value in ((which, mm(act, down)), (2 + which, mm_nt(dh, u_ref[0]))):
            if prev[slot] is not None:
                value = value + prev[slot][rows, :].astype(F32)
            outs[slot][rows, :] = value.astype(BF)
        du_ref[...] += mm_tn(x, dh)
        dd_ref[...] += mm_tn(act, g)

    for which in range(2):
        n0 = info_ref[2 * which]
        n1 = info_ref[2 * which + 1]
        start = jnp.where(e == 0, 0, n0)
        count = jnp.where(e == 0, n0, n1)

        def four(i, carry, which=which, start=start):
            chunk(which, start + 4 * i, 4)
            return carry

        lax.fori_loop(0, count // 4, four, 0)
        at2 = start + (count // 4) * 4

        @pl.when((count // 2) % 2 == 1)
        def _(which=which, at2=at2):
            chunk(which, at2, 2)

        at1 = start + (count // 2) * 2

        @pl.when(count % 2 == 1)
        def _(which=which, at1=at1):
            chunk(which, at1, 1)

    xbit = info_ref[4]
    ybit = info_ref[5]
    groups = ga_ref.shape[1]
    per = cols // groups
    bits = groups.bit_length() - 1

    @pl.when(e == 0)
    def _():
        for w, ref in enumerate((du_ref, dd_ref)):
            for p in range(groups):
                ga_ref[w + xbit - 2 * w * xbit, spot(p, range(bits))] = ref[
                    p * per : (p + 1) * per, :
                ].astype(BF)

    @pl.when(e == 1)
    def _():
        for w, ref in enumerate((du_ref, dd_ref)):
            for p in range(groups):
                y = p % 2
                order = [p >> 1 & 1, w] + [p >> i & 1 for i in range(2, bits)]
                at = functools.reduce(lambda acc, bit: 2 * acc + bit, order, 0)
                gb_ref[y + ybit - 2 * y * ybit, at] = ref[p * per : (p + 1) * per, :].astype(BF)


def spot(index, order):
    return functools.reduce(lambda acc, bit: 2 * acc + (index >> bit & 1), order, 0)


def ffn(call, core, info, x_mine, x_other, g_mine, g_other, up, down, partial, groups):
    slots, model = x_mine.shape
    cols = up.shape[-1]
    per = cols // groups
    whole = pl.BlockSpec((slots, model), lambda e, i: (0, 0), pipeline_mode=pl.Buffered(1))
    first = partial is None
    extra = () if first else tuple(partial)
    return pl.pallas_call(
        functools.partial(ffn_kernel, first),
        grid_spec=pltpu.PrefetchScalarGridSpec(
            num_scalar_prefetch=1,
            grid=(EXPERTS,),
            in_specs=[whole] * 4
            + [
                pl.BlockSpec((1, model, cols), lambda e, i: (e, 0, 0)),
                pl.BlockSpec(
                    (1, groups, 1, 1, per, model), lambda e, i: (e, 0, i[6], call, 0, 0)
                ),
            ]
            + [whole] * len(extra),
            out_specs=[pl.BlockSpec((slots, model), lambda e, i: (0, 0))] * 4
            + [
                pl.BlockSpec((2, groups, per, model), lambda e, i: (0, 0, 0, 0)),
                pl.BlockSpec((2, groups, per, model), lambda e, i: (0, 0, 0, 0)),
            ],
            scratch_shapes=[
                pltpu.VMEM((model, cols), F32),
                pltpu.VMEM((cols, model), F32),
                pltpu.VMEM((4 * BLK, cols), BF),
                pltpu.VMEM((4 * BLK, cols), BF),
            ],
        ),
        out_shape=[jax.ShapeDtypeStruct((slots, model), BF)] * 4
        + [jax.ShapeDtypeStruct((2, groups, per, model), BF)] * 2,
        compiler_params=pltpu.CompilerParams(vmem_limit_bytes=VMEM_BYTES),
        cost_estimate=pl.CostEstimate(
            flops=12 * 2 * slots * model * cols, bytes_accessed=40 * 1024 * 1024,
            transcendentals=2 * 2 * slots * cols,
        ),
        name="ffn",
    )(info, x_mine, x_other, g_mine, g_other, up, down, *extra)


def peers():
    out = {}
    for axis in ("head", "dp"):
        me = lax.axis_index(axis)
        for b in range(lax.axis_size(axis).bit_length() - 1):
            bit = (me // (1 << b)) % 2
            out[axis, b] = bit, {axis: me + (1 - 2 * bit) * (1 << b)}
    return out


class Halving:
    def __init__(self, env, order, buf, gots, sems):
        self.env, self.order, self.buf, self.gots = env, order, buf, gots
        self.sems = sems
        self.path = ()
        self.copies = []
        self.round = 0

    def add(self, into, got):
        lead = len(into.shape) - 2
        for index in range(1 << lead):
            at = tuple(index >> i & 1 for i in range(lead))
            if lead:
                into[at] = into[at] + got[at]
            else:
                into[...] = into[...] + got[...]

    def send(self, got):
        bit, partner = self.env[self.order[self.round]]
        view = self.buf.at[self.path] if self.path else self.buf
        away, stay = view.at[1 - bit], view.at[bit]
        if got is not None:
            self.add(away, got.at[1 - bit])
        copy = pltpu.make_async_remote_copy(
            src_ref=away, dst_ref=self.gots[self.round],
            send_sem=self.sems[0].at[self.sems[2] + self.round],
            recv_sem=self.sems[1].at[self.sems[2] + self.round],
            device_id=partner, device_id_type=pl.DeviceIdType.MESH,
        )
        copy.start()
        self.copies.append(copy)
        if got is not None:
            self.add(stay, got.at[bit])
        self.path = self.path + (bit,)

    def step(self):
        self.copies[self.round].wait_recv()
        got = self.gots[self.round]
        self.round += 1
        if self.round < len(self.order):
            self.send(got)
            return False
        self.add(self.buf.at[self.path], got)
        return True

    def result(self):
        return self.buf.at[self.path]

    def close(self):
        for copy in self.copies:
            copy.wait_send()


def orders(dp_bits):
    rest = [("dp", b) for b in range(2, dp_bits)]
    x, y, z = ("head", 1), ("dp", 0), ("dp", 1)
    return (
        [y, z] + rest,
        [z, x] + rest,
        [("head", 0), y, z, x] + rest,
        [("head", 0), z, y, x] + rest,
    )


def finish_kernel(calls, dp_bits, *refs):
    n = 2 * calls
    kept, came = refs[:n], refs[n : 2 * n]
    att = refs[2 * n : 2 * n + 4]
    small_ref, rows_ref = refs[2 * n + 4 : 2 * n + 6]
    res_ref, table_ref, home_ref = refs[2 * n + 6 : 2 * n + 9]
    scratch = list(refs[2 * n + 9 :])
    send_sem, recv_sem, load_sem = scratch[-3:]
    env = peers()
    order = orders(dp_bits)
    core, x = env["head", 0][0], env["head", 1][0]
    me = lax.axis_index("head")
    heads = lax.axis_size("head")
    groups = 1 << dp_bits
    used = [0]

    def fresh(k):
        used[0] += k
        return send_sem, recv_sem, used[0] - k

    barrier = pltpu.get_barrier_semaphore()
    greet = [partner for _, partner in env.values()]
    for o in range(1, heads):
        if o & (o - 1):
            greet.append({"head": (me // 4) * 4 + flipped(me % 4, o)})
    for partner in greet:
        pl.semaphore_signal(barrier, inc=1, device_id=partner, device_id_type=pl.DeviceIdType.MESH)
    pl.semaphore_wait(barrier, len(greet))

    loads = [0]

    def load(src, dst):
        copy = pltpu.make_async_copy(src, dst, load_sem.at[loads[0]])
        loads[0] += 1
        copy.start()
        return copy

    moves = []
    for o in range(1, heads):
        to = (me // 4) * 4 + flipped(me % 4, o)
        _, _, s = fresh(1)
        copy = pltpu.make_async_remote_copy(
            src_ref=rows_ref.at[to], dst_ref=home_ref.at[me], send_sem=send_sem.at[s],
            recv_sem=recv_sem.at[s], device_id={"head": to}, device_id_type=pl.DeviceIdType.MESH,
        )
        moves.append(copy)

    streams, firsts, waits = [], [], []
    at = 0

    def claim(k):
        nonlocal at
        at += k
        return scratch[at - k : at]

    for half in range(2):
        order_t = order[2 + half]
        buf, *gots = claim(1 + len(order_t))
        copies = []
        lanes = buf.shape[-1]
        for i, ref in enumerate(att):
            for p in range(groups):
                spots = {("head", 0): i >> 1, ("head", 1): i & 1}
                spots.update({("dp", b): p >> b & 1 for b in range(dp_bits)})
                copies.append(
                    load(ref.at[p, :, pl.ds(half * lanes, lanes)], buf.at[tuple(spots[o] for o in order_t)])
                )
        streams.append(Halving(env, order_t, buf, gots, fresh(len(order_t))))
        firsts.append(None)
        waits.append(copies)
    for i in range(n):
        order_e = order[i % 2]
        buf, first, *gots = claim(2 + len(order_e))
        waits.append([load(kept[i], buf), load(came[i], first)])
        streams.append(Halving(env, order_e, buf, gots, fresh(len(order_e))))
        firsts.append(first)
    sbuf, *sgots = claim(2 + 1 + dp_bits)
    sload = load(small_ref, sbuf)

    for stream, first, copies in zip(streams, firsts, waits):
        for copy in copies:
            copy.wait()
        stream.send(first)
    for copy in moves:
        copy.start()
    home_ref[me] = rows_ref[me]

    sload.wait()
    _, _, s0 = fresh(2 + dp_bits)
    scopies = []
    spath = ()
    sorder = [("head", 0), ("head", 1)] + [("dp", b) for b in range(dp_bits)]

    def small_send(r):
        nonlocal spath
        bit, partner = env[sorder[r]]
        view = sbuf.at[spath] if spath else sbuf
        away = view
        if r >= 2:
            away = view.at[1 - bit]
            spath = spath + (bit,)
        copy = pltpu.make_async_remote_copy(
            src_ref=away, dst_ref=sgots[r], send_sem=send_sem.at[s0 + r],
            recv_sem=recv_sem.at[s0 + r], device_id=partner, device_id_type=pl.DeviceIdType.MESH,
        )
        copy.start()
        scopies.append(copy)

    def small_step(r):
        scopies[r].wait()
        view = sbuf.at[spath] if spath else sbuf
        view[...] = view[...] + sgots[r][...]
        if r + 1 < len(sorder):
            small_send(r + 1)

    gathers, after = [], []

    def spread(index, lanes, value):
        mine = res_ref.at[core, x, index, :, lanes]
        mine[...] = value[...]
        for kind in ("head", 1), ("head", 0):
            _, _, s = fresh(1)
            copy = pltpu.make_async_remote_copy(
                src_ref=mine, dst_ref=mine, send_sem=send_sem.at[s], recv_sem=recv_sem.at[s],
                device_id=env[kind][1], device_id_type=pl.DeviceIdType.MESH,
            )
            copy.start()
            (after if kind == ("head", 1) else gathers).append((copy, index, lanes))

    small_send(0)
    model = res_ref.shape[-1]
    done = [False] * len(streams)
    for r in range(max(len(o) for o in order) + 1):
        for i, stream in enumerate(streams):
            if not done[i]:
                done[i] = stream.step()
                if done[i]:
                    if i < 2:
                        lanes = pl.ds(i * (model // 2), model // 2)
                        spread(n, lanes, stream.result())
                    else:
                        spread(i - 2, pl.ds(0, model), stream.result())
        if r < len(sorder):
            small_step(r)
    for r in range(max(len(o) for o in order) + 1, len(sorder)):
        small_step(r)
    table_ref[...] = sbuf[spath]
    forwards = []
    for copy, index, lanes in after:
        copy.wait_recv()
        other = res_ref.at[core, 1 - x, index, :, lanes]
        _, _, s = fresh(1)
        forward = pltpu.make_async_remote_copy(
            src_ref=other, dst_ref=other, send_sem=send_sem.at[s], recv_sem=recv_sem.at[s],
            device_id=env["head", 0][1], device_id_type=pl.DeviceIdType.MESH,
        )
        forward.start()
        forwards.append(forward)
    for copy, _, _ in gathers:
        copy.wait()
    for copy in forwards:
        copy.wait()
    for copy, _, _ in after:
        copy.wait_send()
    for stream in streams:
        stream.close()
    for copy in moves:
        copy.wait()


def flipped(index, offset):
    low, high = index % 2, index // 2
    if offset & 1:
        low = 1 - low
    if offset & 2:
        high = 1 - high
    return 2 * high + low


def finish(calls, dp_bits, kept, came, att, small, rows):
    heads = rows.shape[0]
    assert heads == 4
    groups, per, model = att[0].shape
    order = orders(dp_bits)
    scratch = []
    for o in order[2:]:
        for r in range(len(o) + 1):
            left = len(o) if r == 0 else len(o) - r
            scratch.append(pltpu.VMEM((2,) * left + (per, model // 2), BF))
    for i in range(2 * calls):
        o = order[i % 2]
        scratch.append(pltpu.VMEM((2,) * len(o) + (per, model), BF))
        for r in range(len(o) + 1):
            scratch.append(pltpu.VMEM((2,) * (len(o) - r) + (per, model), BF))
    tail = small.shape[1:]
    view = (2,) * dp_bits + tail
    small = small.reshape(view)
    small = small.transpose(*reversed(range(dp_bits)), dp_bits, dp_bits + 1)
    for r in range(3 + dp_bits):
        left = dp_bits if r < 3 else dp_bits - (r - 2)
        scratch.append(pltpu.VMEM((2,) * left + tail, F32))
    sems = sum(len(order[i % 2]) for i in range(2 * calls)) + sum(len(o) for o in order[2:])
    sems += heads - 1 + 2 + dp_bits + 3 * (2 * calls + 2)
    loads = 2 * 4 * groups + 4 * calls + 1
    kept = [k.reshape((2,) * len(order[i % 2]) + (per, model)) for i, k in enumerate(kept)]
    came = [k.reshape((2,) * len(order[i % 2]) + (per, model)) for i, k in enumerate(came)]
    hbm = pl.BlockSpec(memory_space=pl.ANY)
    vmem = pl.BlockSpec(memory_space=pltpu.VMEM)
    args = (*kept, *came, *att, small, rows)
    return pl.pallas_call(
        functools.partial(finish_kernel, calls, dp_bits),
        in_specs=[hbm] * (len(args) - 1) + [vmem],
        out_specs=[vmem] * 3,
        out_shape=[
            jax.ShapeDtypeStruct((2, 2, 2 * calls + 1, per, model), BF),
            jax.ShapeDtypeStruct(tail, F32),
            jax.ShapeDtypeStruct(rows.shape, BF),
        ],
        scratch_shapes=scratch
        + [
            pltpu.SemaphoreType.DMA((sems,)),
            pltpu.SemaphoreType.DMA((sems,)),
            pltpu.SemaphoreType.DMA((loads,)),
        ],
        compiler_params=pltpu.CompilerParams(
            collective_id=0, has_side_effects=True, vmem_limit_bytes=VMEM_BYTES
        ),
        name="finish",
    )(*args)


def norm(values):
    mean = jnp.mean(values, axis=-1, keepdims=True)
    centered = values - mean
    rstd = lax.rsqrt(jnp.mean(centered * centered, axis=-1, keepdims=True) + EPS)
    return centered * rstd, rstd


def pick(table, kind):
    return jnp.where(kind == 0, table[0], table[1])


def norm_back(grad, gains, z, rstd):
    q = grad * gains
    return rstd * (
        q
        - jnp.mean(q, axis=-1, keepdims=True)
        - z * jnp.mean(q * z, axis=-1, keepdims=True)
    )


def by_expert(values, kind):
    first = jnp.sum(jnp.where(kind == 0, values, 0.0), axis=0)
    second = jnp.sum(jnp.where(kind == 0, 0.0, values), axis=0)
    return jnp.stack([first, second])


def flip(axis, size, bit):
    return functools.partial(
        lax.ppermute, axis_name=axis, perm=[(i, i ^ (1 << bit)) for i in range(size)]
    )


def take(values, dim, index):
    return lax.dynamic_index_in_dim(values, index, dim, keepdims=False)


def body(sizes, tokens, segment, modality, first_gain, first_shift, project_in, project_out,
         second_gain, second_shift, up_weight, down_weight, cotangent):
    heads, groups = sizes["head"], sizes["dp"]
    row_count, length, model = tokens.shape
    rows = row_count // heads
    count = row_count * length
    hidden = up_weight.shape[-1]
    me_h, me_d = lax.axis_index("head"), lax.axis_index("dp")
    core = me_h % 2
    head_bits = heads.bit_length() - 1
    dp_bits = groups.bit_length() - 1
    assert heads == 1 << head_bits and groups == 1 << dp_bits and head_bits >= 2
    hflip = [flip("head", heads, b) for b in range(head_bits)]
    dflip = [flip("dp", groups, b) for b in range(dp_bits)]

    def exchange(values):
        return lax.all_to_all(values, "head", split_axis=0, concat_axis=0, tiled=True)

    grid = (heads, rows, length)
    tok = exchange(tokens.astype(BF).reshape(*grid, model))
    kind = exchange(modality.reshape(grid)).reshape(count)
    cot = exchange(cotangent.astype(BF).reshape(*grid, model)).reshape(count, model)
    seg = lax.dynamic_slice_in_dim(segment, me_h * rows, rows, 0)
    kcol = kind[:, None]

    per = hidden // (groups * 2 * CALLS)
    up_own = take(up_weight.reshape(EXPERTS, model, groups, 2, CALLS, per), 3, core)
    up_own = up_own.transpose(3, 0, 1, 2, 4).reshape(CALLS, EXPERTS, model, groups * per)
    up_own, tok = lax.optimization_barrier((up_own, tok))
    down_view = down_weight.reshape(EXPERTS, groups, 2, CALLS, per, model)

    flat = tok.astype(F32).reshape(count, model)
    z1, rstd1 = norm(flat)
    gain1 = pick(first_gain, kcol)
    low1 = (z1 * gain1 + pick(first_shift, kcol)).astype(BF)
    qkv = mm(low1, project_in).astype(BF).reshape(*grid, 3 * model)
    context = attention_forward(seg, qkv)
    ctx = context.reshape(count, model)
    attention = mm(ctx, project_out)
    residual = flat + attention
    z2, rstd2 = norm(residual)
    gain2 = pick(second_gain, kcol)
    low2 = (z2 * gain2 + pick(second_shift, kcol)).astype(BF)

    slots = count + BLK
    is0 = (kind == 0).astype(F32).reshape(count // BLK, BLK)
    tri = jnp.triu(jnp.ones((BLK, BLK), F32))
    inner = mm(is0, tri)
    ends = jnp.cumsum(inner[:, -1])
    before = (inner + (ends - inner[:, -1])[:, None]).reshape(count).astype(jnp.int32)
    n0 = ends[-1].astype(jnp.int32)
    blocks0 = (n0 + BLK - 1) // BLK
    blocks1 = (count - n0 + BLK - 1) // BLK
    rank1 = jnp.arange(count, dtype=jnp.int32) - before
    slot = jnp.where(kind == 0, before - 1, blocks0 * BLK + rank1)
    place = (slot[None, :] == jnp.arange(slots, dtype=jnp.int32)[:, None]).astype(BF)

    near = hflip[0]
    g_mine = mm(place, cot).astype(BF)
    g_other = near(g_mine)
    blocks = jnp.stack([blocks0, blocks1])
    blocks_other = near(blocks)
    xbit = (me_h // 2) % 2
    ybit = me_d % 2
    info = jnp.concatenate([blocks, blocks_other, jnp.stack([xbit, ybit, core])]).astype(jnp.int32)
    x_mine = mm(place, low2).astype(BF)
    x_other = near(x_mine)

    partial, kept, came = None, [], []
    for call in range(CALLS):
        *partial, ga, gb = ffn(
            call, core, info, x_mine, x_other, g_mine, g_other, up_own[call], down_view, partial,
            groups,
        )
        kept += [ga[0], gb[0]]
        came += [hflip[1](ga[1]), dflip[0](gb[1])]

    branch_mine, branch_other, dx_mine, dx_other = partial
    dx = dx_mine + near(dx_other)
    second_grad = mm_tn(place, dx)
    branch = mm_tn(place, branch_mine + near(branch_other))
    back = exchange((attention + branch).astype(BF).reshape(*grid, model))
    output = tokens + back.reshape(row_count, length, model).astype(F32)

    cot32 = cot.astype(F32)
    gain2_term = by_expert(second_grad * z2, kcol)
    shift2_term = by_expert(second_grad, kcol)
    extra = norm_back(second_grad, gain2, z2, rstd2)
    attention_low = (cot32 + extra).astype(BF)
    out_term = mm_tn(ctx, attention_low)
    context_grad = mm_nt(attention_low, project_out).astype(BF)
    dqkv = attention_backward(seg, qkv, context_grad.reshape(context.shape)).reshape(count, 3 * model)
    first_grad = mm_nt(dqkv, project_in)
    att = [mm_tn(low1, dqkv[:, i * model : (i + 1) * model]) for i in range(3)] + [out_term]
    att = [t.astype(BF).reshape(groups, model // groups, model) for t in att]
    gain1_term = by_expert(first_grad * z1, kcol)
    shift1_term = by_expert(first_grad, kcol)
    tail = (extra + norm_back(first_grad, gain1, z1, rstd1)).astype(BF).reshape(*grid, model)

    small = jnp.concatenate([gain1_term, shift1_term, gain2_term, shift2_term])
    small = small.reshape(8, groups, model // groups).transpose(1, 0, 2)
    small = jnp.pad(small, ((0, 0), (0, 0), (0, BLK - model // groups)))
    sums, table, home = finish(CALLS, dp_bits, kept, came, att, small, tail)
    input_grad = cotangent + home.reshape(row_count, length, model).astype(F32)

    up_grad = sums[:, 0, : 2 * CALLS].reshape(2, CALLS, EXPERTS, model // groups, groups, per)
    up_grad = up_grad.transpose(2, 3, 4, 0, 1, 5).reshape(EXPERTS, model // groups, hidden)
    up_grad = up_grad.astype(F32)
    down_grad = sums[:, 1, : 2 * CALLS].reshape(2, CALLS, EXPERTS, per, model)
    down_grad = down_grad.transpose(2, 0, 1, 3, 4).reshape(EXPERTS, hidden // groups, model)
    down_grad = down_grad.astype(F32)
    parts = sums[:, :, 2 * CALLS].astype(F32)
    in_grad = jnp.concatenate([parts[0, 0], parts[0, 1], parts[1, 0]], axis=-1)
    out_grad = parts[1, 1]
    tables = table[:, : model // groups].reshape(4, EXPERTS, model // groups)
    return (
        output, input_grad, tables[0], tables[1], in_grad, out_grad, tables[2], tables[3],
        up_grad, down_grad,
    )


def solution(mesh):
    return jax.shard_map(
        functools.partial(body, dict(mesh.shape)),
        mesh=mesh,
        in_specs=(
            P("dp", "head", None),
            P("dp", None),
            P("dp", "head"),
            P(),
            P(),
            P(),
            P(),
            P(),
            P(),
            P(),
            P(),
            P("dp", "head", None),
        ),
        out_specs=(
            P("dp", "head", None),
            P("dp", "head", None),
            P(None, "dp"),
            P(None, "dp"),
            P("dp", None),
            P("dp", None),
            P(None, "dp"),
            P(None, "dp"),
            P(None, "dp", None),
            P(None, "dp", None),
        ),
        check_vma=False,
    )
```

```python
import functools

import jax
import jax.numpy as jnp
from jax import lax
from jax.experimental import pallas as pl
from jax.experimental.pallas import tpu as pltpu
from jax.sharding import PartitionSpec as P

HEAD_DIM = 64
EXPERTS = 2
EPS = 1e-05
NEG = -1000000000.0
BLK = 128
CALLS = 2
VMEM_BYTES = 60 * 1024 * 1024
BF = jnp.bfloat16
F32 = jnp.float32
NT = (((1,), (1,)), ((), ()))
TN = (((0,), (0,)), ((), ()))


def mm(a, b):
    return jnp.dot(a, b, preferred_element_type=F32)


def mm_nt(a, b):
    return lax.dot_general(a, b, NT, preferred_element_type=F32)


def mm_tn(a, b):
    return lax.dot_general(a, b, TN, preferred_element_type=F32)


def bias_of(segc_ref, segr_ref, bias_ref):
    same = segc_ref[0] == segr_ref[0]
    bias_ref[...] = jnp.where(same, 0.0, NEG)


def attn_fwd_kernel(segc_ref, segr_ref, q_ref, k_ref, v_ref, o_ref, lse_ref, bias_ref):
    sub, _, length, width = q_ref.shape
    seq = sub * length

    @pl.when(pl.program_id(1) == 0)
    def _():
        bias_of(segc_ref, segr_ref, bias_ref)

    q = q_ref[...].reshape(seq, width) * jnp.asarray(HEAD_DIM**-0.5, BF)
    k = k_ref[...].reshape(seq, width)
    vt = v_ref[...].reshape(seq, width).T
    lane = lax.broadcasted_iota(jnp.int32, (1, width), 1) // HEAD_DIM
    zero = jnp.zeros((), BF)
    per = width // HEAD_DIM
    step = 2 * length
    ks = [jnp.where(lane == h, k, zero) for h in range(per)]
    for b in range(seq // step):
        cols = slice(b * step, (b + 1) * step)
        parts = []
        for h in range(per):
            s = mm_nt(ks[h], q[cols]) + bias_ref[:, cols]
            top = jnp.max(s, axis=0, keepdims=True)
            e = jnp.exp(s - top)
            total = jnp.sum(e, axis=0, keepdims=True)
            parts.append(mm(vt[h * HEAD_DIM : (h + 1) * HEAD_DIM], e.astype(BF)) * (1.0 / total))
            lse_ref[0, 0, h : h + 1, cols] = top + jnp.log(total)
        out = jnp.concatenate(parts, axis=0).T.astype(BF)
        o_ref[2 * b : 2 * b + 2, 0] = out.reshape(2, length, width)


def attn_bwd_kernel(
    segc_ref, segr_ref, q_ref, k_ref, v_ref, do_ref, lse_ref, out_ref, bias_ref
):
    sub, _, length, width = q_ref.shape
    seq = sub * length
    model = out_ref.shape[-1] // 3
    j = pl.program_id(1)

    @pl.when(j == 0)
    def _():
        bias_of(segc_ref, segr_ref, bias_ref)

    scale = HEAD_DIM**-0.5
    q = q_ref[...].reshape(seq, width) * jnp.asarray(scale, BF)
    k = k_ref[...].reshape(seq, width)
    kt = k.T
    v = v_ref[...].reshape(seq, width)
    do = do_ref[...].reshape(seq, width)
    lane = lax.broadcasted_iota(jnp.int32, (1, width), 1) // HEAD_DIM
    zero = jnp.zeros((), BF)
    per = width // HEAD_DIM
    step = 2 * length
    dk = jnp.zeros((seq, width), F32)
    dv = jnp.zeros((seq, width), F32)
    dqs = [[] for _ in range(seq // step)]
    for h in range(per):
        kh = jnp.where(lane == h, k, zero)
        vh = jnp.where(lane == h, v, zero)
        qh = jnp.where(lane == h, q, zero)
        doh = jnp.where(lane == h, do, zero)
        for b in range(seq // step):
            cols = slice(b * step, (b + 1) * step)
            s = mm_nt(kh, q[cols]) + bias_ref[:, cols]
            p = jnp.exp(s - lse_ref[0, 0, h : h + 1, cols])
            dp = mm_nt(vh, do[cols])
            ds = (p * (dp - jnp.sum(p * dp, axis=0, keepdims=True))).astype(BF)
            dv = dv + mm(p.astype(BF), doh[cols])
            dk = dk + mm(ds, qh[cols])
            dqs[b].append(mm(kt[h * HEAD_DIM : (h + 1) * HEAD_DIM], ds) * scale)
    dq = jnp.concatenate([jnp.concatenate(d, axis=0).T for d in dqs], axis=0)
    for i, g in enumerate((dq, dk, dv)):
        at = pl.multiple_of(i * model + j * width, width)
        out_ref[:, :, :, pl.ds(at, width)] = g.astype(BF).reshape(sub, 1, length, width)


def attn_specs(sub, length, pairs):
    def part(i):
        return pl.BlockSpec((sub, 1, length, 128), lambda r, j, i=i: (0, r, 0, i * pairs + j))

    return part


def attention_forward(segment, qkv):
    sub, rows, length, wide = qkv.shape
    seq = sub * length
    model = wide // 3
    pairs = model // 128
    part = attn_specs(sub, length, pairs)
    return pl.pallas_call(
        attn_fwd_kernel,
        grid=(rows, pairs),
        in_specs=[
            pl.BlockSpec((1, seq, 1), lambda r, j: (r, 0, 0)),
            pl.BlockSpec((1, 1, seq), lambda r, j: (r, 0, 0)),
            part(0),
            part(1),
            part(2),
        ],
        out_specs=[part(0), pl.BlockSpec((1, 1, 2, seq), lambda r, j: (r, j, 0, 0))],
        out_shape=[
            jax.ShapeDtypeStruct((sub, rows, length, model), BF),
            jax.ShapeDtypeStruct((rows, pairs, 2, seq), F32),
        ],
        scratch_shapes=[pltpu.VMEM((seq, seq), F32)],
        compiler_params=pltpu.CompilerParams(vmem_limit_bytes=VMEM_BYTES),
        cost_estimate=pl.CostEstimate(
            flops=8 * rows * seq * seq * model, bytes_accessed=8 * rows * seq * model,
            transcendentals=rows * seq * seq * model // HEAD_DIM,
        ),
        name="attn_fwd",
    )(segment[:, :, None], segment[:, None, :], qkv, qkv, qkv)


def attention_backward(segment, qkv, grad, lse):
    sub, rows, length, wide = qkv.shape
    seq = sub * length
    model = wide // 3
    pairs = model // 128
    part = attn_specs(sub, length, pairs)
    return pl.pallas_call(
        attn_bwd_kernel,
        grid=(rows, pairs),
        in_specs=[
            pl.BlockSpec((1, seq, 1), lambda r, j: (r, 0, 0)),
            pl.BlockSpec((1, 1, seq), lambda r, j: (r, 0, 0)),
            part(0),
            part(1),
            part(2),
            part(0),
            pl.BlockSpec((1, 1, 2, seq), lambda r, j: (r, j, 0, 0)),
        ],
        out_specs=pl.BlockSpec((sub, 1, length, wide), lambda r, j: (0, r, 0, 0)),
        out_shape=jax.ShapeDtypeStruct(qkv.shape, BF),
        scratch_shapes=[pltpu.VMEM((seq, seq), F32)],
        compiler_params=pltpu.CompilerParams(vmem_limit_bytes=VMEM_BYTES),
        cost_estimate=pl.CostEstimate(
            flops=20 * rows * seq * seq * model, bytes_accessed=14 * rows * seq * model,
            transcendentals=rows * seq * seq * model // HEAD_DIM,
        ),
        name="attn_bwd",
    )(segment[:, :, None], segment[:, None, :], qkv, qkv, qkv, grad, lse)


def ffn_kernel(first, bits, info_ref, xm_ref, xo_ref, gm_ref, go_ref, u_ref, d_ref, *refs):
    if first:
        prev = (None,) * 4
        outs, grads = refs[:4], refs[4:8]
    else:
        prev, outs, grads = refs[:4], refs[4:8], refs[8:12]
    du_ref, dd_ref, act_ref, dh_ref = refs[-4:]
    e = pl.program_id(0)
    slots, model = xm_ref.shape
    cols = u_ref.shape[-1]
    tile = 256
    down = d_ref[0]

    @pl.when(e == 0)
    def _():
        for out in outs:
            out[slots - BLK :, :] = jnp.zeros((BLK, model), BF)

    du_ref[...] = jnp.zeros_like(du_ref)
    dd_ref[...] = jnp.zeros_like(dd_ref)

    def chunk(which, block, count):
        size = count * BLK
        rows = pl.ds(pl.multiple_of(block * BLK, BLK), size)
        x = (xm_ref, xo_ref)[which][rows, :]
        g = (gm_ref, go_ref)[which][rows, :]
        for n in range(cols // tile):
            part = slice(n * tile, (n + 1) * tile)
            h = mm(x, u_ref[0, :, part])
            da = mm_nt(g, down[part, :])
            cdf = 0.5 + 0.5 * lax.erf(h * 0.7071067811865476)
            pdf = 0.3989422804014327 * jnp.exp(-0.5 * h * h)
            act_ref[:size, part] = (h * cdf).astype(BF)
            dh_ref[:size, part] = (da * (cdf + h * pdf)).astype(BF)
        act = act_ref[:size, :]
        dh = dh_ref[:size, :]
        for slot, value in ((which, mm(act, down)), (2 + which, mm_nt(dh, u_ref[0]))):
            if prev[slot] is not None:
                value = value + prev[slot][rows, :].astype(F32)
            outs[slot][rows, :] = value.astype(BF)
        du_ref[...] += mm_tn(x, dh)
        dd_ref[...] += mm_tn(act, g)

    for which in range(2):
        n0 = info_ref[2 * which]
        n1 = info_ref[2 * which + 1]
        start = jnp.where(e == 0, 0, n0)
        count = jnp.where(e == 0, n0, n1)

        def four(i, carry, which=which, start=start):
            chunk(which, start + 4 * i, 4)
            return carry

        lax.fori_loop(0, count // 4, four, 0)
        at2 = start + (count // 4) * 4

        @pl.when((count // 2) % 2 == 1)
        def _(which=which, at2=at2):
            chunk(which, at2, 2)

        at1 = start + (count // 2) * 2

        @pl.when(count % 2 == 1)
        def _(which=which, at1=at1):
            chunk(which, at1, 1)

    up_keep, up_send, down_keep, down_send = grads
    groups = 1 << bits
    per = model // groups
    wide = down_keep.shape[2]
    xbit, ybit = info_ref[4], info_ref[5]
    for ref, here in ((up_keep, e == xbit), (up_send, e != xbit)):

        @pl.when(here)
        def _(ref=ref):
            for p in range(groups):
                ref[spot(p, range(bits))] = du_ref[p * per : (p + 1) * per, :].astype(BF)

    for y in range(2):
        for ref, here in ((down_keep, ybit == y), (down_send, ybit != y)):

            @pl.when(here)
            def _(ref=ref, y=y):
                for p in range(y, cols // wide, 2):
                    at = spot(p >> 1, range(bits - 3))
                    ref[at, e] = dd_ref[p * wide : (p + 1) * wide, :].astype(BF)


def spot(index, order):
    return functools.reduce(lambda acc, bit: 2 * acc + (index >> bit & 1), order, 0)


def ffn(call, info, x_mine, x_other, g_mine, g_other, up, down, partial, groups):
    slots, model = x_mine.shape
    hidden = up.shape[-1]
    cols = hidden // (2 * CALLS)
    bits = groups.bit_length() - 1
    whole = pl.BlockSpec((slots, model), lambda e, i: (0, 0), pipeline_mode=pl.Buffered(1))
    first = partial is None
    extra = () if first else tuple(partial)
    grads = [(groups, model // groups, model)] * 2
    grads += [(groups // 8, EXPERTS, hidden // groups, model)] * 2
    return pl.pallas_call(
        functools.partial(ffn_kernel, first, bits),
        grid_spec=pltpu.PrefetchScalarGridSpec(
            num_scalar_prefetch=1,
            grid=(EXPERTS,),
            in_specs=[whole] * 4
            + [
                pl.BlockSpec((1, model, cols), lambda e, i: (e, 0, i[6] * CALLS + call)),
                pl.BlockSpec((1, cols, model), lambda e, i: (e, i[6] * CALLS + call, 0)),
            ]
            + [whole] * len(extra),
            out_specs=[pl.BlockSpec((slots, model), lambda e, i: (0, 0))] * 4
            + [pl.BlockSpec(g, lambda e, i, n=len(g): (0,) * n) for g in grads],
            scratch_shapes=[
                pltpu.VMEM((model, cols), F32),
                pltpu.VMEM((cols, model), F32),
                pltpu.VMEM((4 * BLK, cols), BF),
                pltpu.VMEM((4 * BLK, cols), BF),
            ],
        ),
        out_shape=[jax.ShapeDtypeStruct((slots, model), BF)] * 4
        + [jax.ShapeDtypeStruct(g, BF) for g in grads],
        compiler_params=pltpu.CompilerParams(vmem_limit_bytes=VMEM_BYTES),
        cost_estimate=pl.CostEstimate(
            flops=12 * 2 * slots * model * cols, bytes_accessed=40 * 1024 * 1024,
            transcendentals=2 * 2 * slots * cols,
        ),
        name="ffn",
    )(info, x_mine, x_other, g_mine, g_other, up, down, *extra)


def peers():
    out = {}
    for axis in ("head", "dp"):
        me = lax.axis_index(axis)
        for b in range(lax.axis_size(axis).bit_length() - 1):
            bit = (me // (1 << b)) % 2
            out[axis, b] = bit, {axis: me + (1 - 2 * bit) * (1 << b)}
    return out


class Halving:
    def __init__(self, env, order, buf, gots, sems):
        self.env, self.order, self.buf, self.gots = env, order, buf, gots
        self.sems = sems
        self.path = ()
        self.copies = []
        self.round = 0

    def add(self, into, got):
        lead = len(into.shape) - 2
        for index in range(1 << lead):
            at = tuple(index >> i & 1 for i in range(lead))
            if lead:
                into[at] = into[at] + got[at]
            else:
                into[...] = into[...] + got[...]

    def send(self, got):
        bit, partner = self.env[self.order[self.round]]
        view = self.buf.at[self.path] if self.path else self.buf
        away, stay = view.at[1 - bit], view.at[bit]
        if got is not None:
            self.add(away, got.at[1 - bit])
        copy = pltpu.make_async_remote_copy(
            src_ref=away, dst_ref=self.gots[self.round],
            send_sem=self.sems[0].at[self.sems[2] + self.round],
            recv_sem=self.sems[1].at[self.sems[2] + self.round],
            device_id=partner, device_id_type=pl.DeviceIdType.MESH,
        )
        copy.start()
        self.copies.append(copy)
        if got is not None:
            self.add(stay, got.at[bit])
        self.path = self.path + (bit,)

    def step(self):
        self.copies[self.round].wait_recv()
        got = self.gots[self.round]
        self.round += 1
        if self.round < len(self.order):
            self.send(got)
            return False
        self.add(self.buf.at[self.path], got)
        return True

    def result(self):
        return self.buf.at[self.path]

    def close(self):
        for copy in self.copies:
            copy.wait_send()


def orders(dp_bits):
    rest = [("dp", b) for b in range(2, dp_bits)]
    x, y, z = ("head", 1), ("dp", 0), ("dp", 1)
    return (
        [("dp", b) for b in range(dp_bits)],
        [("dp", b) for b in range(1, dp_bits - 2)] + [("dp", dp_bits - 2), x],
        [("head", 0), y, z, x] + rest,
        [("head", 0), z, y, x] + rest,
    )


def finish_kernel(calls, dp_bits, *refs):
    refs = list(refs)

    def draw(k):
        out = refs[:k]
        del refs[:k]
        return out

    up_kept, up_came, down_kept, down_came = (draw(calls) for _ in range(4))
    att = draw(4)
    tables = draw(4)
    rows_ref, res_ref, down_ref, table_ref, home_ref = draw(5)
    send_sem, recv_sem, load_sem = refs[-3:]
    env = peers()
    order = orders(dp_bits)
    core, x = env["head", 0][0], env["head", 1][0]
    me = lax.axis_index("head")
    heads = lax.axis_size("head")
    groups = 1 << dp_bits
    used = [0]

    def fresh(k):
        used[0] += k
        return send_sem, recv_sem, used[0] - k

    def remote(src, dst, to):
        _, _, s = fresh(1)
        return pltpu.make_async_remote_copy(
            src_ref=src, dst_ref=dst, send_sem=send_sem.at[s], recv_sem=recv_sem.at[s],
            device_id=to, device_id_type=pl.DeviceIdType.MESH,
        )

    barrier = pltpu.get_barrier_semaphore()
    greet = [partner for _, partner in env.values()]
    for o in range(1, heads):
        if o & (o - 1):
            greet.append({"head": (me // 4) * 4 + flipped(me % 4, o)})
    for partner in greet:
        pl.semaphore_signal(barrier, inc=1, device_id=partner, device_id_type=pl.DeviceIdType.MESH)
    pl.semaphore_wait(barrier, len(greet))

    loads = [0]

    def load(src, dst):
        copy = pltpu.make_async_copy(src, dst, load_sem.at[loads[0]])
        loads[0] += 1
        copy.start()
        return copy

    streams, firsts, waits = [], [], []
    for half in range(2):
        order_t = order[2 + half]
        buf, *gots = draw(1 + len(order_t))
        copies = []
        lanes = buf.shape[-1]
        for i, ref in enumerate(att):
            for p in range(groups):
                spots = {("head", 0): i >> 1, ("head", 1): i & 1}
                spots.update({("dp", b): p >> b & 1 for b in range(dp_bits)})
                copies.append(
                    load(ref.at[p, :, pl.ds(half * lanes, lanes)], buf.at[tuple(spots[o] for o in order_t)])
                )
        streams.append(Halving(env, order_t, buf, gots, fresh(len(order_t))))
        firsts.append(None)
        waits.append(copies)
    for i in range(calls):
        buf, first, *gots = draw(2 + len(order[0]))
        waits.append([load(up_kept[i], buf), load(up_came[i], first)])
        streams.append(Halving(env, order[0], buf, gots, fresh(len(order[0]))))
        firsts.append(first)
    buf, first, *gots = draw(2 + len(order[1]))
    copies = []
    lead = dp_bits - 3
    for i in range(calls):
        for p in range(1 << lead):
            at = tuple(p >> (lead - 1 - b) & 1 for b in range(lead)) + (i,)
            copies += [load(down_kept[i].at[p], buf.at[at]), load(down_came[i].at[p], first.at[at])]
    waits.append(copies)
    down = Halving(env, order[1], buf, gots, fresh(len(order[1])))
    streams.append(down)
    firsts.append(first)
    (last_got,) = draw(1)
    sbuf, *sgots = draw(2 + 1 + dp_bits)

    for stream, first, copies in zip(streams, firsts, waits):
        for copy in copies:
            copy.wait()
        stream.send(first)

    moves = []
    for o in range(1, heads):
        to = (me // 4) * 4 + flipped(me % 4, o)
        moves.append(remote(rows_ref.at[to], home_ref.at[me], {"head": to}))
        moves[-1].start()
    home_ref[me] = rows_ref[me]

    for i, ref in enumerate(tables):
        sbuf[2 * i : 2 * i + 2, :] = ref[...]
    sorder = [("head", 0), ("head", 1)] + [("dp", b) for b in range(dp_bits)]
    scopies = [remote(sbuf, got, env[o][1]) for o, got in zip(sorder, sgots)]
    scopies[0].start()

    def small_step(r):
        scopies[r].wait()
        sbuf[...] = sbuf[...] + sgots[r][...]
        if r + 1 < len(sorder):
            scopies[r + 1].start()

    gathers, after = [], []

    def spread(index, lanes, value):
        mine = res_ref.at[core, x, index, :, lanes]
        mine[...] = value[...]
        for kind in ("head", 1), ("head", 0):
            copy = remote(mine, mine, env[kind][1])
            copy.start()
            (after if kind == ("head", 1) else gathers).append((copy, index, lanes))

    top, beyond = env["dp", dp_bits - 1]
    owner = top == core

    def finish_down():
        value = down.result()
        here = down_ref.at[x]
        over = down_ref.at[1 - x]
        last = remote(value, last_got, beyond)
        to_x, to_core, forward = (
            remote(here, here, env["head", 1][1]),
            remote(here, here, env["head", 0][1]),
            remote(over, over, env["head", 0][1]),
        )

        @pl.when(top != core)
        def _():
            last.start()

        def collect():
            @pl.when(owner)
            def _():
                last.wait_recv()
                here[...] = value[...] + last_got[...]
                to_x.start()
                to_core.start()

        def close():
            @pl.when(owner)
            def _():
                to_x.wait_recv()
                forward.start()
                to_core.wait_send()
                to_x.wait_send()
                forward.wait_send()

            @pl.when(top != core)
            def _():
                last.wait_send()
                to_core.wait_recv()
                forward.wait_recv()

        return collect, close

    model = res_ref.shape[-1]
    done = [False] * len(streams)
    for r in range(max(len(o) for o in order) + 1):
        collect = None
        for i, stream in enumerate(streams):
            if not done[i]:
                done[i] = stream.step()
                if done[i]:
                    if stream is down:
                        collect, close = finish_down()
                    elif i < 2:
                        spread(calls, pl.ds(i * (model // 2), model // 2), stream.result())
                    else:
                        spread(i - 2, pl.ds(0, model), stream.result())
        if r < len(sorder):
            small_step(r)
        if collect is not None:
            collect()
    for r in range(max(len(o) for o in order) + 1, len(sorder)):
        small_step(r)
    table_ref[...] = sbuf[...]
    forwards = []
    for copy, index, lanes in after:
        copy.wait_recv()
        other = res_ref.at[core, 1 - x, index, :, lanes]
        forward = remote(other, other, env["head", 0][1])
        forward.start()
        forwards.append(forward)
    close()
    for copy, _, _ in gathers:
        copy.wait()
    for copy in forwards:
        copy.wait()
    for copy, _, _ in after:
        copy.wait_send()
    for stream in streams:
        stream.close()
    for copy in moves:
        copy.wait()


def flipped(index, offset):
    low, high = index % 2, index // 2
    if offset & 1:
        low = 1 - low
    if offset & 2:
        high = 1 - high
    return 2 * high + low


def finish(calls, dp_bits, up_kept, up_came, down_kept, down_came, att, tables, rows):
    heads = rows.shape[0]
    assert heads == 4
    groups, per, model = att[0].shape
    wide = down_kept[0].shape[2]
    order = orders(dp_bits)
    scratch = []
    sems = 0

    def stream(o, tail, both):
        nonlocal sems
        sems += len(o)
        scratch.append(pltpu.VMEM((2,) * len(o) + tail, BF))
        for r in range(0 if both else 1, len(o) + 1):
            scratch.append(pltpu.VMEM((2,) * (len(o) - r) + tail, BF))

    for o in order[2:]:
        stream(o, (per, model // 2), False)
    for i in range(calls):
        stream(order[0], (per, model), True)
    stream(order[1], (wide, model), True)
    scratch.append(pltpu.VMEM((wide, model), BF))
    scratch += [pltpu.VMEM((8, model), F32)] * (3 + dp_bits)
    sems += heads - 1 + 2 + dp_bits + 3 * (calls + 2) + 4
    loads = 2 * 4 * groups + 2 * calls + 2 * calls * (groups // 8)
    up_kept, up_came = (
        [k.reshape((2,) * dp_bits + (per, model)) for k in ks] for ks in (up_kept, up_came)
    )
    hbm = pl.BlockSpec(memory_space=pl.ANY)
    vmem = pl.BlockSpec(memory_space=pltpu.VMEM)
    args = (*up_kept, *up_came, *down_kept, *down_came, *att, *tables, rows)
    return pl.pallas_call(
        functools.partial(finish_kernel, calls, dp_bits),
        in_specs=[hbm] * (len(args) - 5) + [vmem] * 5,
        out_specs=[vmem] * 4,
        out_shape=[
            jax.ShapeDtypeStruct((2, 2, calls + 1, per, model), BF),
            jax.ShapeDtypeStruct((2, wide, model), BF),
            jax.ShapeDtypeStruct((8, model), F32),
            jax.ShapeDtypeStruct(rows.shape, BF),
        ],
        scratch_shapes=scratch
        + [
            pltpu.SemaphoreType.DMA((sems,)),
            pltpu.SemaphoreType.DMA((sems,)),
            pltpu.SemaphoreType.DMA((loads,)),
        ],
        compiler_params=pltpu.CompilerParams(
            collective_id=0, has_side_effects=True, vmem_limit_bytes=VMEM_BYTES
        ),
        cost_estimate=pl.CostEstimate(
            flops=0, bytes_accessed=160 * 1024 * 1024, transcendentals=0
        ),
        name="finish",
    )(*args)


def norm(values):
    mean = jnp.mean(values, axis=-1, keepdims=True)
    centered = values - mean
    rstd = lax.rsqrt(jnp.mean(centered * centered, axis=-1, keepdims=True) + EPS)
    return centered * rstd, rstd


def pick(table, kind):
    return jnp.where(kind == 0, table[0], table[1])


def norm_back(grad, gains, z, rstd):
    q = grad * gains
    return rstd * (
        q
        - jnp.mean(q, axis=-1, keepdims=True)
        - z * jnp.mean(q * z, axis=-1, keepdims=True)
    )


def by_expert(values, kind):
    first = jnp.sum(jnp.where(kind == 0, values, 0.0), axis=0)
    second = jnp.sum(jnp.where(kind == 0, 0.0, values), axis=0)
    return jnp.stack([first, second])


def flip(axis, size, bit):
    return functools.partial(
        lax.ppermute, axis_name=axis, perm=[(i, i ^ (1 << bit)) for i in range(size)]
    )


def take(values, dim, index):
    return lax.dynamic_index_in_dim(values, index, dim, keepdims=False)


def body(sizes, tokens, segment, modality, first_gain, first_shift, project_in, project_out,
         second_gain, second_shift, up_weight, down_weight, cotangent):
    heads, groups = sizes["head"], sizes["dp"]
    row_count, length, model = tokens.shape
    rows = row_count // heads
    count = row_count * length
    hidden = up_weight.shape[-1]
    me_h, me_d = lax.axis_index("head"), lax.axis_index("dp")
    core = me_h % 2
    head_bits = heads.bit_length() - 1
    dp_bits = groups.bit_length() - 1
    assert heads == 1 << head_bits and groups == 1 << dp_bits and head_bits >= 2
    hflip = [flip("head", heads, b) for b in range(head_bits)]
    dflip = [flip("dp", groups, b) for b in range(dp_bits)]

    def exchange(values):
        return lax.all_to_all(values, "head", split_axis=0, concat_axis=0, tiled=True)

    grid = (heads, rows, length)
    tok = exchange(tokens.astype(BF).reshape(*grid, model))
    kind = exchange(modality.reshape(grid)).reshape(count)
    later, tok = lax.optimization_barrier((cotangent, tok))
    cot = exchange(later.astype(BF).reshape(*grid, model)).reshape(count, model)
    seg = lax.dynamic_slice_in_dim(segment, me_h * rows, rows, 0)
    kcol = kind[:, None]

    flat = tok.astype(F32).reshape(count, model)
    z1, rstd1 = norm(flat)
    gain1 = pick(first_gain, kcol)
    low1 = (z1 * gain1 + pick(first_shift, kcol)).astype(BF)
    qkv = mm(low1, project_in).astype(BF).reshape(*grid, 3 * model)
    context, lse = attention_forward(seg, qkv)
    ctx = context.reshape(count, model)
    attention = mm(ctx, project_out)
    residual = flat + attention
    z2, rstd2 = norm(residual)
    gain2 = pick(second_gain, kcol)
    low2 = (z2 * gain2 + pick(second_shift, kcol)).astype(BF)

    slots = count + BLK
    is0 = (kind == 0).astype(F32).reshape(count // BLK, BLK)
    tri = jnp.triu(jnp.ones((BLK, BLK), F32))
    inner = mm(is0, tri)
    ends = jnp.cumsum(inner[:, -1])
    before = (inner + (ends - inner[:, -1])[:, None]).reshape(count).astype(jnp.int32)
    n0 = ends[-1].astype(jnp.int32)
    blocks0 = (n0 + BLK - 1) // BLK
    blocks1 = (count - n0 + BLK - 1) // BLK
    rank1 = jnp.arange(count, dtype=jnp.int32) - before
    slot = jnp.where(kind == 0, before - 1, blocks0 * BLK + rank1)
    place = (slot[None, :] == jnp.arange(slots, dtype=jnp.int32)[:, None]).astype(BF)

    near = hflip[0]
    g_mine = mm(place, cot).astype(BF)
    g_other = near(g_mine)
    blocks = jnp.stack([blocks0, blocks1])
    blocks_other = near(blocks)
    xbit = (me_h // 2) % 2
    ybit = me_d % 2
    info = jnp.concatenate([blocks, blocks_other, jnp.stack([xbit, ybit, core])]).astype(jnp.int32)
    x_mine = mm(place, low2).astype(BF)
    x_other = near(x_mine)

    partial, kept, came = None, ([], []), ([], [])
    for call in range(CALLS):
        *partial, up_keep, up_send, down_keep, down_send = ffn(
            call, info, x_mine, x_other, g_mine, g_other, up_weight, down_weight, partial, groups
        )
        kept[0].append(up_keep)
        kept[1].append(down_keep)
        came[0].append(hflip[1](up_send))
        came[1].append(dflip[0](down_send))

    branch_mine, branch_other, dx_mine, dx_other = partial
    dx = dx_mine + near(dx_other)
    second_grad = mm_tn(place, dx)
    branch = mm_tn(place, branch_mine + near(branch_other))
    leaving = (attention + branch).astype(BF).reshape(*grid, model)

    cot32 = cot.astype(F32)
    gain2_term = by_expert(second_grad * z2, kcol)
    shift2_term = by_expert(second_grad, kcol)
    extra = norm_back(second_grad, gain2, z2, rstd2)
    attention_low = (cot32 + extra).astype(BF)
    out_term = mm_tn(ctx, attention_low)
    context_grad = mm_nt(attention_low, project_out).astype(BF)
    context_grad, leaving = lax.optimization_barrier((context_grad, leaving))
    back = exchange(leaving)
    dqkv = attention_backward(seg, qkv, context_grad.reshape(context.shape), lse).reshape(count, 3 * model)
    first_grad = mm_nt(dqkv, project_in)
    att = [mm_tn(low1, dqkv[:, i * model : (i + 1) * model]) for i in range(3)] + [out_term]
    att = [t.astype(BF).reshape(groups, model // groups, model) for t in att]
    gain1_term = by_expert(first_grad * z1, kcol)
    shift1_term = by_expert(first_grad, kcol)
    tail = (extra + norm_back(first_grad, gain1, z1, rstd1)).astype(BF).reshape(*grid, model)

    tail, back = lax.optimization_barrier((tail, back))
    output = tokens + back.reshape(row_count, length, model).astype(F32)
    sums, down_sum, table, home = finish(
        CALLS, dp_bits, kept[0], came[0], kept[1], came[1], att,
        (gain1_term, shift1_term, gain2_term, shift2_term), tail,
    )
    input_grad = cotangent + home.reshape(row_count, length, model).astype(F32)

    up_grad = sums[:, :, :CALLS].transpose(1, 3, 0, 2, 4)
    up_grad = up_grad.reshape(EXPERTS, model // groups, hidden).astype(F32)
    down_grad = down_sum.astype(F32)
    parts = sums[:, :, CALLS].astype(F32)
    in_grad = jnp.concatenate([parts[0, 0], parts[0, 1], parts[1, 0]], axis=-1)
    out_grad = parts[1, 1]
    tables = lax.dynamic_slice_in_dim(table, me_d * (model // groups), model // groups, 1)
    tables = tables.reshape(4, EXPERTS, model // groups)
    return (
        output, input_grad, tables[0], tables[1], in_grad, out_grad, tables[2], tables[3],
        up_grad, down_grad,
    )


def solution(mesh):
    return jax.shard_map(
        functools.partial(body, dict(mesh.shape)),
        mesh=mesh,
        in_specs=(
            P("dp", "head", None),
            P("dp", None),
            P("dp", "head"),
            P(),
            P(),
            P(),
            P(),
            P(),
            P(),
            P(),
            P(),
            P("dp", "head", None),
        ),
        out_specs=(
            P("dp", "head", None),
            P("dp", "head", None),
            P(None, "dp"),
            P(None, "dp"),
            P("dp", None),
            P("dp", None),
            P(None, "dp"),
            P(None, "dp"),
            P(None, "dp", None),
            P(None, "dp", None),
        ),
        check_vma=False,
    )
```

```python
import functools

import jax
import jax.numpy as jnp
from jax import lax
from jax.experimental import pallas as pl
from jax.experimental.pallas import tpu as pltpu
from jax.sharding import PartitionSpec as P

HEAD_DIM = 64
EXPERTS = 2
EPS = 1e-05
NEG = -1000000000.0
BLK = 128
CALLS = 2
VMEM_BYTES = 60 * 1024 * 1024
BF = jnp.bfloat16
F32 = jnp.float32
NT = (((1,), (1,)), ((), ()))
TN = (((0,), (0,)), ((), ()))


def mm(a, b):
    return jnp.dot(a, b, preferred_element_type=F32)


def mm_nt(a, b):
    return lax.dot_general(a, b, NT, preferred_element_type=F32)


def mm_tn(a, b):
    return lax.dot_general(a, b, TN, preferred_element_type=F32)


def bias_of(segc_ref, segr_ref, bias_ref):
    same = segc_ref[0] == segr_ref[0]
    bias_ref[...] = jnp.where(same, 0.0, NEG)


def attn_fwd_kernel(segc_ref, segr_ref, q_ref, k_ref, v_ref, o_ref, lse_ref, bias_ref):
    sub, _, length, width = q_ref.shape
    seq = sub * length

    @pl.when(pl.program_id(1) == 0)
    def _():
        bias_of(segc_ref, segr_ref, bias_ref)

    q = q_ref[...].reshape(seq, width) * jnp.asarray(HEAD_DIM**-0.5, BF)
    k = k_ref[...].reshape(seq, width)
    vt = v_ref[...].reshape(seq, width).T
    lane = lax.broadcasted_iota(jnp.int32, (1, width), 1) // HEAD_DIM
    zero = jnp.zeros((), BF)
    per = width // HEAD_DIM
    step = 2 * length
    ks = [jnp.where(lane == h, k, zero) for h in range(per)]
    for b in range(seq // step):
        cols = slice(b * step, (b + 1) * step)
        parts = []
        for h in range(per):
            s = mm_nt(ks[h], q[cols]) + bias_ref[:, cols]
            top = jnp.max(s, axis=0, keepdims=True)
            e = jnp.exp(s - top)
            total = jnp.sum(e, axis=0, keepdims=True)
            parts.append(mm(vt[h * HEAD_DIM : (h + 1) * HEAD_DIM], e.astype(BF)) * (1.0 / total))
            lse_ref[0, 0, h : h + 1, cols] = top + jnp.log(total)
        out = jnp.concatenate(parts, axis=0).T.astype(BF)
        o_ref[2 * b : 2 * b + 2, 0] = out.reshape(2, length, width)


def attn_specs(sub, length, pairs):
    def part(i):
        return pl.BlockSpec((sub, 1, length, 128), lambda r, j, i=i: (0, r, 0, i * pairs + j))

    return part


def attention_forward(segment, qkv):
    sub, rows, length, wide = qkv.shape
    seq = sub * length
    model = wide // 3
    pairs = model // 128
    part = attn_specs(sub, length, pairs)
    return pl.pallas_call(
        attn_fwd_kernel,
        grid=(rows, pairs),
        in_specs=[
            pl.BlockSpec((1, seq, 1), lambda r, j: (r, 0, 0)),
            pl.BlockSpec((1, 1, seq), lambda r, j: (r, 0, 0)),
            part(0),
            part(1),
            part(2),
        ],
        out_specs=[part(0), pl.BlockSpec((1, 1, 2, seq), lambda r, j: (r, j, 0, 0))],
        out_shape=[
            jax.ShapeDtypeStruct((sub, rows, length, model), BF),
            jax.ShapeDtypeStruct((rows, pairs, 2, seq), F32),
        ],
        scratch_shapes=[pltpu.VMEM((seq, seq), F32)],
        compiler_params=pltpu.CompilerParams(vmem_limit_bytes=VMEM_BYTES),
        cost_estimate=pl.CostEstimate(
            flops=8 * rows * seq * seq * model, bytes_accessed=8 * rows * seq * model,
            transcendentals=rows * seq * seq * model // HEAD_DIM,
        ),
        name="attn_fwd",
    )(segment[:, :, None], segment[:, None, :], qkv, qkv, qkv)


def ffn_kernel(first, bits, info_ref, xm_ref, xo_ref, gm_ref, go_ref, u_ref, d_ref, *refs):
    if first:
        prev = (None,) * 4
        outs, grads = refs[:4], refs[4:8]
    else:
        prev, outs, grads = refs[:4], refs[4:8], refs[8:12]
    du_ref, dd_ref, act_ref, dh_ref = refs[-4:]
    e = pl.program_id(0)
    slots, model = xm_ref.shape
    cols = u_ref.shape[-1]
    tile = 256
    down = d_ref[0]

    @pl.when(e == 0)
    def _():
        for out in outs:
            out[slots - BLK :, :] = jnp.zeros((BLK, model), BF)

    du_ref[...] = jnp.zeros_like(du_ref)
    dd_ref[...] = jnp.zeros_like(dd_ref)

    def chunk(which, block, count):
        size = count * BLK
        rows = pl.ds(pl.multiple_of(block * BLK, BLK), size)
        x = (xm_ref, xo_ref)[which][rows, :]
        g = (gm_ref, go_ref)[which][rows, :]
        for n in range(cols // tile):
            part = slice(n * tile, (n + 1) * tile)
            h = mm(x, u_ref[0, :, part])
            da = mm_nt(g, down[part, :])
            cdf = 0.5 + 0.5 * lax.erf(h * 0.7071067811865476)
            pdf = 0.3989422804014327 * jnp.exp(-0.5 * h * h)
            act_ref[:size, part] = (h * cdf).astype(BF)
            dh_ref[:size, part] = (da * (cdf + h * pdf)).astype(BF)
        act = act_ref[:size, :]
        dh = dh_ref[:size, :]
        for slot, value in ((which, mm(act, down)), (2 + which, mm_nt(dh, u_ref[0]))):
            if prev[slot] is not None:
                value = value + prev[slot][rows, :].astype(F32)
            outs[slot][rows, :] = value.astype(BF)
        du_ref[...] += mm_tn(x, dh)
        dd_ref[...] += mm_tn(act, g)

    for which in range(2):
        n0 = info_ref[2 * which]
        n1 = info_ref[2 * which + 1]
        start = jnp.where(e == 0, 0, n0)
        count = jnp.where(e == 0, n0, n1)

        def four(i, carry, which=which, start=start):
            chunk(which, start + 4 * i, 4)
            return carry

        lax.fori_loop(0, count // 4, four, 0)
        at2 = start + (count // 4) * 4

        @pl.when((count // 2) % 2 == 1)
        def _(which=which, at2=at2):
            chunk(which, at2, 2)

        at1 = start + (count // 2) * 2

        @pl.when(count % 2 == 1)
        def _(which=which, at1=at1):
            chunk(which, at1, 1)

    up_keep, up_send, down_keep, down_send = grads
    groups = 1 << bits
    per = model // groups
    wide = down_keep.shape[2]
    xbit, ybit = info_ref[4], info_ref[5]
    for ref, here in ((up_keep, e == xbit), (up_send, e != xbit)):

        @pl.when(here)
        def _(ref=ref):
            for p in range(groups):
                ref[spot(p, range(bits))] = du_ref[p * per : (p + 1) * per, :].astype(BF)

    for y in range(2):
        for ref, here in ((down_keep, ybit == y), (down_send, ybit != y)):

            @pl.when(here)
            def _(ref=ref, y=y):
                for p in range(y, cols // wide, 2):
                    at = spot(p >> 1, range(bits - 3))
                    ref[at, e] = dd_ref[p * wide : (p + 1) * wide, :].astype(BF)


def spot(index, order):
    return functools.reduce(lambda acc, bit: 2 * acc + (index >> bit & 1), order, 0)


def ffn(call, info, x_mine, x_other, g_mine, g_other, up, down, partial, groups):
    slots, model = x_mine.shape
    hidden = up.shape[-1]
    cols = hidden // (2 * CALLS)
    bits = groups.bit_length() - 1
    whole = pl.BlockSpec((slots, model), lambda e, i: (0, 0), pipeline_mode=pl.Buffered(1))
    first = partial is None
    extra = () if first else tuple(partial)
    grads = [(groups, model // groups, model)] * 2
    grads += [(groups // 8, EXPERTS, hidden // groups, model)] * 2
    return pl.pallas_call(
        functools.partial(ffn_kernel, first, bits),
        grid_spec=pltpu.PrefetchScalarGridSpec(
            num_scalar_prefetch=1,
            grid=(EXPERTS,),
            in_specs=[whole] * 4
            + [
                pl.BlockSpec((1, model, cols), lambda e, i: (e, 0, i[6] * CALLS + call)),
                pl.BlockSpec((1, cols, model), lambda e, i: (e, i[6] * CALLS + call, 0)),
            ]
            + [whole] * len(extra),
            out_specs=[pl.BlockSpec((slots, model), lambda e, i: (0, 0))] * 4
            + [pl.BlockSpec(g, lambda e, i, n=len(g): (0,) * n) for g in grads],
            scratch_shapes=[
                pltpu.VMEM((model, cols), F32),
                pltpu.VMEM((cols, model), F32),
                pltpu.VMEM((4 * BLK, cols), BF),
                pltpu.VMEM((4 * BLK, cols), BF),
            ],
        ),
        out_shape=[jax.ShapeDtypeStruct((slots, model), BF)] * 4
        + [jax.ShapeDtypeStruct(g, BF) for g in grads],
        compiler_params=pltpu.CompilerParams(vmem_limit_bytes=VMEM_BYTES),
        cost_estimate=pl.CostEstimate(
            flops=12 * 2 * slots * model * cols, bytes_accessed=40 * 1024 * 1024,
            transcendentals=2 * 2 * slots * cols,
        ),
        name="ffn",
    )(info, x_mine, x_other, g_mine, g_other, up, down, *extra)


def peers():
    out = {}
    for axis in ("head", "dp"):
        me = lax.axis_index(axis)
        for b in range(lax.axis_size(axis).bit_length() - 1):
            bit = (me // (1 << b)) % 2
            out[axis, b] = bit, {axis: me + (1 - 2 * bit) * (1 << b)}
    return out


class Halving:
    def __init__(self, env, order, buf, gots, first, remote):
        self.rounds, path, prev = [], (), first
        for o, got in zip(order, gots):
            bit, partner = env[o]
            view = buf.at[path] if path else buf
            away, stay = view.at[1 - bit], view.at[bit]
            halves = (None, None) if prev is None else (prev.at[1 - bit], prev.at[bit])
            self.rounds.append((away, stay, *halves, remote(away, got, partner)))
            path, prev = path + (bit,), got
        self.result, self.last, self.at = buf.at[path], prev, 0
        self.done = False

    def send(self):
        away, stay, got_away, got_stay, copy = self.rounds[self.at]
        accumulate(away, got_away)
        copy.start()
        accumulate(stay, got_stay)

    def step(self):
        self.rounds[self.at][-1].wait_recv()
        self.at += 1
        if self.at < len(self.rounds):
            self.send()
        else:
            accumulate(self.result, self.last)
            self.done = True

    def close(self):
        for *_, copy in self.rounds:
            copy.wait_send()


def spots(ref):
    lead = len(ref.shape) - 2
    return [tuple(i >> b & 1 for b in range(lead)) for i in range(1 << lead)]


def accumulate(into, got):
    if got is not None:
        for at in spots(into):
            at = at or ...
            into[at] = into[at] + got[at]


def neighbours(env):
    me = lax.axis_index("head")
    out = [partner for _, partner in env.values()]
    for o in range(1, lax.axis_size("head")):
        if o & (o - 1):
            out.append({"head": (me // 4) * 4 + flipped(me % 4, o)})
    return out


def greet(env):
    barrier = pltpu.get_barrier_semaphore()
    partners = neighbours(env)
    for partner in partners:
        pl.semaphore_signal(barrier, inc=1, device_id=partner, device_id_type=pl.DeviceIdType.MESH)
    pl.semaphore_wait(barrier, len(partners))


class Copies:
    def __init__(self, send_sem, recv_sem, load_sem):
        self.send_sem, self.recv_sem, self.load_sem = send_sem, recv_sem, load_sem
        self.used, self.loads = 0, 0

    def remote(self, src, dst, to):
        s = self.used
        self.used += 1
        return pltpu.make_async_remote_copy(
            src_ref=src, dst_ref=dst, send_sem=self.send_sem.at[s], recv_sem=self.recv_sem.at[s],
            device_id=to, device_id_type=pl.DeviceIdType.MESH,
        )

    def local(self, src, dst):
        self.loads += 1
        return pltpu.make_async_copy(src, dst, self.load_sem.at[self.loads - 1])


def draw(refs, k):
    out = refs[:k]
    del refs[:k]
    return out


def up_order(dp_bits):
    return [("dp", b) for b in range(dp_bits)]


def down_order(dp_bits):
    return [("dp", b) for b in range(1, dp_bits - 1)] + [("head", 1)]


def attention_orders(dp_bits):
    rest = [("dp", b) for b in range(1, dp_bits)]
    core, x, y = ("head", 0), ("head", 1), ("dp", 0)
    return [core, y, x] + rest, [core, x, y] + rest


def stream_scratch(order, tail, first):
    sizes = [len(order)] * (2 if first else 1) + [len(order) - r for r in range(1, len(order) + 1)]
    return [pltpu.VMEM((2,) * k + tail, BF) for k in sizes]


def attn_bwd_kernel(calls, dp_bits, *refs):
    refs = list(refs)
    (segc_ref, segr_ref, q_ref, k_ref, v_ref, do_ref, lse_ref, low_ref, w_ref) = draw(refs, 9)
    up_kept, up_came, down_kept, down_came = (draw(refs, calls) for _ in range(4))
    leaving_ref, in_ref, first_ref, up_ref, down_ref, back_ref = draw(refs, 6)
    bias_ref, dqkv_ref, lowt_ref, acc_ref = draw(refs, 4)
    env = peers()
    copies = Copies(*refs[-3:])
    r, j = pl.program_id(0), pl.program_id(1)
    rows, pairs = pl.num_programs(0), pl.num_programs(1)
    me = lax.axis_index("head")

    streams, loads = [], []
    order = up_order(dp_bits)[:2]
    for i in range(calls):
        buf, first, *gots = draw(refs, 2 + len(order))
        loads.append([copies.local(up_kept[i], buf), copies.local(up_came[i], first)])
        streams.append(Halving(env, order, buf, gots, first, copies.remote))
    order = down_order(dp_bits)
    buf, first, *gots = draw(refs, 2 + len(order))
    lead = dp_bits - 3
    loads.append([])
    for i in range(calls):
        for p in range(1 << lead):
            at = tuple(p >> (lead - 1 - b) & 1 for b in range(lead)) + (i,)
            loads[-1].append(copies.local(down_kept[i].at[p], buf.at[at]))
            loads[-1].append(copies.local(down_came[i].at[p], first.at[at]))
    streams.append(Halving(env, order, buf, gots, first, copies.remote))
    moves = []
    for o in range(1, 4):
        to = (me // 4) * 4 + flipped(me % 4, o)
        moves.append(copies.remote(leaving_ref.at[to], back_ref.at[me], {"head": to}))
    stays = copies.local(leaving_ref.at[me], back_ref.at[me])

    @pl.when((r == 0) & (j == 0))
    def _():
        for group in loads:
            for copy in group:
                copy.start()
        stays.start()
        greet(env)
        for stream, group in zip(reversed(streams), reversed(loads)):
            for copy in group:
                copy.wait()
            stream.send()
        for copy in moves:
            copy.start()

    @pl.when((r == rows - 1) & (j == 0))
    def _():
        streams[0].step()

    sub, _, length, width = q_ref.shape
    seq = sub * length
    model = dqkv_ref.shape[-1] // 3

    @pl.when(j == 0)
    def _():
        bias_of(segc_ref, segr_ref, bias_ref)

    scale = HEAD_DIM**-0.5
    q = q_ref[...].reshape(seq, width) * jnp.asarray(scale, BF)
    k = k_ref[...].reshape(seq, width)
    kt = k.T
    v = v_ref[...].reshape(seq, width)
    do = do_ref[...].reshape(seq, width)
    lane = lax.broadcasted_iota(jnp.int32, (1, width), 1) // HEAD_DIM
    zero = jnp.zeros((), BF)
    per = width // HEAD_DIM
    step = 2 * length
    dk = jnp.zeros((seq, width), F32)
    dv = jnp.zeros((seq, width), F32)
    dqs = [[] for _ in range(seq // step)]
    for h in range(per):
        kh = jnp.where(lane == h, k, zero)
        vh = jnp.where(lane == h, v, zero)
        qh = jnp.where(lane == h, q, zero)
        doh = jnp.where(lane == h, do, zero)
        for b in range(seq // step):
            cols = slice(b * step, (b + 1) * step)
            s = mm_nt(kh, q[cols]) + bias_ref[:, cols]
            p = jnp.exp(s - lse_ref[0, 0, h : h + 1, cols])
            dp = mm_nt(vh, do[cols])
            ds = (p * (dp - jnp.sum(p * dp, axis=0, keepdims=True))).astype(BF)
            dv = dv + mm(p.astype(BF), doh[cols])
            dk = dk + mm(ds, qh[cols])
            dqs[b].append(mm(kt[h * HEAD_DIM : (h + 1) * HEAD_DIM], ds) * scale)
    dq = jnp.concatenate([jnp.concatenate(d, axis=0).T for d in dqs], axis=0)
    for i, g in enumerate((dq, dk, dv)):
        at = pl.multiple_of(i * model + j * width, width)
        dqkv_ref[:, pl.ds(at, width)] = g.astype(BF)

    @pl.when((r == rows - 1) & (j == pairs - 1))
    def _():
        for stream in streams[1:]:
            stream.step()

    @pl.when(j == pairs - 1)
    def _():
        tile = 256
        lowt_ref[...] = low_ref[...].reshape(seq, model).T
        first_ref[...] = jnp.zeros_like(first_ref)

        @pl.when(r == 0)
        def _():
            acc_ref[...] = jnp.zeros_like(acc_ref)

        def piece(n, carry):
            cols = pl.ds(pl.multiple_of(n * tile, tile), tile)
            part = dqkv_ref[:, cols]
            acc_ref[:, cols] += mm(lowt_ref[...], part)
            first_ref[...] += mm_nt(part, w_ref[:, cols]).reshape(first_ref.shape)
            return carry

        lax.fori_loop(0, 3 * model // tile, piece, 0)

    @pl.when((r == rows - 1) & (j == pairs - 1))
    def _():
        height = in_ref.shape[1]
        for p in range(in_ref.shape[0]):
            in_ref[p] = acc_ref[p * height : (p + 1) * height, :].astype(BF)
        while not all(stream.done for stream in streams):
            for stream in streams:
                if not stream.done:
                    stream.step()
        for i in range(calls):
            for at in spots(streams[i].result):
                up_ref[(i, *at)] = streams[i].result[at or ...]
        down_ref[...] = streams[-1].result[...]
        stays.wait()
        for copy in moves:
            copy.wait()
        for stream in streams:
            stream.close()


def attention_backward(
    segment, qkv, grad, lse, low, weight, up_kept, up_came, down_kept, down_came, leaving, dp_bits
):
    sub, rows, length, wide = qkv.shape
    seq = sub * length
    model = wide // 3
    pairs = model // 128
    groups = 1 << dp_bits
    calls = len(up_kept)
    part = attn_specs(sub, length, pairs)
    per, high = model // groups, down_kept[0].shape[2]
    row = pl.BlockSpec((sub, 1, length, model), lambda r, j: (0, r, 0, 0))
    hbm = pl.BlockSpec(memory_space=pl.ANY)

    def fixed(*shape):
        return pl.BlockSpec(shape, lambda r, j: (0,) * len(shape), pipeline_mode=pl.Buffered(1))

    up_kept, up_came = (
        [k.reshape((2,) * dp_bits + (per, model)) for k in ks] for ks in (up_kept, up_came)
    )
    ups, downs = up_order(dp_bits), down_order(dp_bits)
    scratch = [
        s
        for _ in range(calls)
        for s in [pltpu.VMEM((2,) * dp_bits + (per, model), BF)] * 2
        + [pltpu.VMEM((2,) * (dp_bits - 1 - i) + (per, model), BF) for i in range(2)]
    ]
    scratch += stream_scratch(downs, (high, model), True)
    sems = 2 * calls + len(downs) + 3
    loads = 2 * calls + 2 * calls * (groups // 8) + 1
    up_tail = (calls,) + (2,) * (dp_bits - 2) + (per, model)
    return pl.pallas_call(
        functools.partial(attn_bwd_kernel, calls, dp_bits),
        grid=(rows, pairs),
        in_specs=[
            pl.BlockSpec((1, seq, 1), lambda r, j: (r, 0, 0)),
            pl.BlockSpec((1, 1, seq), lambda r, j: (r, 0, 0)),
            part(0),
            part(1),
            part(2),
            part(0),
            pl.BlockSpec((1, 1, 2, seq), lambda r, j: (r, j, 0, 0)),
            row,
            fixed(*weight.shape),
        ]
        + [hbm] * (4 * calls + 1),
        out_specs=[fixed(groups, per, wide), row, fixed(*up_tail), fixed(high, model), hbm],
        out_shape=[
            jax.ShapeDtypeStruct((groups, per, wide), BF),
            jax.ShapeDtypeStruct((sub, rows, length, model), F32),
            jax.ShapeDtypeStruct(up_tail, BF),
            jax.ShapeDtypeStruct((high, model), BF),
            jax.ShapeDtypeStruct(leaving.shape, BF),
        ],
        scratch_shapes=[
            pltpu.VMEM((seq, seq), F32),
            pltpu.VMEM((seq, wide), BF),
            pltpu.VMEM((model, seq), BF),
            pltpu.VMEM((model, wide), F32),
        ]
        + scratch
        + [
            pltpu.SemaphoreType.DMA((sems,)),
            pltpu.SemaphoreType.DMA((sems,)),
            pltpu.SemaphoreType.DMA((loads,)),
        ],
        compiler_params=pltpu.CompilerParams(
            collective_id=1, has_side_effects=True, vmem_limit_bytes=VMEM_BYTES
        ),
        cost_estimate=pl.CostEstimate(
            flops=20 * rows * seq * seq * model + 4 * rows * seq * model * wide,
            bytes_accessed=100 * 1024 * 1024,
            transcendentals=rows * seq * seq * model // HEAD_DIM,
        ),
        name="attn_bwd",
    )(
        segment[:, :, None], segment[:, None, :], qkv, qkv, qkv, grad, lse, low, weight,
        *up_kept, *up_came, *down_kept, *down_came, leaving,
    )


def finish_kernel(calls, dp_bits, *refs):
    refs = list(refs)
    up_ref, in_ref, out_ref = draw(refs, 3)
    tables = draw(refs, 4)
    last_ref, rows_ref, att_ref, up_out, down_ref, table_ref, home_ref = draw(refs, 7)
    env = peers()
    copies = Copies(*refs[-3:])
    remote = copies.remote
    core, x = env["head", 0][0], env["head", 1][0]
    me = lax.axis_index("head")
    groups = 1 << dp_bits
    model = home_ref.shape[-1]
    x_partner, core_partner = env["head", 1][1], env["head", 0][1]

    streams, loads = [], []
    for half, order in enumerate(attention_orders(dp_bits)):
        buf, *gots = draw(refs, 1 + len(order))
        loads.append([])
        lanes = buf.shape[-1]
        for i in range(4):
            ref, start = (out_ref, 0) if i == 3 else (in_ref, i * model)
            for p in range(groups):
                spot_of = {("head", 0): i >> 1, ("head", 1): i & 1}
                spot_of.update({("dp", b): p >> b & 1 for b in range(dp_bits)})
                cols = pl.ds(start + half * lanes, lanes)
                loads[-1].append(
                    copies.local(ref.at[p, :, cols], buf.at[tuple(spot_of[o] for o in order)])
                )
        streams.append(Halving(env, order, buf, gots, None, remote))
    order = up_order(dp_bits)[2:]
    for i in range(calls):
        buf, *gots = draw(refs, 1 + len(order))
        loads.append([copies.local(up_ref.at[i], buf)])
        streams.append(Halving(env, order, buf, gots, None, remote))
    (last_got,) = draw(refs, 1)
    sbuf, *sgots = draw(refs, 3 + dp_bits)

    for group in loads:
        for copy in group:
            copy.start()
    moves = []
    for o in range(1, 4):
        to = (me // 4) * 4 + flipped(me % 4, o)
        moves.append(remote(rows_ref.at[to], home_ref.at[me], {"head": to}))

    top, beyond = env["dp", dp_bits - 1]
    here, over = down_ref.at[x], down_ref.at[1 - x]
    last = remote(last_ref, last_got, beyond)
    to_x, to_core = remote(here, here, x_partner), remote(here, here, core_partner)
    forward = remote(over, over, core_partner)
    greet(env)

    @pl.when(top != core)
    def _():
        last.start()

    for stream, group in zip(streams, loads):
        for copy in group:
            copy.wait()
        stream.send()

    for i, ref in enumerate(tables):
        sbuf[2 * i : 2 * i + 2, :] = ref[...]
    sorder = [("head", 0), ("head", 1)] + [("dp", b) for b in range(dp_bits)]
    scopies = [remote(sbuf, got, env[o][1]) for o, got in zip(sorder, sgots)]
    scopies[0].start()
    home_ref[me] = rows_ref[me]

    gathers, after = [], []

    def spread(place, value):
        mine = place(x)
        mine[...] = value[...]
        for to, where in ((x_partner, after), (core_partner, gathers)):
            copy = remote(mine, mine, to)
            copy.start()
            where.append((copy, place))

    def att_place(half, side):
        at = (2 * core + side) * model + half * (model // 2)
        return att_ref.at[:, pl.ds(pl.multiple_of(at, 128), model // 2)]

    def up_place(call, side):
        at = (core * calls + call) * model
        return up_out.at[side, :, pl.ds(pl.multiple_of(at, 128), model)]

    rounds = max(len(sorder), max(len(stream.rounds) for stream in streams))
    for r in range(rounds):
        for i, stream in enumerate(streams):
            if not stream.done:
                stream.step()
                if stream.done:
                    if i < 2:
                        spread(functools.partial(att_place, i), stream.result)
                    else:
                        spread(functools.partial(up_place, i - 2), stream.result)
        if r < len(sorder):
            scopies[r].wait()
            sbuf[...] = sbuf[...] + sgots[r][...]
            if r + 1 < len(sorder):
                scopies[r + 1].start()
        if r == 1:
            for copy in moves:
                copy.start()

            @pl.when(top == core)
            def _():
                last.wait_recv()
                here[...] = last_ref[...] + last_got[...]
                to_x.start()
                to_core.start()

    table_ref[...] = sbuf[...]
    forwards = []
    for copy, place in after:
        copy.wait_recv()
        other = place(1 - x)
        forwards.append(remote(other, other, core_partner))
        forwards[-1].start()

    @pl.when(top == core)
    def _():
        to_x.wait_recv()
        forward.start()
        to_core.wait_send()
        to_x.wait_send()
        forward.wait_send()

    @pl.when(top != core)
    def _():
        last.wait_send()
        to_core.wait_recv()
        forward.wait_recv()

    for copy, _ in gathers:
        copy.wait()
    for copy in forwards:
        copy.wait()
    for copy, _ in after:
        copy.wait_send()
    for stream in streams:
        stream.close()
    for copy in moves:
        copy.wait()


def flipped(index, offset):
    low, high = index % 2, index // 2
    if offset & 1:
        low = 1 - low
    if offset & 2:
        high = 1 - high
    return 2 * high + low


def finish(dp_bits, up, down, in_term, out_term, tables, rows):
    assert rows.shape[0] == 4
    calls = up.shape[0]
    groups, per, model = out_term.shape
    high = down.shape[0]
    orders = attention_orders(dp_bits)
    ups = up_order(dp_bits)[2:]
    scratch = [s for o in orders for s in stream_scratch(o, (per, model // 2), False)]
    scratch += [s for _ in range(calls) for s in stream_scratch(ups, (per, model), False)]
    scratch.append(pltpu.VMEM((high, model), BF))
    scratch += [pltpu.VMEM((8, model), F32)] * (3 + dp_bits)
    sems = sum(map(len, orders)) + calls * len(ups) + 3 + 4 + 2 + dp_bits + 3 * (calls + 2)
    loads = 2 * 4 * groups + calls
    hbm = pl.BlockSpec(memory_space=pl.ANY)
    vmem = pl.BlockSpec(memory_space=pltpu.VMEM)
    return pl.pallas_call(
        functools.partial(finish_kernel, calls, dp_bits),
        in_specs=[hbm] * 3 + [vmem] * 6,
        out_specs=[vmem] * 5,
        out_shape=[
            jax.ShapeDtypeStruct((per, 4 * model), BF),
            jax.ShapeDtypeStruct((2, per, 2 * calls * model), BF),
            jax.ShapeDtypeStruct((2, high, model), BF),
            jax.ShapeDtypeStruct((8, model), F32),
            jax.ShapeDtypeStruct(rows.shape, BF),
        ],
        scratch_shapes=scratch
        + [
            pltpu.SemaphoreType.DMA((sems,)),
            pltpu.SemaphoreType.DMA((sems,)),
            pltpu.SemaphoreType.DMA((loads,)),
        ],
        compiler_params=pltpu.CompilerParams(
            collective_id=0, has_side_effects=True, vmem_limit_bytes=VMEM_BYTES
        ),
        cost_estimate=pl.CostEstimate(
            flops=0, bytes_accessed=100 * 1024 * 1024, transcendentals=0
        ),
        name="finish",
    )(up, in_term, out_term, *tables, down, rows)


def enter_kernel(tokens_ref, modality_ref, gain_ref, shift_ref, w_ref, *refs):
    refs = list(refs)
    tok_ref, kind_ref, low_ref, qkv_ref, wide_ref, send_ref = draw(refs, 6)
    copies = Copies(*refs)
    me = lax.axis_index("head")
    heads, rows, length, model = tok_ref.shape
    others = [(me // 4) * 4 + flipped(me % 4, o) for o in (3, 2, 1)]
    loads = {
        (o, r): copies.local(tokens_ref.at[to, r], wide_ref.at[to, r])
        for r in range(rows)
        for o, to in enumerate([*others, me])
    }
    kinds = [copies.remote(modality_ref.at[to], kind_ref.at[me], {"head": to}) for to in others]
    sends = {
        (o, r): copies.remote(send_ref.at[to, r], tok_ref.at[me, r], {"head": to})
        for r in range(rows)
        for o, to in enumerate(others)
    }
    for copy in loads.values():
        copy.start()
    barrier = pltpu.get_barrier_semaphore()
    for to in others:
        pl.semaphore_signal(
            barrier, inc=1, device_id={"head": to}, device_id_type=pl.DeviceIdType.MESH
        )
    pl.semaphore_wait(barrier, len(others))
    for copy in kinds:
        copy.start()
    kind_ref[me] = modality_ref[me]
    for r in range(rows):
        for o, to in enumerate(others):
            loads[o, r].wait()
            send_ref[to, r] = wide_ref[to, r].astype(BF)
            sends[o, r].start()
        loads[len(others), r].wait()
        tok_ref[me, r] = wide_ref[me, r].astype(BF)
    for copy in kinds:
        copy.wait()
    ones = jnp.ones((8, length), BF)
    row = lax.broadcasted_iota(jnp.int32, (8, length), 0)
    for r in range(rows):
        for o in range(len(others)):
            sends[o, r].wait_recv()
        for h in range(heads):
            kind = kind_ref[h, r : r + 1, :].astype(F32)
            kind = jnp.where(row == 0, jnp.broadcast_to(kind, (8, length)), 0.0).astype(BF)
            kind = mm_tn(kind, ones)[:, :1]
            z, _ = norm(tok_ref[h, r].astype(F32))
            low = z * jnp.where(kind < 0.5, gain_ref[0:1], gain_ref[1:2])
            low_ref[h, r] = (low + jnp.where(kind < 0.5, shift_ref[0:1], shift_ref[1:2])).astype(BF)
        low = low_ref[:, r].reshape(heads * length, model)
        for n in range(w_ref.shape[1] // model):
            cols = slice(n * model, (n + 1) * model)
            part = mm(low, w_ref[:, cols]).astype(BF)
            qkv_ref[:, r, :, cols] = part.reshape(heads, length, model)
    for copy in sends.values():
        copy.wait_send()


def enter(tokens, modality, gain, shift, weight):
    heads, rows, _, model = tokens.shape
    assert heads == 4
    vmem = pl.BlockSpec(memory_space=pltpu.VMEM)
    sems = 3 * rows + 3
    return pl.pallas_call(
        enter_kernel,
        in_specs=[pl.BlockSpec(memory_space=pl.ANY)] + [vmem] * 4,
        out_specs=[vmem] * 4,
        out_shape=[
            jax.ShapeDtypeStruct(tokens.shape, BF),
            jax.ShapeDtypeStruct(modality.shape, jnp.int32),
            jax.ShapeDtypeStruct(tokens.shape, BF),
            jax.ShapeDtypeStruct(tokens.shape[:3] + weight.shape[1:], BF),
        ],
        scratch_shapes=[
            pltpu.VMEM(tokens.shape, F32),
            pltpu.VMEM(tokens.shape, BF),
            pltpu.SemaphoreType.DMA((sems,)),
            pltpu.SemaphoreType.DMA((sems,)),
            pltpu.SemaphoreType.DMA((4 * rows,)),
        ],
        compiler_params=pltpu.CompilerParams(
            collective_id=2, has_side_effects=True, vmem_limit_bytes=VMEM_BYTES
        ),
        cost_estimate=pl.CostEstimate(
            flops=2 * tokens.size * weight.shape[1], bytes_accessed=40 * 1024 * 1024,
            transcendentals=0,
        ),
        name="enter",
    )(tokens, modality, gain, shift, weight)


def norm(values):
    mean = jnp.mean(values, axis=-1, keepdims=True)
    centered = values - mean
    rstd = lax.rsqrt(jnp.mean(centered * centered, axis=-1, keepdims=True) + EPS)
    return centered * rstd, rstd


def pick(table, kind):
    return jnp.where(kind == 0, table[0], table[1])


def norm_back(grad, gains, z, rstd):
    q = grad * gains
    return rstd * (
        q
        - jnp.mean(q, axis=-1, keepdims=True)
        - z * jnp.mean(q * z, axis=-1, keepdims=True)
    )


def by_expert(values, kind):
    first = jnp.sum(jnp.where(kind == 0, values, 0.0), axis=0)
    second = jnp.sum(jnp.where(kind == 0, 0.0, values), axis=0)
    return jnp.stack([first, second])


def flip(axis, size, bit):
    return functools.partial(
        lax.ppermute, axis_name=axis, perm=[(i, i ^ (1 << bit)) for i in range(size)]
    )


def take(values, dim, index):
    return lax.dynamic_index_in_dim(values, index, dim, keepdims=False)


def body(sizes, tokens, segment, modality, first_gain, first_shift, project_in, project_out,
         second_gain, second_shift, up_weight, down_weight, cotangent):
    heads, groups = sizes["head"], sizes["dp"]
    row_count, length, model = tokens.shape
    rows = row_count // heads
    count = row_count * length
    hidden = up_weight.shape[-1]
    me_h, me_d = lax.axis_index("head"), lax.axis_index("dp")
    core = me_h % 2
    head_bits = heads.bit_length() - 1
    dp_bits = groups.bit_length() - 1
    assert heads == 1 << head_bits and groups == 1 << dp_bits and head_bits >= 2
    hflip = [flip("head", heads, b) for b in range(head_bits)]
    dflip = [flip("dp", groups, b) for b in range(dp_bits)]

    def exchange(values):
        return lax.all_to_all(values, "head", split_axis=0, concat_axis=0, tiled=True)

    grid = (heads, rows, length)
    tok, kind, low1, qkv = enter(
        tokens.reshape(*grid, model), modality.reshape(grid), first_gain, first_shift, project_in
    )
    later, tok = lax.optimization_barrier((cotangent, tok))
    cot = exchange(later.astype(BF).reshape(*grid, model)).reshape(count, model)
    seg = lax.dynamic_slice_in_dim(segment, me_h * rows, rows, 0)
    kind = kind.reshape(count)
    kcol = kind[:, None]

    flat = tok.astype(F32).reshape(count, model)
    z1, rstd1 = norm(flat)
    gain1 = pick(first_gain, kcol)
    context, lse = attention_forward(seg, qkv)
    ctx = context.reshape(count, model)
    attention = mm(ctx, project_out)
    residual = flat + attention
    z2, rstd2 = norm(residual)
    gain2 = pick(second_gain, kcol)
    low2 = (z2 * gain2 + pick(second_shift, kcol)).astype(BF)

    slots = count + BLK
    is0 = (kind == 0).astype(F32).reshape(count // BLK, BLK)
    tri = jnp.triu(jnp.ones((BLK, BLK), F32))
    inner = mm(is0, tri)
    ends = jnp.cumsum(inner[:, -1])
    before = (inner + (ends - inner[:, -1])[:, None]).reshape(count).astype(jnp.int32)
    n0 = ends[-1].astype(jnp.int32)
    blocks0 = (n0 + BLK - 1) // BLK
    blocks1 = (count - n0 + BLK - 1) // BLK
    rank1 = jnp.arange(count, dtype=jnp.int32) - before
    slot = jnp.where(kind == 0, before - 1, blocks0 * BLK + rank1)
    place = (slot[None, :] == jnp.arange(slots, dtype=jnp.int32)[:, None]).astype(BF)

    near = hflip[0]
    g_mine = mm(place, cot).astype(BF)
    g_other = near(g_mine)
    blocks = jnp.stack([blocks0, blocks1])
    blocks_other = near(blocks)
    xbit = (me_h // 2) % 2
    ybit = me_d % 2
    info = jnp.concatenate([blocks, blocks_other, jnp.stack([xbit, ybit, core])]).astype(jnp.int32)
    x_mine = mm(place, low2).astype(BF)
    x_other = near(x_mine)

    partial, kept, came = None, ([], []), ([], [])
    for call in range(CALLS):
        *partial, up_keep, up_send, down_keep, down_send = ffn(
            call, info, x_mine, x_other, g_mine, g_other, up_weight, down_weight, partial, groups
        )
        kept[0].append(up_keep)
        kept[1].append(down_keep)
        came[0].append(hflip[1](up_send))
        came[1].append(dflip[0](down_send))

    partial, early = lax.optimization_barrier((partial, [c[:-1] for c in came]))
    came = [e + c[-1:] for e, c in zip(early, came)]
    branch_mine, branch_other, dx_mine, dx_other = partial
    dx = dx_mine + near(dx_other)
    second_grad = mm_tn(place, dx)
    branch = mm_tn(place, branch_mine + near(branch_other))
    leaving = (attention + branch).astype(BF).reshape(*grid, model)

    cot32 = cot.astype(F32)
    gain2_term = by_expert(second_grad * z2, kcol)
    shift2_term = by_expert(second_grad, kcol)
    extra = norm_back(second_grad, gain2, z2, rstd2)
    attention_low = (cot32 + extra).astype(BF)
    out_term = mm_tn(ctx, attention_low)
    context_grad = mm_nt(attention_low, project_out).astype(BF)
    in_term, first_grad, up_sum, down_sum, back = attention_backward(
        seg, qkv, context_grad.reshape(context.shape), lse, low1, project_in,
        kept[0], came[0], kept[1], came[1], leaving, dp_bits,
    )
    first_grad = first_grad.reshape(count, model)
    gain1_term = by_expert(first_grad * z1, kcol)
    shift1_term = by_expert(first_grad, kcol)
    tail = (extra + norm_back(first_grad, gain1, z1, rstd1)).astype(BF).reshape(*grid, model)

    output = tokens + back.reshape(row_count, length, model).astype(F32)
    att_sum, up_sum, down_sum, table, home = finish(
        dp_bits, up_sum, down_sum, in_term,
        out_term.astype(BF).reshape(groups, model // groups, model),
        (gain1_term, shift1_term, gain2_term, shift2_term), tail,
    )
    input_grad = cotangent + home.reshape(row_count, length, model).astype(F32)

    up_grad, down_grad = up_sum.astype(F32), down_sum.astype(F32)
    in_grad = att_sum[:, : 3 * model].astype(F32)
    out_grad = att_sum[:, 3 * model :].astype(F32)
    tables = lax.dynamic_slice_in_dim(table, me_d * (model // groups), model // groups, 1)
    tables = tables.reshape(4, EXPERTS, model // groups)
    return (
        output, input_grad, tables[0], tables[1], in_grad, out_grad, tables[2], tables[3],
        up_grad, down_grad,
    )


def solution(mesh):
    return jax.shard_map(
        functools.partial(body, dict(mesh.shape)),
        mesh=mesh,
        in_specs=(
            P("dp", "head", None),
            P("dp", None),
            P("dp", "head"),
            P(),
            P(),
            P(),
            P(),
            P(),
            P(),
            P(),
            P(),
            P("dp", "head", None),
        ),
        out_specs=(
            P("dp", "head", None),
            P("dp", "head", None),
            P(None, "dp"),
            P(None, "dp"),
            P("dp", None),
            P("dp", None),
            P(None, "dp"),
            P(None, "dp"),
            P(None, "dp", None),
            P(None, "dp", None),
        ),
        check_vma=False,
    )
```

```python
import functools

import jax
import jax.numpy as jnp
from jax import lax
from jax.experimental import pallas as pl
from jax.experimental.pallas import tpu as pltpu
from jax.sharding import PartitionSpec as P

HEAD_DIM = 64
EXPERTS = 2
EPS = 1e-05
NEG = -1000000000.0
BLK = 128
CALLS = 2
VMEM_BYTES = 60 * 1024 * 1024
BF = jnp.bfloat16
F32 = jnp.float32
NT = (((1,), (1,)), ((), ()))
TN = (((0,), (0,)), ((), ()))


def mm(a, b):
    return jnp.dot(a, b, preferred_element_type=F32)


def mm_nt(a, b):
    return lax.dot_general(a, b, NT, preferred_element_type=F32)


def mm_tn(a, b):
    return lax.dot_general(a, b, TN, preferred_element_type=F32)


def bias_of(segc_ref, segr_ref, bias_ref):
    same = segc_ref[0] == segr_ref[0]
    bias_ref[...] = jnp.where(same, 0.0, NEG)


def attn_specs(sub, length, pairs):
    def part(i):
        return pl.BlockSpec((sub, 1, length, 128), lambda r, j, i=i: (0, r, 0, i * pairs + j))

    return part


def ffn_kernel(first, bits, info_ref, xm_ref, xo_ref, gm_ref, go_ref, u_ref, d_ref, *refs):
    if first:
        prev = (None,) * 4
        outs, grads = refs[:4], refs[4:8]
    else:
        prev, outs, grads = refs[:4], refs[4:8], refs[8:12]
    du_ref, dd_ref, act_ref, dh_ref = refs[-4:]
    e = pl.program_id(0)
    slots, model = xm_ref.shape
    cols = u_ref.shape[-1]
    tile = 256
    down = d_ref[0]

    @pl.when(e == 0)
    def _():
        for out in outs:
            out[slots - BLK :, :] = jnp.zeros((BLK, model), BF)

    du_ref[...] = jnp.zeros_like(du_ref)
    dd_ref[...] = jnp.zeros_like(dd_ref)

    def chunk(which, block, count):
        size = count * BLK
        rows = pl.ds(pl.multiple_of(block * BLK, BLK), size)
        x = (xm_ref, xo_ref)[which][rows, :]
        g = (gm_ref, go_ref)[which][rows, :]
        for n in range(cols // tile):
            part = slice(n * tile, (n + 1) * tile)
            h = mm(x, u_ref[0, :, part])
            da = mm_nt(g, down[part, :])
            cdf = 0.5 + 0.5 * lax.erf(h * 0.7071067811865476)
            pdf = 0.3989422804014327 * jnp.exp(-0.5 * h * h)
            act_ref[:size, part] = (h * cdf).astype(BF)
            dh_ref[:size, part] = (da * (cdf + h * pdf)).astype(BF)
        act = act_ref[:size, :]
        dh = dh_ref[:size, :]
        for slot, value in ((which, mm(act, down)), (2 + which, mm_nt(dh, u_ref[0]))):
            if prev[slot] is not None:
                value = value + prev[slot][rows, :].astype(F32)
            outs[slot][rows, :] = value.astype(BF)
        du_ref[...] += mm_tn(x, dh)
        dd_ref[...] += mm_tn(act, g)

    for which in range(2):
        n0 = info_ref[2 * which]
        n1 = info_ref[2 * which + 1]
        start = jnp.where(e == 0, 0, n0)
        count = jnp.where(e == 0, n0, n1)

        def four(i, carry, which=which, start=start):
            chunk(which, start + 4 * i, 4)
            return carry

        lax.fori_loop(0, count // 4, four, 0)
        at2 = start + (count // 4) * 4

        @pl.when((count // 2) % 2 == 1)
        def _(which=which, at2=at2):
            chunk(which, at2, 2)

        at1 = start + (count // 2) * 2

        @pl.when(count % 2 == 1)
        def _(which=which, at1=at1):
            chunk(which, at1, 1)

    up_keep, up_send, down_keep, down_send = grads
    groups = 1 << bits
    per = model // groups
    wide = down_keep.shape[2]
    xbit, ybit = info_ref[4], info_ref[5]
    for ref, here in ((up_keep, e == xbit), (up_send, e != xbit)):

        @pl.when(here)
        def _(ref=ref):
            for p in range(groups):
                ref[spot(p, range(bits))] = du_ref[p * per : (p + 1) * per, :].astype(BF)

    for y in range(2):
        for ref, here in ((down_keep, ybit == y), (down_send, ybit != y)):

            @pl.when(here)
            def _(ref=ref, y=y):
                for p in range(y, cols // wide, 2):
                    at = spot(p >> 1, range(bits - 3))
                    ref[at, e] = dd_ref[p * wide : (p + 1) * wide, :].astype(BF)


def spot(index, order):
    return functools.reduce(lambda acc, bit: 2 * acc + (index >> bit & 1), order, 0)


def ffn(call, info, x_mine, x_other, g_mine, g_other, up, down, partial, groups):
    slots, model = x_mine.shape
    hidden = up.shape[-1]
    cols = hidden // (2 * CALLS)
    bits = groups.bit_length() - 1
    whole = pl.BlockSpec((slots, model), lambda e, i: (0, 0), pipeline_mode=pl.Buffered(1))
    first = partial is None
    extra = () if first else tuple(partial)
    grads = [(groups, model // groups, model)] * 2
    grads += [(groups // 8, EXPERTS, hidden // groups, model)] * 2
    return pl.pallas_call(
        functools.partial(ffn_kernel, first, bits),
        grid_spec=pltpu.PrefetchScalarGridSpec(
            num_scalar_prefetch=1,
            grid=(EXPERTS,),
            in_specs=[whole] * 4
            + [
                pl.BlockSpec((1, model, cols), lambda e, i: (e, 0, i[6] * CALLS + call)),
                pl.BlockSpec((1, cols, model), lambda e, i: (e, i[6] * CALLS + call, 0)),
            ]
            + [whole] * len(extra),
            out_specs=[pl.BlockSpec((slots, model), lambda e, i: (0, 0))] * 4
            + [pl.BlockSpec(g, lambda e, i, n=len(g): (0,) * n) for g in grads],
            scratch_shapes=[
                pltpu.VMEM((model, cols), F32),
                pltpu.VMEM((cols, model), F32),
                pltpu.VMEM((4 * BLK, cols), BF),
                pltpu.VMEM((4 * BLK, cols), BF),
            ],
        ),
        out_shape=[jax.ShapeDtypeStruct((slots, model), BF)] * 4
        + [jax.ShapeDtypeStruct(g, BF) for g in grads],
        compiler_params=pltpu.CompilerParams(vmem_limit_bytes=VMEM_BYTES),
        cost_estimate=pl.CostEstimate(
            flops=12 * 2 * slots * model * cols, bytes_accessed=40 * 1024 * 1024,
            transcendentals=2 * 2 * slots * cols,
        ),
        name="ffn",
    )(info, x_mine, x_other, g_mine, g_other, up, down, *extra)


def peers():
    out = {}
    for axis in ("head", "dp"):
        me = lax.axis_index(axis)
        for b in range(lax.axis_size(axis).bit_length() - 1):
            bit = (me // (1 << b)) % 2
            out[axis, b] = bit, {axis: me + (1 - 2 * bit) * (1 << b)}
    return out


class Halving:
    def __init__(self, env, order, buf, gots, first, remote):
        self.rounds, path, prev = [], (), first
        for o, got in zip(order, gots):
            bit, partner = env[o]
            view = buf.at[path] if path else buf
            away, stay = view.at[1 - bit], view.at[bit]
            halves = (None, None) if prev is None else (prev.at[1 - bit], prev.at[bit])
            self.rounds.append((away, stay, *halves, remote(away, got, partner)))
            path, prev = path + (bit,), got
        self.result, self.last, self.at = buf.at[path], prev, 0
        self.done = False

    def send(self):
        away, stay, got_away, got_stay, copy = self.rounds[self.at]
        accumulate(away, got_away)
        copy.start()
        accumulate(stay, got_stay)

    def step(self):
        self.rounds[self.at][-1].wait_recv()
        self.at += 1
        if self.at < len(self.rounds):
            self.send()
        else:
            accumulate(self.result, self.last)
            self.done = True

    def close(self):
        for *_, copy in self.rounds:
            copy.wait_send()


def spots(ref):
    lead = len(ref.shape) - 2
    return [tuple(i >> b & 1 for b in range(lead)) for i in range(1 << lead)]


def accumulate(into, got):
    if got is not None:
        for at in spots(into):
            at = at or ...
            into[at] = into[at] + got[at]


def neighbours(env):
    me = lax.axis_index("head")
    out = [partner for _, partner in env.values()]
    for o in range(1, lax.axis_size("head")):
        if o & (o - 1):
            out.append({"head": (me // 4) * 4 + flipped(me % 4, o)})
    return out


def greet(env):
    barrier = pltpu.get_barrier_semaphore()
    partners = neighbours(env)
    for partner in partners:
        pl.semaphore_signal(barrier, inc=1, device_id=partner, device_id_type=pl.DeviceIdType.MESH)
    pl.semaphore_wait(barrier, len(partners))


class Copies:
    def __init__(self, send_sem, recv_sem, load_sem):
        self.send_sem, self.recv_sem, self.load_sem = send_sem, recv_sem, load_sem
        self.used, self.loads = 0, 0

    def remote(self, src, dst, to):
        s = self.used
        self.used += 1
        return pltpu.make_async_remote_copy(
            src_ref=src, dst_ref=dst, send_sem=self.send_sem.at[s], recv_sem=self.recv_sem.at[s],
            device_id=to, device_id_type=pl.DeviceIdType.MESH,
        )

    def local(self, src, dst):
        self.loads += 1
        return pltpu.make_async_copy(src, dst, self.load_sem.at[self.loads - 1])


def draw(refs, k):
    out = refs[:k]
    del refs[:k]
    return out


def others():
    me = lax.axis_index("head")
    return [(me // 4) * 4 + flipped(me % 4, o) for o in (3, 2, 1)]


def attn_fwd_kernel(
    segc_ref, segr_ref, q_ref, k_ref, v_ref, cot_ref, o_ref, lse_ref, got_ref,
    bias_ref, wide_ref, send_ref, *sems,
):
    sub, _, length, width = q_ref.shape
    seq = sub * length
    copies = Copies(*sems)
    me = lax.axis_index("head")
    targets = others()
    order = [*targets, me]
    loads = [copies.local(cot_ref.at[to], wide_ref.at[to]) for to in order]
    sends = [copies.remote(send_ref.at[to], got_ref.at[me], {"head": to}) for to in targets]
    stays = copies.local(send_ref.at[me], got_ref.at[me])
    barrier = pltpu.get_barrier_semaphore()
    at = pl.program_id(0) * pl.num_programs(1) + pl.program_id(1)

    @pl.when(at == 0)
    def _():
        for copy in loads:
            copy.start()
        for to in targets:
            pl.semaphore_signal(
                barrier, inc=1, device_id={"head": to}, device_id_type=pl.DeviceIdType.MESH
            )

    @pl.when(at == 1)
    def _():
        pl.semaphore_wait(barrier, len(targets))
        for to, load, copy in zip(order, loads, [*sends, stays]):
            load.wait()
            send_ref[to] = wide_ref[to].astype(BF)
            copy.start()

    @pl.when(at == pl.num_programs(0) * pl.num_programs(1) - 1)
    def _():
        for copy in [*sends, stays]:
            copy.wait()

    @pl.when(pl.program_id(1) == 0)
    def _():
        bias_of(segc_ref, segr_ref, bias_ref)

    q = q_ref[...].reshape(seq, width) * jnp.asarray(HEAD_DIM**-0.5, BF)
    k = k_ref[...].reshape(seq, width)
    vt = v_ref[...].reshape(seq, width).T
    lane = lax.broadcasted_iota(jnp.int32, (1, width), 1) // HEAD_DIM
    zero = jnp.zeros((), BF)
    per = width // HEAD_DIM
    step = 2 * length
    ks = [jnp.where(lane == h, k, zero) for h in range(per)]
    for b in range(seq // step):
        cols = slice(b * step, (b + 1) * step)
        parts = []
        for h in range(per):
            s = mm_nt(ks[h], q[cols]) + bias_ref[:, cols]
            top = jnp.max(s, axis=0, keepdims=True)
            e = jnp.exp(s - top)
            total = jnp.sum(e, axis=0, keepdims=True)
            parts.append(mm(vt[h * HEAD_DIM : (h + 1) * HEAD_DIM], e.astype(BF)) * (1.0 / total))
            lse_ref[0, 0, h : h + 1, cols] = top + jnp.log(total)
        out = jnp.concatenate(parts, axis=0).T.astype(BF)
        o_ref[2 * b : 2 * b + 2, 0] = out.reshape(2, length, width)


def attention_forward(segment, qkv, cotangent):
    sub, rows, length, wide = qkv.shape
    seq = sub * length
    model = wide // 3
    pairs = model // 128
    part = attn_specs(sub, length, pairs)
    hbm = pl.BlockSpec(memory_space=pl.ANY)
    return pl.pallas_call(
        attn_fwd_kernel,
        grid=(rows, pairs),
        in_specs=[
            pl.BlockSpec((1, seq, 1), lambda r, j: (r, 0, 0)),
            pl.BlockSpec((1, 1, seq), lambda r, j: (r, 0, 0)),
            part(0),
            part(1),
            part(2),
            hbm,
        ],
        out_specs=[part(0), pl.BlockSpec((1, 1, 2, seq), lambda r, j: (r, j, 0, 0)), hbm],
        out_shape=[
            jax.ShapeDtypeStruct((sub, rows, length, model), BF),
            jax.ShapeDtypeStruct((rows, pairs, 2, seq), F32),
            jax.ShapeDtypeStruct(cotangent.shape, BF),
        ],
        scratch_shapes=[
            pltpu.VMEM((seq, seq), F32),
            pltpu.VMEM(cotangent.shape, F32),
            pltpu.VMEM(cotangent.shape, BF),
            pltpu.SemaphoreType.DMA((3,)),
            pltpu.SemaphoreType.DMA((3,)),
            pltpu.SemaphoreType.DMA((5,)),
        ],
        compiler_params=pltpu.CompilerParams(
            collective_id=3, has_side_effects=True, vmem_limit_bytes=VMEM_BYTES
        ),
        cost_estimate=pl.CostEstimate(
            flops=8 * rows * seq * seq * model, bytes_accessed=8 * rows * seq * model,
            transcendentals=rows * seq * seq * model // HEAD_DIM,
        ),
        name="attn_fwd",
    )(segment[:, :, None], segment[:, None, :], qkv, qkv, qkv, cotangent)


def up_order(dp_bits):
    return [("dp", b) for b in range(dp_bits)]


def down_order(dp_bits):
    return [("dp", b) for b in range(1, dp_bits - 1)] + [("head", 1)]


def attention_orders(dp_bits):
    rest = [("dp", b) for b in range(1, dp_bits)]
    core, x, y = ("head", 0), ("head", 1), ("dp", 0)
    return [core, y, x] + rest, [core, x, y] + rest


def stream_scratch(order, tail, first):
    sizes = [len(order)] * (2 if first else 1) + [len(order) - r for r in range(1, len(order) + 1)]
    return [pltpu.VMEM((2,) * k + tail, BF) for k in sizes]


def attn_bwd_kernel(calls, dp_bits, *refs):
    refs = list(refs)
    segc_ref, segr_ref, q_ref, k_ref, v_ref, do_ref, lse_ref, low_ref, w_ref = draw(refs, 9)
    tok_ref, extra_ref, col_ref, gain_ref = draw(refs, 4)
    up_kept, up_came, down_kept, down_came = (draw(refs, calls) for _ in range(4))
    leaving_ref, in_ref, table_ref, tail_ref, up_ref, down_ref, back_ref, home_ref = draw(refs, 8)
    bias_ref, dqkv_ref, lowt_ref, acc_ref, first_ref, rows_ref = draw(refs, 6)
    env = peers()
    copies = Copies(*refs[-3:])
    r, j = pl.program_id(0), pl.program_id(1)
    rows, pairs = pl.num_programs(0), pl.num_programs(1)
    me = lax.axis_index("head")

    streams, loads = [], []
    order = up_order(dp_bits)[:2]
    for i in range(calls):
        buf, first, *gots = draw(refs, 2 + len(order))
        loads.append([copies.local(up_kept[i], buf), copies.local(up_came[i], first)])
        streams.append(Halving(env, order, buf, gots, first, copies.remote))
    order = down_order(dp_bits)
    buf, first, *gots = draw(refs, 2 + len(order))
    lead = dp_bits - 3
    loads.append([])
    for i in range(calls):
        for p in range(1 << lead):
            at = tuple(p >> (lead - 1 - b) & 1 for b in range(lead)) + (i,)
            loads[-1].append(copies.local(down_kept[i].at[p], buf.at[at]))
            loads[-1].append(copies.local(down_came[i].at[p], first.at[at]))
    streams.append(Halving(env, order, buf, gots, first, copies.remote))
    moves = []
    for o in range(1, 4):
        to = (me // 4) * 4 + flipped(me % 4, o)
        moves.append(copies.remote(leaving_ref.at[to], back_ref.at[me], {"head": to}))
    stays = [copies.local(leaving_ref.at[me], back_ref.at[me])]
    early = rows_ref.shape[1]
    homes = []
    for i in range(early):
        homes.append([copies.local(rows_ref.at[me, i], home_ref.at[me, i])])
        for to in others():
            homes[i].append(copies.remote(rows_ref.at[to, i], home_ref.at[me, i], {"head": to}))

    @pl.when((r == 0) & (j == 0))
    def _():
        for group in loads:
            for copy in group:
                copy.start()
        stays[0].start()
        greet(env)
        for stream, group in zip(reversed(streams), reversed(loads)):
            for copy in group:
                copy.wait()
            stream.send()
        for copy in moves:
            copy.start()

    @pl.when((r == rows - 1) & (j == 0))
    def _():
        streams[0].step()

    sub, _, length, width = q_ref.shape
    seq = sub * length
    model = dqkv_ref.shape[-1] // 3

    @pl.when(j == 0)
    def _():
        bias_of(segc_ref, segr_ref, bias_ref)

    scale = HEAD_DIM**-0.5
    q = q_ref[...].reshape(seq, width) * jnp.asarray(scale, BF)
    k = k_ref[...].reshape(seq, width)
    kt = k.T
    v = v_ref[...].reshape(seq, width)
    do = do_ref[...].reshape(seq, width)
    lane = lax.broadcasted_iota(jnp.int32, (1, width), 1) // HEAD_DIM
    zero = jnp.zeros((), BF)
    per = width // HEAD_DIM
    step = 2 * length
    dk = jnp.zeros((seq, width), F32)
    dv = jnp.zeros((seq, width), F32)
    dqs = [[] for _ in range(seq // step)]
    for h in range(per):
        kh = jnp.where(lane == h, k, zero)
        vh = jnp.where(lane == h, v, zero)
        qh = jnp.where(lane == h, q, zero)
        doh = jnp.where(lane == h, do, zero)
        for b in range(seq // step):
            cols = slice(b * step, (b + 1) * step)
            s = mm_nt(kh, q[cols]) + bias_ref[:, cols]
            p = jnp.exp(s - lse_ref[0, 0, h : h + 1, cols])
            dp = mm_nt(vh, do[cols])
            ds = (p * (dp - jnp.sum(p * dp, axis=0, keepdims=True))).astype(BF)
            dv = dv + mm(p.astype(BF), doh[cols])
            dk = dk + mm(ds, qh[cols])
            dqs[b].append(mm(kt[h * HEAD_DIM : (h + 1) * HEAD_DIM], ds) * scale)
    dq = jnp.concatenate([jnp.concatenate(d, axis=0).T for d in dqs], axis=0)
    for i, g in enumerate((dq, dk, dv)):
        at = pl.multiple_of(i * model + j * width, width)
        dqkv_ref[:, pl.ds(at, width)] = g.astype(BF)

    @pl.when((r == rows - 1) & (j == pairs - 1))
    def _():
        for stream in streams[1:]:
            stream.step()

    @pl.when(j == pairs - 1)
    def _():
        tile = 256
        lowt_ref[...] = low_ref[...].reshape(seq, model).T
        first_ref[...] = jnp.zeros_like(first_ref)

        @pl.when(r == 0)
        def _():
            acc_ref[...] = jnp.zeros_like(acc_ref)
            table_ref[...] = jnp.zeros_like(table_ref)

        def piece(n, carry):
            cols = pl.ds(pl.multiple_of(n * tile, tile), tile)
            part = dqkv_ref[:, cols]
            acc_ref[:, cols] += mm(lowt_ref[...], part)
            first_ref[...] += mm_nt(part, w_ref[:, cols])
            return carry

        lax.fori_loop(0, 3 * model // tile, piece, 0)
        for h in range(sub):
            grad = first_ref[h * length : (h + 1) * length, :]
            vision = col_ref[h, 0] > 0.5
            z, rstd = norm(tok_ref[h, 0].astype(F32))
            gain = jnp.where(vision, gain_ref[1:2], gain_ref[0:1])
            for i, term in enumerate((grad * z, grad)):
                for e, part in enumerate((jnp.where(vision, 0.0, term), jnp.where(vision, term, 0.0))):
                    at = 2 * i + e
                    table_ref[at : at + 1, :] += jnp.sum(part, axis=0, keepdims=True)
            tail = (extra_ref[h, 0] + norm_back(grad, gain, z, rstd)).astype(BF)

            @pl.when(r < early)
            def _(h=h, tail=tail):
                rows_ref[h, jnp.minimum(r, early - 1)] = tail

            @pl.when(r == early)
            def _(h=h, tail=tail):
                tail_ref[h, 0] = tail

        for i in range(early):

            @pl.when(r == i)
            def _(i=i):
                for copy in homes[i]:
                    copy.start()

    @pl.when((r == rows - 1) & (j == pairs - 1))
    def _():
        height = in_ref.shape[1]
        for p in range(in_ref.shape[0]):
            in_ref[p] = acc_ref[p * height : (p + 1) * height, :].astype(BF)
        while not all(stream.done for stream in streams):
            for stream in streams:
                if not stream.done:
                    stream.step()
        for i in range(calls):
            for at in spots(streams[i].result):
                up_ref[(i, *at)] = streams[i].result[at or ...]
        down_ref[...] = streams[-1].result[...]
        for copy in [*stays, *moves, *sum(homes, [])]:
            copy.wait()
        for stream in streams:
            stream.close()


def attention_backward(
    segment, qkv, grad, lse, low, weight, tok, extra, col, gain, up_kept, up_came, down_kept, down_came, leaving, dp_bits
):
    sub, rows, length, wide = qkv.shape
    seq = sub * length
    model = wide // 3
    pairs = model // 128
    groups = 1 << dp_bits
    calls = len(up_kept)
    part = attn_specs(sub, length, pairs)
    per, high = model // groups, down_kept[0].shape[2]
    row = pl.BlockSpec((sub, 1, length, model), lambda r, j: (0, r, 0, 0))
    hbm = pl.BlockSpec(memory_space=pl.ANY)

    def fixed(*shape):
        return pl.BlockSpec(shape, lambda r, j: (0,) * len(shape), pipeline_mode=pl.Buffered(1))

    up_kept, up_came = (
        [k.reshape((2,) * dp_bits + (per, model)) for k in ks] for ks in (up_kept, up_came)
    )
    ups, downs = up_order(dp_bits), down_order(dp_bits)
    scratch = [
        s
        for _ in range(calls)
        for s in [pltpu.VMEM((2,) * dp_bits + (per, model), BF)] * 2
        + [pltpu.VMEM((2,) * (dp_bits - 1 - i) + (per, model), BF) for i in range(2)]
    ]
    scratch += stream_scratch(downs, (high, model), True)
    sems = 2 * calls + len(downs) + 3 * rows
    loads = 2 * calls + 2 * calls * (groups // 8) + rows
    up_tail = (calls,) + (2,) * (dp_bits - 2) + (per, model)
    return pl.pallas_call(
        functools.partial(attn_bwd_kernel, calls, dp_bits),
        grid=(rows, pairs),
        in_specs=[
            pl.BlockSpec((1, seq, 1), lambda r, j: (r, 0, 0)),
            pl.BlockSpec((1, 1, seq), lambda r, j: (r, 0, 0)),
            part(0),
            part(1),
            part(2),
            part(0),
            pl.BlockSpec((1, 1, 2, seq), lambda r, j: (r, j, 0, 0)),
            row,
            fixed(*weight.shape),
            row,
            row,
            pl.BlockSpec((sub, 1, length, 1), lambda r, j: (0, r, 0, 0)),
            fixed(*gain.shape),
        ]
        + [hbm] * (4 * calls + 1),
        out_specs=[
            fixed(groups, per, wide), fixed(4, model), fixed(sub, 1, length, model),
            fixed(*up_tail), fixed(high, model), hbm, hbm,
        ],
        out_shape=[
            jax.ShapeDtypeStruct((groups, per, wide), BF),
            jax.ShapeDtypeStruct((4, model), F32),
            jax.ShapeDtypeStruct((sub, 1, length, model), BF),
            jax.ShapeDtypeStruct(up_tail, BF),
            jax.ShapeDtypeStruct((high, model), BF),
            jax.ShapeDtypeStruct(leaving.shape, BF),
            jax.ShapeDtypeStruct((sub, rows - 1, length, model), BF),
        ],
        scratch_shapes=[
            pltpu.VMEM((seq, seq), F32),
            pltpu.VMEM((seq, wide), BF),
            pltpu.VMEM((model, seq), BF),
            pltpu.VMEM((model, wide), F32),
            pltpu.VMEM((seq, model), F32),
            pltpu.VMEM((sub, rows - 1, length, model), BF),
        ]
        + scratch
        + [
            pltpu.SemaphoreType.DMA((sems,)),
            pltpu.SemaphoreType.DMA((sems,)),
            pltpu.SemaphoreType.DMA((loads,)),
        ],
        compiler_params=pltpu.CompilerParams(
            collective_id=1, has_side_effects=True, vmem_limit_bytes=VMEM_BYTES
        ),
        cost_estimate=pl.CostEstimate(
            flops=20 * rows * seq * seq * model + 4 * rows * seq * model * wide,
            bytes_accessed=100 * 1024 * 1024,
            transcendentals=rows * seq * seq * model // HEAD_DIM,
        ),
        name="attn_bwd",
    )(
        segment[:, :, None], segment[:, None, :], qkv, qkv, qkv, grad, lse, low, weight,
        tok, extra, col, gain,
        *up_kept, *up_came, *down_kept, *down_came, leaving,
    )


def finish_kernel(calls, dp_bits, *refs):
    refs = list(refs)
    up_ref, in_ref, out_ref = draw(refs, 3)
    tables = draw(refs, 3)
    last_ref, rows_ref, att_ref, up_out, down_ref, table_ref, home_ref = draw(refs, 7)
    env = peers()
    copies = Copies(*refs[-3:])
    remote = copies.remote
    core, x = env["head", 0][0], env["head", 1][0]
    me = lax.axis_index("head")
    groups = 1 << dp_bits
    model = home_ref.shape[-1]
    x_partner, core_partner = env["head", 1][1], env["head", 0][1]

    streams, loads = [], []
    for half, order in enumerate(attention_orders(dp_bits)):
        buf, *gots = draw(refs, 1 + len(order))
        loads.append([])
        lanes = buf.shape[-1]
        for i in range(4):
            ref, start = (out_ref, 0) if i == 3 else (in_ref, i * model)
            for p in range(groups):
                spot_of = {("head", 0): i >> 1, ("head", 1): i & 1}
                spot_of.update({("dp", b): p >> b & 1 for b in range(dp_bits)})
                cols = pl.ds(start + half * lanes, lanes)
                loads[-1].append(
                    copies.local(ref.at[p, :, cols], buf.at[tuple(spot_of[o] for o in order)])
                )
        streams.append(Halving(env, order, buf, gots, None, remote))
    order = up_order(dp_bits)[2:]
    for i in range(calls):
        buf, *gots = draw(refs, 1 + len(order))
        loads.append([copies.local(up_ref.at[i], buf)])
        streams.append(Halving(env, order, buf, gots, None, remote))
    (last_got,) = draw(refs, 1)
    sbuf, *sgots = draw(refs, 3 + dp_bits)

    for group in loads:
        for copy in group:
            copy.start()
    moves = []
    for o in range(1, 4):
        to = (me // 4) * 4 + flipped(me % 4, o)
        moves.append(remote(rows_ref.at[to], home_ref.at[me], {"head": to}))

    top, beyond = env["dp", dp_bits - 1]
    here, over = down_ref.at[x], down_ref.at[1 - x]
    last = remote(last_ref, last_got, beyond)
    to_x, to_core = remote(here, here, x_partner), remote(here, here, core_partner)
    forward = remote(over, over, core_partner)
    greet(env)

    @pl.when(top != core)
    def _():
        last.start()

    for stream, group in zip(streams, loads):
        for copy in group:
            copy.wait()
        stream.send()

    for at, ref in zip((0, 4, 6), tables):
        sbuf[at : at + ref.shape[0], :] = ref[...]
    sorder = [("head", 0), ("head", 1)] + [("dp", b) for b in range(dp_bits)]
    scopies = [remote(sbuf, got, env[o][1]) for o, got in zip(sorder, sgots)]
    scopies[0].start()
    home_ref[me] = rows_ref[me]

    gathers, after = [], []

    def spread(place, value):
        mine = place(x)
        mine[...] = value[...]
        for to, where in ((x_partner, after), (core_partner, gathers)):
            copy = remote(mine, mine, to)
            copy.start()
            where.append((copy, place))

    def att_place(half, side):
        at = (2 * core + side) * model + half * (model // 2)
        return att_ref.at[:, pl.ds(pl.multiple_of(at, 128), model // 2)]

    def up_place(call, side):
        at = (core * calls + call) * model
        return up_out.at[side, :, pl.ds(pl.multiple_of(at, 128), model)]

    rounds = max(len(sorder), max(len(stream.rounds) for stream in streams))
    for r in range(rounds):
        for i, stream in enumerate(streams):
            if not stream.done:
                stream.step()
                if stream.done:
                    if i < 2:
                        spread(functools.partial(att_place, i), stream.result)
                    else:
                        spread(functools.partial(up_place, i - 2), stream.result)
        if r < len(sorder):
            scopies[r].wait()
            sbuf[...] = sbuf[...] + sgots[r][...]
            if r + 1 < len(sorder):
                scopies[r + 1].start()
        if r == 1:
            for copy in moves:
                copy.start()

            @pl.when(top == core)
            def _():
                last.wait_recv()
                here[...] = last_ref[...] + last_got[...]
                to_x.start()
                to_core.start()

    table_ref[...] = sbuf[...]
    forwards = []
    for copy, place in after:
        copy.wait_recv()
        other = place(1 - x)
        forwards.append(remote(other, other, core_partner))
        forwards[-1].start()

    @pl.when(top == core)
    def _():
        to_x.wait_recv()
        forward.start()
        to_core.wait_send()
        to_x.wait_send()
        forward.wait_send()

    @pl.when(top != core)
    def _():
        last.wait_send()
        to_core.wait_recv()
        forward.wait_recv()

    for copy, _ in gathers:
        copy.wait()
    for copy in forwards:
        copy.wait()
    for copy, _ in after:
        copy.wait_send()
    for stream in streams:
        stream.close()
    for copy in moves:
        copy.wait()


def flipped(index, offset):
    low, high = index % 2, index // 2
    if offset & 1:
        low = 1 - low
    if offset & 2:
        high = 1 - high
    return 2 * high + low


def finish(dp_bits, up, down, in_term, out_term, tables, rows):
    assert rows.shape[0] == 4
    calls = up.shape[0]
    groups, per, model = out_term.shape
    high = down.shape[0]
    orders = attention_orders(dp_bits)
    ups = up_order(dp_bits)[2:]
    scratch = [s for o in orders for s in stream_scratch(o, (per, model // 2), False)]
    scratch += [s for _ in range(calls) for s in stream_scratch(ups, (per, model), False)]
    scratch.append(pltpu.VMEM((high, model), BF))
    scratch += [pltpu.VMEM((8, model), F32)] * (3 + dp_bits)
    sems = sum(map(len, orders)) + calls * len(ups) + 3 + 4 + 2 + dp_bits + 3 * (calls + 2)
    loads = 2 * 4 * groups + calls
    hbm = pl.BlockSpec(memory_space=pl.ANY)
    vmem = pl.BlockSpec(memory_space=pltpu.VMEM)
    return pl.pallas_call(
        functools.partial(finish_kernel, calls, dp_bits),
        in_specs=[hbm] * 3 + [vmem] * 5,
        out_specs=[vmem] * 5,
        out_shape=[
            jax.ShapeDtypeStruct((per, 4 * model), BF),
            jax.ShapeDtypeStruct((2, per, 2 * calls * model), BF),
            jax.ShapeDtypeStruct((2, high, model), BF),
            jax.ShapeDtypeStruct((8, model), F32),
            jax.ShapeDtypeStruct(rows.shape, BF),
        ],
        scratch_shapes=scratch
        + [
            pltpu.SemaphoreType.DMA((sems,)),
            pltpu.SemaphoreType.DMA((sems,)),
            pltpu.SemaphoreType.DMA((loads,)),
        ],
        compiler_params=pltpu.CompilerParams(
            collective_id=0, has_side_effects=True, vmem_limit_bytes=VMEM_BYTES
        ),
        cost_estimate=pl.CostEstimate(
            flops=0, bytes_accessed=100 * 1024 * 1024, transcendentals=0
        ),
        name="finish",
    )(up, in_term, out_term, *tables, down, rows)


def enter_kernel(tokens_ref, modality_ref, gain_ref, shift_ref, w_ref, *refs):
    refs = list(refs)
    tok_ref, kind_ref, col_ref, low_ref, qkv_ref, wide_ref, send_ref = draw(refs, 7)
    copies = Copies(*refs)
    me = lax.axis_index("head")
    heads, rows, length, model = tok_ref.shape
    core = me % 2
    targets = others()
    loads = {
        (o, r): copies.local(tokens_ref.at[to, r], wide_ref.at[to, r])
        for r in range(rows)
        for o, to in enumerate([*targets, me])
    }
    kinds = [copies.remote(modality_ref.at[to // 2], kind_ref.at[me], {"head": to}) for to in targets]
    sends = {
        (o, r): copies.remote(send_ref.at[to, r], tok_ref.at[me, r], {"head": to})
        for r in range(rows)
        for o, to in enumerate(targets)
    }
    for copy in loads.values():
        copy.start()
    barrier = pltpu.get_barrier_semaphore()
    for to in targets:
        pl.semaphore_signal(
            barrier, inc=1, device_id={"head": to}, device_id_type=pl.DeviceIdType.MESH
        )
    pl.semaphore_wait(barrier, len(targets))
    for copy in kinds:
        copy.start()
    kind_ref[me] = modality_ref[me // 2]
    for r in range(rows):
        for o, to in enumerate(targets):
            loads[o, r].wait()
            send_ref[to, r] = wide_ref[to, r].astype(BF)
            sends[o, r].start()
        loads[len(targets), r].wait()
        tok_ref[me, r] = wide_ref[me, r].astype(BF)
    for copy in kinds:
        copy.wait()
    ones = jnp.ones((8, length), BF)
    row = lax.broadcasted_iota(jnp.int32, (8, length), 0)
    for r in range(rows):
        for o in range(len(targets)):
            sends[o, r].wait_recv()
        for h in range(heads):
            kind = kind_ref[h, core, r : r + 1, :].astype(F32)
            kind = jnp.where(row == 0, jnp.broadcast_to(kind, (8, length)), 0.0).astype(BF)
            kind = mm_tn(kind, ones)[:, :1]
            col_ref[h, r] = kind
            z, _ = norm(tok_ref[h, r].astype(F32))
            low = z * jnp.where(kind < 0.5, gain_ref[0:1], gain_ref[1:2])
            low_ref[h, r] = (low + jnp.where(kind < 0.5, shift_ref[0:1], shift_ref[1:2])).astype(BF)
        low = low_ref[:, r].reshape(heads * length, model)
        for n in range(w_ref.shape[1] // model):
            cols = slice(n * model, (n + 1) * model)
            part = mm(low, w_ref[:, cols]).astype(BF)
            qkv_ref[:, r, :, cols] = part.reshape(heads, length, model)
    for copy in sends.values():
        copy.wait_send()


def enter(tokens, modality, gain, shift, weight):
    heads, rows, _, model = tokens.shape
    assert heads == 4
    vmem = pl.BlockSpec(memory_space=pltpu.VMEM)
    sems = 3 * rows + 3
    return pl.pallas_call(
        enter_kernel,
        in_specs=[pl.BlockSpec(memory_space=pl.ANY)] + [vmem] * 4,
        out_specs=[vmem] * 5,
        out_shape=[
            jax.ShapeDtypeStruct(tokens.shape, BF),
            jax.ShapeDtypeStruct((heads,) + modality.shape[1:], jnp.int32),
            jax.ShapeDtypeStruct(tokens.shape[:3] + (1,), F32),
            jax.ShapeDtypeStruct(tokens.shape, BF),
            jax.ShapeDtypeStruct(tokens.shape[:3] + weight.shape[1:], BF),
        ],
        scratch_shapes=[
            pltpu.VMEM(tokens.shape, F32),
            pltpu.VMEM(tokens.shape, BF),
            pltpu.SemaphoreType.DMA((sems,)),
            pltpu.SemaphoreType.DMA((sems,)),
            pltpu.SemaphoreType.DMA((4 * rows,)),
        ],
        compiler_params=pltpu.CompilerParams(
            collective_id=2, has_side_effects=True, vmem_limit_bytes=VMEM_BYTES
        ),
        cost_estimate=pl.CostEstimate(
            flops=2 * tokens.size * weight.shape[1], bytes_accessed=40 * 1024 * 1024,
            transcendentals=0,
        ),
        name="enter",
    )(tokens, modality, gain, shift, weight)


def norm(values):
    mean = jnp.mean(values, axis=-1, keepdims=True)
    centered = values - mean
    rstd = lax.rsqrt(jnp.mean(centered * centered, axis=-1, keepdims=True) + EPS)
    return centered * rstd, rstd


def pick(table, kind):
    return jnp.where(kind == 0, table[0], table[1])


def norm_back(grad, gains, z, rstd):
    q = grad * gains
    return rstd * (
        q
        - jnp.mean(q, axis=-1, keepdims=True)
        - z * jnp.mean(q * z, axis=-1, keepdims=True)
    )


def by_expert(values, kind):
    first = jnp.sum(jnp.where(kind == 0, values, 0.0), axis=0)
    second = jnp.sum(jnp.where(kind == 0, 0.0, values), axis=0)
    return jnp.stack([first, second])


def flip(axis, size, bit):
    return functools.partial(
        lax.ppermute, axis_name=axis, perm=[(i, i ^ (1 << bit)) for i in range(size)]
    )


def take(values, dim, index):
    return lax.dynamic_index_in_dim(values, index, dim, keepdims=False)


def body(sizes, tokens, segment, modality, first_gain, first_shift, project_in, project_out,
         second_gain, second_shift, up_weight, down_weight, cotangent):
    heads, groups = sizes["head"], sizes["dp"]
    row_count, length, model = tokens.shape
    rows = row_count // heads
    count = row_count * length
    hidden = up_weight.shape[-1]
    me_h, me_d = lax.axis_index("head"), lax.axis_index("dp")
    core = me_h % 2
    head_bits = heads.bit_length() - 1
    dp_bits = groups.bit_length() - 1
    assert heads == 1 << head_bits and groups == 1 << dp_bits and head_bits >= 2
    hflip = [flip("head", heads, b) for b in range(head_bits)]
    dflip = [flip("dp", groups, b) for b in range(dp_bits)]

    grid = (heads, rows, length)
    tok, kinds, col, low1, qkv = enter(
        tokens.reshape(*grid, model), modality.reshape(heads // 2, 2, rows, length),
        first_gain, first_shift, project_in,
    )
    seg = lax.dynamic_slice_in_dim(segment, me_h * rows, rows, 0)
    kind = take(kinds, 1, core).reshape(count)
    kcol = col.reshape(count, 1)

    flat = tok.astype(F32).reshape(count, model)
    context, lse, cot = attention_forward(seg, qkv, cotangent.reshape(*grid, model))
    cot = cot.reshape(count, model)
    ctx = context.reshape(count, model)
    attention = mm(ctx, project_out)
    residual = flat + attention
    z2, rstd2 = norm(residual)
    gain2 = pick(second_gain, kcol)
    low2 = (z2 * gain2 + pick(second_shift, kcol)).astype(BF)

    slots = count + BLK
    is0 = (kind == 0).astype(F32).reshape(count // BLK, BLK)
    tri = jnp.triu(jnp.ones((BLK, BLK), F32))
    inner = mm(is0, tri)
    ends = jnp.cumsum(inner[:, -1])
    before = (inner + (ends - inner[:, -1])[:, None]).reshape(count).astype(jnp.int32)
    n0 = ends[-1].astype(jnp.int32)
    blocks0 = (n0 + BLK - 1) // BLK
    blocks1 = (count - n0 + BLK - 1) // BLK
    rank1 = jnp.arange(count, dtype=jnp.int32) - before
    slot = jnp.where(kind == 0, before - 1, blocks0 * BLK + rank1)
    place = (slot[None, :] == jnp.arange(slots, dtype=jnp.int32)[:, None]).astype(BF)

    near = hflip[0]
    g_mine = mm(place, cot).astype(BF)
    g_other = near(g_mine)
    zeros = jnp.sum(kinds == 0, axis=(0, 2, 3))
    full = jnp.stack([(zeros + BLK - 1) // BLK, (count - zeros + BLK - 1) // BLK], axis=1)
    blocks, blocks_other = take(full, 0, core), take(full, 0, 1 - core)
    xbit = (me_h // 2) % 2
    ybit = me_d % 2
    info = jnp.concatenate([blocks, blocks_other, jnp.stack([xbit, ybit, core])]).astype(jnp.int32)
    x_mine = mm(place, low2).astype(BF)
    x_other = near(x_mine)

    partial, kept, came = None, ([], []), ([], [])
    for call in range(CALLS):
        *partial, up_keep, up_send, down_keep, down_send = ffn(
            call, info, x_mine, x_other, g_mine, g_other, up_weight, down_weight, partial, groups
        )
        kept[0].append(up_keep)
        kept[1].append(down_keep)
        came[0].append(hflip[1](up_send))
        came[1].append(dflip[0](down_send))

    partial, early = lax.optimization_barrier((partial, [c[:-1] for c in came]))
    came = [e + c[-1:] for e, c in zip(early, came)]
    branch_mine, branch_other, dx_mine, dx_other = partial
    dx = dx_mine + near(dx_other)
    second_grad = mm_tn(place, dx)
    branch = mm_tn(place, branch_mine + near(branch_other))
    leaving = (attention + branch).astype(BF).reshape(*grid, model)

    cot32 = cot.astype(F32)
    gain2_term = by_expert(second_grad * z2, kcol)
    shift2_term = by_expert(second_grad, kcol)
    extra = norm_back(second_grad, gain2, z2, rstd2)
    attention_low = (cot32 + extra).astype(BF)
    out_term = mm_tn(ctx, attention_low)
    context_grad = mm_nt(attention_low, project_out).astype(BF)
    in_term, table1, tail, up_sum, down_sum, back, home0 = attention_backward(
        seg, qkv, context_grad.reshape(context.shape), lse, low1, project_in,
        tok, extra.reshape(*grid, model), col, first_gain,
        kept[0], came[0], kept[1], came[1], leaving, dp_bits,
    )
    output = tokens + back.reshape(row_count, length, model).astype(F32)
    att_sum, up_sum, down_sum, table, home = finish(
        dp_bits, up_sum, down_sum, in_term,
        out_term.astype(BF).reshape(groups, model // groups, model),
        (table1, gain2_term, shift2_term), tail,
    )
    home = jnp.concatenate([home0, home], axis=1)
    input_grad = cotangent + home.reshape(row_count, length, model).astype(F32)

    up_grad, down_grad = up_sum.astype(F32), down_sum.astype(F32)
    in_grad = att_sum[:, : 3 * model].astype(F32)
    out_grad = att_sum[:, 3 * model :].astype(F32)
    tables = lax.dynamic_slice_in_dim(table, me_d * (model // groups), model // groups, 1)
    tables = tables.reshape(4, EXPERTS, model // groups)
    return (
        output, input_grad, tables[0], tables[1], in_grad, out_grad, tables[2], tables[3],
        up_grad, down_grad,
    )


def solution(mesh):
    return jax.shard_map(
        functools.partial(body, dict(mesh.shape)),
        mesh=mesh,
        in_specs=(
            P("dp", "head", None),
            P("dp", None),
            P("dp", "head"),
            P(),
            P(),
            P(),
            P(),
            P(),
            P(),
            P(),
            P(),
            P("dp", "head", None),
        ),
        out_specs=(
            P("dp", "head", None),
            P("dp", "head", None),
            P(None, "dp"),
            P(None, "dp"),
            P("dp", None),
            P("dp", None),
            P(None, "dp"),
            P(None, "dp"),
            P(None, "dp", None),
            P(None, "dp", None),
        ),
        check_vma=False,
    )
```

```python
import functools

import jax
import jax.numpy as jnp
from jax import lax
from jax.experimental import pallas as pl
from jax.experimental.pallas import tpu as pltpu
from jax.sharding import PartitionSpec as P

HEAD_DIM = 64
EXPERTS = 2
EPS = 1e-05
NEG = -1000000000.0
BLK = 128
CALLS = 2
VMEM_BYTES = 60 * 1024 * 1024
BF = jnp.bfloat16
F32 = jnp.float32
NT = (((1,), (1,)), ((), ()))
TN = (((0,), (0,)), ((), ()))


def mm(a, b):
    return jnp.dot(a, b, preferred_element_type=F32)


def mm_nt(a, b):
    return lax.dot_general(a, b, NT, preferred_element_type=F32)


def mm_tn(a, b):
    return lax.dot_general(a, b, TN, preferred_element_type=F32)


def bias_of(segc_ref, segr_ref, bias_ref):
    same = segc_ref[0] == segr_ref[0]
    bias_ref[...] = jnp.where(same, 0.0, NEG)


def attn_specs(sub, length, pairs):
    def part(i):
        return pl.BlockSpec((sub, 1, length, 128), lambda r, j, i=i: (0, r, 0, i * pairs + j))

    return part


def ffn_kernel(first, bits, info_ref, xm_ref, xo_ref, gm_ref, go_ref, u_ref, d_ref, *refs):
    refs = list(refs)
    prev = [] if first else draw(refs, 4)
    outs, grads = draw(refs, 4), draw(refs, 4)
    du_ref, dd_ref, act_ref, dh_ref, x_ref, g_ref = draw(refs, 6)
    held, up_ref, keep_ref, send_ref, sem = draw(refs, 2), *refs
    e = pl.program_id(0)
    slots, model = xm_ref.shape
    cols = u_ref.shape[-1]
    tile = 256
    down = d_ref[0]
    made = [0]

    def local(src, dst):
        made[0] += 1
        return pltpu.make_async_copy(src, dst, sem.at[made[0] - 1])

    loads = [
        [local(x, x_ref.at[i]), local(g, g_ref.at[i])]
        + [local(p, h.at[i]) for p, h in zip(prev[i::2], held)]
        for i, (x, g) in enumerate(((xm_ref, gm_ref), (xo_ref, go_ref)))
    ]
    stores = [[local(h.at[i], out) for h, out in zip(held, outs[i::2])] for i in range(2)]

    @pl.when(e == 0)
    def _():
        for copy in loads[0] + loads[1]:
            copy.start()
        if first:
            for h in held:
                for which in range(2):
                    h[which, slots - BLK :, :] = jnp.zeros((BLK, model), BF)

    du_ref[...] = jnp.zeros_like(du_ref)
    dd_ref[...] = jnp.zeros_like(dd_ref)

    def chunk(which, block, count):
        size = count * BLK
        rows = pl.ds(pl.multiple_of(block * BLK, BLK), size)
        x = x_ref[which, rows, :]
        g = g_ref[which, rows, :]
        for n in range(cols // tile):
            part = slice(n * tile, (n + 1) * tile)
            h = mm(x, u_ref[0, :, part])
            da = mm_nt(g, down[part, :])
            cdf = 0.5 + 0.5 * lax.erf(h * 0.7071067811865476)
            pdf = 0.3989422804014327 * jnp.exp(-0.5 * h * h)
            act_ref[:size, part] = (h * cdf).astype(BF)
            dh_ref[:size, part] = (da * (cdf + h * pdf)).astype(BF)
        act = act_ref[:size, :]
        dh = dh_ref[:size, :]
        for slot, value in enumerate((mm(act, down), mm_nt(dh, u_ref[0]))):
            if not first:
                value = value + held[slot][which, rows, :].astype(F32)
            held[slot][which, rows, :] = value.astype(BF)
        du_ref[...] += mm_tn(x, dh)
        dd_ref[...] += mm_tn(act, g)

    def side(which, carry):
        for i in range(2):

            @pl.when((e == 0) & (which == i))
            def _(i=i):
                for copy in loads[i]:
                    copy.wait()

        n0 = info_ref[2 * which]
        n1 = info_ref[2 * which + 1]
        start = jnp.where(e == 0, 0, n0)
        count = jnp.where(e == 0, n0, n1)
        fours = count // 4 - jnp.where((count % 4 == 1) & (count > 4), 1, 0)

        def four(i, carry):
            chunk(which, start + 4 * i, 4)
            return carry

        lax.fori_loop(0, fours, four, 0)
        for left in (1, 2, 3, 5):

            @pl.when(count - 4 * fours == left)
            def _(left=left):
                chunk(which, start + 4 * fours, left)

        for i in range(2):

            @pl.when((e == EXPERTS - 1) & (which == i))
            def _(i=i):
                for copy in stores[i]:
                    copy.start()

        return carry

    lax.fori_loop(0, 2, side, 0)

    up_keep, up_send, down_keep, down_send = grads
    groups = 1 << bits
    per = model // groups
    wide = keep_ref.shape[2]
    xbit, ybit = info_ref[4], info_ref[5]
    for p in range(groups):
        up_ref[e, spot(p, range(bits))] = du_ref[p * per : (p + 1) * per, :].astype(BF)
    for y in range(2):
        for ref, here in ((keep_ref, ybit == y), (send_ref, ybit != y)):

            @pl.when(here)
            def _(ref=ref, y=y):
                for p in range(y, cols // wide, 2):
                    at = spot(p >> 1, range(bits - 3))
                    ref[at, e] = dd_ref[p * wide : (p + 1) * wide, :].astype(BF)

    sends = []
    for i in range(EXPERTS):
        ups = local(up_ref.at[i], up_keep), local(up_ref.at[i], up_send)
        downs = [
            local(src.at[:, i], dst.at[:, i])
            for src, dst in ((keep_ref, down_keep), (send_ref, down_send))
        ]
        sends.append((ups, downs))

        @pl.when(e == i)
        def _(ups=ups, downs=downs, i=i):
            for copy in downs:
                copy.start()
            for copy, here in zip(ups, (xbit == i, xbit != i)):

                @pl.when(here)
                def _(copy=copy):
                    copy.start()

    @pl.when(e == EXPERTS - 1)
    def _():
        for copy in stores[0] + stores[1]:
            copy.wait()
        for i, (ups, downs) in enumerate(sends):
            for copy in downs:
                copy.wait()
            for copy, here in zip(ups, (xbit == i, xbit != i)):

                @pl.when(here)
                def _(copy=copy):
                    copy.wait()


def spot(index, order):
    return functools.reduce(lambda acc, bit: 2 * acc + (index >> bit & 1), order, 0)


def ffn(call, info, x_mine, x_other, g_mine, g_other, up, down, partial, groups):
    slots, model = x_mine.shape
    hidden = up.shape[-1]
    cols = hidden // (2 * CALLS)
    bits = groups.bit_length() - 1
    hbm = pl.BlockSpec(memory_space=pl.ANY)
    first = partial is None
    extra = () if first else tuple(partial)
    grads = [(groups, model // groups, model)] * 2
    grads += [(groups // 8, EXPERTS, hidden // groups, model)] * 2
    return pl.pallas_call(
        functools.partial(ffn_kernel, first, bits),
        grid_spec=pltpu.PrefetchScalarGridSpec(
            num_scalar_prefetch=1,
            grid=(EXPERTS,),
            in_specs=[hbm] * 4
            + [
                pl.BlockSpec((1, model, cols), lambda e, i: (e, 0, i[6] * CALLS + call)),
                pl.BlockSpec((1, cols, model), lambda e, i: (e, i[6] * CALLS + call, 0)),
            ]
            + [hbm] * len(extra),
            out_specs=[hbm] * 8,
            scratch_shapes=[
                pltpu.VMEM((model, cols), F32),
                pltpu.VMEM((cols, model), F32),
                pltpu.VMEM((5 * BLK, cols), BF),
                pltpu.VMEM((5 * BLK, cols), BF),
                pltpu.VMEM((2, slots, model), BF),
                pltpu.VMEM((2, slots, model), BF),
                pltpu.VMEM((2, slots, model), BF),
                pltpu.VMEM((2, slots, model), BF),
                pltpu.VMEM((EXPERTS,) + grads[0], BF),
                pltpu.VMEM(grads[2], BF),
                pltpu.VMEM(grads[2], BF),
                pltpu.SemaphoreType.DMA((24,)),
            ],
        ),
        out_shape=[jax.ShapeDtypeStruct((slots, model), BF)] * 4
        + [jax.ShapeDtypeStruct(g, BF) for g in grads],
        compiler_params=pltpu.CompilerParams(vmem_limit_bytes=VMEM_BYTES),
        cost_estimate=pl.CostEstimate(
            flops=12 * 2 * slots * model * cols, bytes_accessed=40 * 1024 * 1024,
            transcendentals=2 * 2 * slots * cols,
        ),
        name="ffn",
    )(info, x_mine, x_other, g_mine, g_other, up, down, *extra)


def peers():
    out = {}
    for axis in ("head", "dp"):
        me = lax.axis_index(axis)
        for b in range(lax.axis_size(axis).bit_length() - 1):
            bit = (me // (1 << b)) % 2
            out[axis, b] = bit, {axis: me + (1 - 2 * bit) * (1 << b)}
    return out


class Halving:
    def __init__(self, env, order, buf, gots, first, remote):
        self.rounds, path, prev = [], (), first
        for o, got in zip(order, gots):
            bit, partner = env[o]
            view = buf.at[path] if path else buf
            away, stay = view.at[1 - bit], view.at[bit]
            halves = (None, None) if prev is None else (prev.at[1 - bit], prev.at[bit])
            self.rounds.append((away, stay, *halves, remote(away, got, partner)))
            path, prev = path + (bit,), got
        self.result, self.last, self.at = buf.at[path], prev, 0
        self.done = False

    def send(self):
        away, stay, got_away, got_stay, copy = self.rounds[self.at]
        accumulate(away, got_away)
        copy.start()
        accumulate(stay, got_stay)

    def step(self):
        self.rounds[self.at][-1].wait_recv()
        self.at += 1
        if self.at < len(self.rounds):
            self.send()
        else:
            accumulate(self.result, self.last)
            self.done = True

    def close(self):
        for *_, copy in self.rounds:
            copy.wait_send()


def spots(ref):
    lead = len(ref.shape) - 2
    return [tuple(i >> b & 1 for b in range(lead)) for i in range(1 << lead)]


def accumulate(into, got):
    if got is not None:
        for at in spots(into):
            at = at or ...
            into[at] = into[at] + got[at]


def neighbours(env):
    me = lax.axis_index("head")
    out = [partner for _, partner in env.values()]
    for o in range(1, lax.axis_size("head")):
        if o & (o - 1):
            out.append({"head": (me // 4) * 4 + flipped(me % 4, o)})
    return out


def greet(env):
    barrier = pltpu.get_barrier_semaphore()
    partners = neighbours(env)
    for partner in partners:
        pl.semaphore_signal(barrier, inc=1, device_id=partner, device_id_type=pl.DeviceIdType.MESH)
    pl.semaphore_wait(barrier, len(partners))


class Copies:
    def __init__(self, send_sem, recv_sem, load_sem):
        self.send_sem, self.recv_sem, self.load_sem = send_sem, recv_sem, load_sem
        self.used, self.loads = 0, 0

    def remote(self, src, dst, to):
        s = self.used
        self.used += 1
        return pltpu.make_async_remote_copy(
            src_ref=src, dst_ref=dst, send_sem=self.send_sem.at[s], recv_sem=self.recv_sem.at[s],
            device_id=to, device_id_type=pl.DeviceIdType.MESH,
        )

    def local(self, src, dst):
        self.loads += 1
        return pltpu.make_async_copy(src, dst, self.load_sem.at[self.loads - 1])


def draw(refs, k):
    out = refs[:k]
    del refs[:k]
    return out


def others():
    me = lax.axis_index("head")
    return [(me // 4) * 4 + flipped(me % 4, o) for o in (3, 2, 1)]


def attn_fwd_kernel(
    segc_ref, segr_ref, q_ref, k_ref, v_ref, cot_ref, o_ref, lse_ref, got_ref,
    bias_ref, wide_ref, send_ref, *sems,
):
    sub, _, length, width = q_ref.shape
    seq = sub * length
    copies = Copies(*sems)
    me = lax.axis_index("head")
    targets = others()
    order = [*targets, me]
    loads = [copies.local(cot_ref.at[to], wide_ref.at[to]) for to in order]
    sends = [copies.remote(send_ref.at[to], got_ref.at[me], {"head": to}) for to in targets]
    stays = copies.local(send_ref.at[me], got_ref.at[me])
    barrier = pltpu.get_barrier_semaphore()
    at = pl.program_id(0) * pl.num_programs(1) + pl.program_id(1)

    @pl.when(at == 0)
    def _():
        for copy in loads:
            copy.start()
        for to in targets:
            pl.semaphore_signal(
                barrier, inc=1, device_id={"head": to}, device_id_type=pl.DeviceIdType.MESH
            )

    @pl.when(at == 1)
    def _():
        pl.semaphore_wait(barrier, len(targets))
        for to, load, copy in zip(order, loads, [*sends, stays]):
            load.wait()
            send_ref[to] = wide_ref[to].astype(BF)
            copy.start()

    @pl.when(at == pl.num_programs(0) * pl.num_programs(1) - 1)
    def _():
        for copy in [*sends, stays]:
            copy.wait()

    @pl.when(pl.program_id(1) == 0)
    def _():
        bias_of(segc_ref, segr_ref, bias_ref)

    q = q_ref[...].reshape(seq, width) * jnp.asarray(HEAD_DIM**-0.5, BF)
    k = k_ref[...].reshape(seq, width)
    vt = v_ref[...].reshape(seq, width).T
    lane = lax.broadcasted_iota(jnp.int32, (1, width), 1) // HEAD_DIM
    zero = jnp.zeros((), BF)
    per = width // HEAD_DIM
    step = seq
    ks = [jnp.where(lane == h, k, zero) for h in range(per)]
    for b in range(seq // step):
        cols = slice(b * step, (b + 1) * step)
        parts = []
        for h in range(per):
            s = mm_nt(ks[h], q[cols]) + bias_ref[:, cols]
            top = jnp.max(s, axis=0, keepdims=True)
            e = jnp.exp(s - top)
            total = jnp.sum(e, axis=0, keepdims=True)
            parts.append(mm(vt[h * HEAD_DIM : (h + 1) * HEAD_DIM], e.astype(BF)) * (1.0 / total))
            lse_ref[0, 0, h : h + 1, cols] = top + jnp.log(total)
        out = jnp.concatenate(parts, axis=0).T.astype(BF)
        o_ref[:, 0] = out.reshape(sub, length, width)


def attention_forward(segment, qkv, cotangent):
    sub, rows, length, wide = qkv.shape
    seq = sub * length
    model = wide // 3
    pairs = model // 128
    part = attn_specs(sub, length, pairs)
    hbm = pl.BlockSpec(memory_space=pl.ANY)
    return pl.pallas_call(
        attn_fwd_kernel,
        grid=(rows, pairs),
        in_specs=[
            pl.BlockSpec((1, seq, 1), lambda r, j: (r, 0, 0)),
            pl.BlockSpec((1, 1, seq), lambda r, j: (r, 0, 0)),
            part(0),
            part(1),
            part(2),
            hbm,
        ],
        out_specs=[part(0), pl.BlockSpec((1, 1, 2, seq), lambda r, j: (r, j, 0, 0)), hbm],
        out_shape=[
            jax.ShapeDtypeStruct((sub, rows, length, model), BF),
            jax.ShapeDtypeStruct((rows, pairs, 2, seq), F32),
            jax.ShapeDtypeStruct(cotangent.shape, BF),
        ],
        scratch_shapes=[
            pltpu.VMEM((seq, seq), F32),
            pltpu.VMEM(cotangent.shape, F32),
            pltpu.VMEM(cotangent.shape, BF),
            pltpu.SemaphoreType.DMA((3,)),
            pltpu.SemaphoreType.DMA((3,)),
            pltpu.SemaphoreType.DMA((5,)),
        ],
        compiler_params=pltpu.CompilerParams(
            collective_id=3, has_side_effects=True, vmem_limit_bytes=VMEM_BYTES
        ),
        cost_estimate=pl.CostEstimate(
            flops=8 * rows * seq * seq * model, bytes_accessed=8 * rows * seq * model,
            transcendentals=rows * seq * seq * model // HEAD_DIM,
        ),
        name="attn_fwd",
    )(segment[:, :, None], segment[:, None, :], qkv, qkv, qkv, cotangent)


def up_order(dp_bits):
    return [("dp", b) for b in range(dp_bits)]


def down_order(dp_bits):
    return [("dp", b) for b in range(1, dp_bits - 1)] + [("head", 1)]


def attention_orders(dp_bits):
    rest = [("dp", b) for b in range(1, dp_bits)]
    core, x, y = ("head", 0), ("head", 1), ("dp", 0)
    return [core, y, x] + rest, [core, x, y] + rest


def stream_scratch(order, tail, first):
    sizes = [len(order)] * (2 if first else 1) + [len(order) - r for r in range(1, len(order) + 1)]
    return [pltpu.VMEM((2,) * k + tail, BF) for k in sizes]


def attn_bwd_kernel(calls, dp_bits, *refs):
    refs = list(refs)
    segc_ref, segr_ref, q_ref, k_ref, v_ref, do_ref, lse_ref, low_ref, w_ref = draw(refs, 9)
    tok_ref, extra_ref, col_ref, gain_ref = draw(refs, 4)
    up_kept, up_came, down_kept, down_came = (draw(refs, calls) for _ in range(4))
    leaving_ref, in_ref, table_ref, tail_ref, up_ref, down_ref, back_ref, home_ref = draw(refs, 8)
    bias_ref, dqkv_ref, lowt_ref, acc_ref, first_ref, rows_ref = draw(refs, 6)
    env = peers()
    copies = Copies(*refs[-3:])
    r, j = pl.program_id(0), pl.program_id(1)
    rows, pairs = pl.num_programs(0), pl.num_programs(1)
    me = lax.axis_index("head")

    streams, loads = [], []
    order = up_order(dp_bits)[:2]
    for i in range(calls):
        buf, first, *gots = draw(refs, 2 + len(order))
        loads.append([copies.local(up_kept[i], buf), copies.local(up_came[i], first)])
        streams.append(Halving(env, order, buf, gots, first, copies.remote))
    order = down_order(dp_bits)
    buf, first, *gots = draw(refs, 2 + len(order))
    lead = dp_bits - 3
    loads.append([])
    for i in range(calls):
        for p in range(1 << lead):
            at = tuple(p >> (lead - 1 - b) & 1 for b in range(lead)) + (i,)
            loads[-1].append(copies.local(down_kept[i].at[p], buf.at[at]))
            loads[-1].append(copies.local(down_came[i].at[p], first.at[at]))
    streams.append(Halving(env, order, buf, gots, first, copies.remote))
    moves = []
    for o in range(1, 4):
        to = (me // 4) * 4 + flipped(me % 4, o)
        moves.append(copies.remote(leaving_ref.at[to], back_ref.at[me], {"head": to}))
    stays = [copies.local(leaving_ref.at[me], back_ref.at[me])]
    early = rows_ref.shape[1]
    homes = []
    for i in range(early):
        homes.append([copies.local(rows_ref.at[me, i], home_ref.at[me, i])])
        for to in others():
            homes[i].append(copies.remote(rows_ref.at[to, i], home_ref.at[me, i], {"head": to}))

    @pl.when((r == 0) & (j == 0))
    def _():
        for group in loads:
            for copy in group:
                copy.start()
        stays[0].start()
        greet(env)
        for stream, group in zip(reversed(streams), reversed(loads)):
            for copy in group:
                copy.wait()
            stream.send()
        for copy in moves:
            copy.start()

    @pl.when((r == rows - 1) & (j == 0))
    def _():
        streams[0].step()

    sub, _, length, width = q_ref.shape
    seq = sub * length
    model = dqkv_ref.shape[-1] // 3

    @pl.when(j == 0)
    def _():
        bias_of(segc_ref, segr_ref, bias_ref)

    scale = HEAD_DIM**-0.5
    q = q_ref[...].reshape(seq, width) * jnp.asarray(scale, BF)
    k = k_ref[...].reshape(seq, width)
    kt = k.T
    v = v_ref[...].reshape(seq, width)
    do = do_ref[...].reshape(seq, width)
    lane = lax.broadcasted_iota(jnp.int32, (1, width), 1) // HEAD_DIM
    zero = jnp.zeros((), BF)
    per = width // HEAD_DIM
    step = seq
    dk = jnp.zeros((seq, width), F32)
    dv = jnp.zeros((seq, width), F32)
    dqs = [[] for _ in range(seq // step)]
    for h in range(per):
        kh = jnp.where(lane == h, k, zero)
        vh = jnp.where(lane == h, v, zero)
        qh = jnp.where(lane == h, q, zero)
        doh = jnp.where(lane == h, do, zero)
        for b in range(seq // step):
            cols = slice(b * step, (b + 1) * step)
            s = mm_nt(kh, q[cols]) + bias_ref[:, cols]
            p = jnp.exp(s - lse_ref[0, 0, h : h + 1, cols])
            dp = mm_nt(vh, do[cols])
            ds = (p * (dp - jnp.sum(p * dp, axis=0, keepdims=True))).astype(BF)
            dv = dv + mm(p.astype(BF), doh[cols])
            dk = dk + mm(ds, qh[cols])
            dqs[b].append(mm(kt[h * HEAD_DIM : (h + 1) * HEAD_DIM], ds) * scale)
    dq = jnp.concatenate([jnp.concatenate(d, axis=0).T for d in dqs], axis=0)
    for i, g in enumerate((dq, dk, dv)):
        at = pl.multiple_of(i * model + j * width, width)
        dqkv_ref[:, pl.ds(at, width)] = g.astype(BF)

    @pl.when((r == rows - 1) & (j == pairs - 1))
    def _():
        for stream in streams[1:]:
            stream.step()

    @pl.when(j == pairs - 1)
    def _():
        tile = 256
        lowt_ref[...] = low_ref[...].reshape(seq, model).T
        first_ref[...] = jnp.zeros_like(first_ref)

        @pl.when(r == 0)
        def _():
            acc_ref[...] = jnp.zeros_like(acc_ref)
            table_ref[...] = jnp.zeros_like(table_ref)

        def piece(n, carry):
            cols = pl.ds(pl.multiple_of(n * tile, tile), tile)
            part = dqkv_ref[:, cols]
            acc_ref[:, cols] += mm(lowt_ref[...], part)
            first_ref[...] += mm_nt(part, w_ref[:, cols])
            return carry

        lax.fori_loop(0, 3 * model // tile, piece, 0)
        for h in range(sub):
            grad = first_ref[h * length : (h + 1) * length, :]
            vision = col_ref[h, 0] > 0.5
            z, rstd = norm(tok_ref[h, 0].astype(F32))
            gain = jnp.where(vision, gain_ref[1:2], gain_ref[0:1])
            for i, term in enumerate((grad * z, grad)):
                for e, part in enumerate((jnp.where(vision, 0.0, term), jnp.where(vision, term, 0.0))):
                    at = 2 * i + e
                    table_ref[at : at + 1, :] += jnp.sum(part, axis=0, keepdims=True)
            tail = (extra_ref[h, 0] + norm_back(grad, gain, z, rstd)).astype(BF)

            @pl.when(r < early)
            def _(h=h, tail=tail):
                rows_ref[h, jnp.minimum(r, early - 1)] = tail

            @pl.when(r == early)
            def _(h=h, tail=tail):
                tail_ref[h, 0] = tail

        for i in range(early):

            @pl.when(r == i)
            def _(i=i):
                for copy in homes[i]:
                    copy.start()

    @pl.when((r == rows - 1) & (j == pairs - 1))
    def _():
        height = in_ref.shape[1]
        for p in range(in_ref.shape[0]):
            in_ref[p] = acc_ref[p * height : (p + 1) * height, :].astype(BF)
        while not all(stream.done for stream in streams):
            for stream in streams:
                if not stream.done:
                    stream.step()
        for i in range(calls):
            for at in spots(streams[i].result):
                up_ref[(i, *at)] = streams[i].result[at or ...]
        down_ref[...] = streams[-1].result[...]
        for copy in [*stays, *moves, *sum(homes, [])]:
            copy.wait()
        for stream in streams:
            stream.close()


def attention_backward(
    segment, qkv, grad, lse, low, weight, tok, extra, col, gain, up_kept, up_came, down_kept, down_came, leaving, dp_bits
):
    sub, rows, length, wide = qkv.shape
    seq = sub * length
    model = wide // 3
    pairs = model // 128
    groups = 1 << dp_bits
    calls = len(up_kept)
    part = attn_specs(sub, length, pairs)
    per, high = model // groups, down_kept[0].shape[2]
    row = pl.BlockSpec((sub, 1, length, model), lambda r, j: (0, r, 0, 0))
    hbm = pl.BlockSpec(memory_space=pl.ANY)

    def fixed(*shape):
        return pl.BlockSpec(shape, lambda r, j: (0,) * len(shape), pipeline_mode=pl.Buffered(1))

    up_kept, up_came = (
        [k.reshape((2,) * dp_bits + (per, model)) for k in ks] for ks in (up_kept, up_came)
    )
    ups, downs = up_order(dp_bits), down_order(dp_bits)
    scratch = [
        s
        for _ in range(calls)
        for s in [pltpu.VMEM((2,) * dp_bits + (per, model), BF)] * 2
        + [pltpu.VMEM((2,) * (dp_bits - 1 - i) + (per, model), BF) for i in range(2)]
    ]
    scratch += stream_scratch(downs, (high, model), True)
    sems = 2 * calls + len(downs) + 3 * rows
    loads = 2 * calls + 2 * calls * (groups // 8) + rows
    up_tail = (calls,) + (2,) * (dp_bits - 2) + (per, model)
    return pl.pallas_call(
        functools.partial(attn_bwd_kernel, calls, dp_bits),
        grid=(rows, pairs),
        in_specs=[
            pl.BlockSpec((1, seq, 1), lambda r, j: (r, 0, 0)),
            pl.BlockSpec((1, 1, seq), lambda r, j: (r, 0, 0)),
            part(0),
            part(1),
            part(2),
            part(0),
            pl.BlockSpec((1, 1, 2, seq), lambda r, j: (r, j, 0, 0)),
            row,
            fixed(*weight.shape),
            row,
            row,
            pl.BlockSpec((sub, 1, length, 1), lambda r, j: (0, r, 0, 0)),
            fixed(*gain.shape),
        ]
        + [hbm] * (4 * calls + 1),
        out_specs=[
            fixed(groups, per, wide), fixed(4, model), fixed(sub, 1, length, model),
            fixed(*up_tail), fixed(high, model), hbm, hbm,
        ],
        out_shape=[
            jax.ShapeDtypeStruct((groups, per, wide), BF),
            jax.ShapeDtypeStruct((4, model), F32),
            jax.ShapeDtypeStruct((sub, 1, length, model), BF),
            jax.ShapeDtypeStruct(up_tail, BF),
            jax.ShapeDtypeStruct((high, model), BF),
            jax.ShapeDtypeStruct(leaving.shape, BF),
            jax.ShapeDtypeStruct((sub, rows - 1, length, model), BF),
        ],
        scratch_shapes=[
            pltpu.VMEM((seq, seq), F32),
            pltpu.VMEM((seq, wide), BF),
            pltpu.VMEM((model, seq), BF),
            pltpu.VMEM((model, wide), F32),
            pltpu.VMEM((seq, model), F32),
            pltpu.VMEM((sub, rows - 1, length, model), BF),
        ]
        + scratch
        + [
            pltpu.SemaphoreType.DMA((sems,)),
            pltpu.SemaphoreType.DMA((sems,)),
            pltpu.SemaphoreType.DMA((loads,)),
        ],
        compiler_params=pltpu.CompilerParams(
            collective_id=1, has_side_effects=True, vmem_limit_bytes=VMEM_BYTES
        ),
        cost_estimate=pl.CostEstimate(
            flops=20 * rows * seq * seq * model + 4 * rows * seq * model * wide,
            bytes_accessed=100 * 1024 * 1024,
            transcendentals=rows * seq * seq * model // HEAD_DIM,
        ),
        name="attn_bwd",
    )(
        segment[:, :, None], segment[:, None, :], qkv, qkv, qkv, grad, lse, low, weight,
        tok, extra, col, gain,
        *up_kept, *up_came, *down_kept, *down_came, leaving,
    )


def finish_kernel(calls, dp_bits, *refs):
    refs = list(refs)
    up_ref, in_ref, out_ref = draw(refs, 3)
    tables = draw(refs, 3)
    last_ref, rows_ref, att_ref, up_out, down_ref, table_ref, home_ref = draw(refs, 7)
    env = peers()
    copies = Copies(*refs[-3:])
    remote = copies.remote
    core, x = env["head", 0][0], env["head", 1][0]
    me = lax.axis_index("head")
    groups = 1 << dp_bits
    model = home_ref.shape[-1]
    x_partner, core_partner = env["head", 1][1], env["head", 0][1]

    streams, loads = [], []
    for half, order in enumerate(attention_orders(dp_bits)):
        buf, *gots = draw(refs, 1 + len(order))
        loads.append([])
        lanes = buf.shape[-1]
        for i in range(4):
            ref, start = (out_ref, 0) if i == 3 else (in_ref, i * model)
            for p in range(groups):
                spot_of = {("head", 0): i >> 1, ("head", 1): i & 1}
                spot_of.update({("dp", b): p >> b & 1 for b in range(dp_bits)})
                cols = pl.ds(start + half * lanes, lanes)
                loads[-1].append(
                    copies.local(ref.at[p, :, cols], buf.at[tuple(spot_of[o] for o in order)])
                )
        streams.append(Halving(env, order, buf, gots, None, remote))
    order = up_order(dp_bits)[2:]
    for i in range(calls):
        buf, *gots = draw(refs, 1 + len(order))
        loads.append([copies.local(up_ref.at[i], buf)])
        streams.append(Halving(env, order, buf, gots, None, remote))
    (last_got,) = draw(refs, 1)
    sbuf, *sgots = draw(refs, 3 + dp_bits)

    for group in loads:
        for copy in group:
            copy.start()
    moves = []
    for o in range(1, 4):
        to = (me // 4) * 4 + flipped(me % 4, o)
        moves.append(remote(rows_ref.at[to], home_ref.at[me], {"head": to}))

    top, beyond = env["dp", dp_bits - 1]
    here, over = down_ref.at[x], down_ref.at[1 - x]
    last = remote(last_ref, last_got, beyond)
    to_x, to_core = remote(here, here, x_partner), remote(here, here, core_partner)
    forward = remote(over, over, core_partner)
    greet(env)

    @pl.when(top != core)
    def _():
        last.start()

    for stream, group in zip(streams, loads):
        for copy in group:
            copy.wait()
        stream.send()

    for at, ref in zip((0, 4, 6), tables):
        sbuf[at : at + ref.shape[0], :] = ref[...]
    sorder = [("head", 0), ("head", 1)] + [("dp", b) for b in range(dp_bits)]
    scopies = [remote(sbuf, got, env[o][1]) for o, got in zip(sorder, sgots)]
    scopies[0].start()
    home_ref[me] = rows_ref[me]

    gathers, after = [], []

    def spread(place, value):
        mine = place(x)
        mine[...] = value[...]
        for to, where in ((x_partner, after), (core_partner, gathers)):
            copy = remote(mine, mine, to)
            copy.start()
            where.append((copy, place))

    def att_place(half, side):
        at = (2 * core + side) * model + half * (model // 2)
        return att_ref.at[:, pl.ds(pl.multiple_of(at, 128), model // 2)]

    def up_place(call, side):
        at = (core * calls + call) * model
        return up_out.at[side, :, pl.ds(pl.multiple_of(at, 128), model)]

    rounds = max(len(sorder), max(len(stream.rounds) for stream in streams))
    for r in range(rounds):
        for i, stream in enumerate(streams):
            if not stream.done:
                stream.step()
                if stream.done:
                    if i < 2:
                        spread(functools.partial(att_place, i), stream.result)
                    else:
                        spread(functools.partial(up_place, i - 2), stream.result)
        if r < len(sorder):
            scopies[r].wait()
            sbuf[...] = sbuf[...] + sgots[r][...]
            if r + 1 < len(sorder):
                scopies[r + 1].start()
        if r == 1:
            for copy in moves:
                copy.start()

            @pl.when(top == core)
            def _():
                last.wait_recv()
                here[...] = last_ref[...] + last_got[...]
                to_x.start()
                to_core.start()

    table_ref[...] = sbuf[...]
    forwards = []
    for copy, place in after:
        copy.wait_recv()
        other = place(1 - x)
        forwards.append(remote(other, other, core_partner))
        forwards[-1].start()

    @pl.when(top == core)
    def _():
        to_x.wait_recv()
        forward.start()
        to_core.wait_send()
        to_x.wait_send()
        forward.wait_send()

    @pl.when(top != core)
    def _():
        last.wait_send()
        to_core.wait_recv()
        forward.wait_recv()

    for copy, _ in gathers:
        copy.wait()
    for copy in forwards:
        copy.wait()
    for copy, _ in after:
        copy.wait_send()
    for stream in streams:
        stream.close()
    for copy in moves:
        copy.wait()


def flipped(index, offset):
    low, high = index % 2, index // 2
    if offset & 1:
        low = 1 - low
    if offset & 2:
        high = 1 - high
    return 2 * high + low


def finish(dp_bits, up, down, in_term, out_term, tables, rows):
    assert rows.shape[0] == 4
    calls = up.shape[0]
    groups, per, model = out_term.shape
    high = down.shape[0]
    orders = attention_orders(dp_bits)
    ups = up_order(dp_bits)[2:]
    scratch = [s for o in orders for s in stream_scratch(o, (per, model // 2), False)]
    scratch += [s for _ in range(calls) for s in stream_scratch(ups, (per, model), False)]
    scratch.append(pltpu.VMEM((high, model), BF))
    scratch += [pltpu.VMEM((8, model), F32)] * (3 + dp_bits)
    sems = sum(map(len, orders)) + calls * len(ups) + 3 + 4 + 2 + dp_bits + 3 * (calls + 2)
    loads = 2 * 4 * groups + calls
    hbm = pl.BlockSpec(memory_space=pl.ANY)
    vmem = pl.BlockSpec(memory_space=pltpu.VMEM)
    return pl.pallas_call(
        functools.partial(finish_kernel, calls, dp_bits),
        in_specs=[hbm] * 3 + [vmem] * 5,
        out_specs=[vmem] * 5,
        out_shape=[
            jax.ShapeDtypeStruct((per, 4 * model), BF),
            jax.ShapeDtypeStruct((2, per, 2 * calls * model), BF),
            jax.ShapeDtypeStruct((2, high, model), BF),
            jax.ShapeDtypeStruct((8, model), F32),
            jax.ShapeDtypeStruct(rows.shape, BF),
        ],
        scratch_shapes=scratch
        + [
            pltpu.SemaphoreType.DMA((sems,)),
            pltpu.SemaphoreType.DMA((sems,)),
            pltpu.SemaphoreType.DMA((loads,)),
        ],
        compiler_params=pltpu.CompilerParams(
            collective_id=0, has_side_effects=True, vmem_limit_bytes=VMEM_BYTES
        ),
        cost_estimate=pl.CostEstimate(
            flops=0, bytes_accessed=100 * 1024 * 1024, transcendentals=0
        ),
        name="finish",
    )(up, in_term, out_term, *tables, down, rows)


def enter_kernel(tokens_ref, modality_ref, gain_ref, shift_ref, w_ref, *refs):
    refs = list(refs)
    tok_ref, kind_ref, col_ref, low_ref, qkv_ref, wide_ref, send_ref = draw(refs, 7)
    copies = Copies(*refs)
    me = lax.axis_index("head")
    heads, rows, length, model = tok_ref.shape
    core = me % 2
    targets = others()
    loads = {
        (o, r): copies.local(tokens_ref.at[to, r], wide_ref.at[to, r])
        for r in range(rows)
        for o, to in enumerate([*targets, me])
    }
    kinds = [copies.remote(modality_ref.at[to // 2], kind_ref.at[me], {"head": to}) for to in targets]
    sends = {
        (o, r): copies.remote(send_ref.at[to, r], tok_ref.at[me, r], {"head": to})
        for r in range(rows)
        for o, to in enumerate(targets)
    }
    for copy in loads.values():
        copy.start()
    barrier = pltpu.get_barrier_semaphore()
    for to in targets:
        pl.semaphore_signal(
            barrier, inc=1, device_id={"head": to}, device_id_type=pl.DeviceIdType.MESH
        )
    pl.semaphore_wait(barrier, len(targets))
    for copy in kinds:
        copy.start()
    kind_ref[me] = modality_ref[me // 2]
    for r in range(rows):
        for o, to in enumerate(targets):
            loads[o, r].wait()
            send_ref[to, r] = wide_ref[to, r].astype(BF)
            sends[o, r].start()
        loads[len(targets), r].wait()
        tok_ref[me, r] = wide_ref[me, r].astype(BF)
    for copy in kinds:
        copy.wait()
    ones = jnp.ones((8, length), BF)
    row = lax.broadcasted_iota(jnp.int32, (8, length), 0)
    for r in range(rows):
        for o in range(len(targets)):
            sends[o, r].wait_recv()
        for h in range(heads):
            kind = kind_ref[h, core, r : r + 1, :].astype(F32)
            kind = jnp.where(row == 0, jnp.broadcast_to(kind, (8, length)), 0.0).astype(BF)
            kind = mm_tn(kind, ones)[:, :1]
            col_ref[h, r] = kind
            z, _ = norm(tok_ref[h, r].astype(F32))
            low = z * jnp.where(kind < 0.5, gain_ref[0:1], gain_ref[1:2])
            low_ref[h, r] = (low + jnp.where(kind < 0.5, shift_ref[0:1], shift_ref[1:2])).astype(BF)
        low = low_ref[:, r].reshape(heads * length, model)
        for n in range(w_ref.shape[1] // model):
            cols = slice(n * model, (n + 1) * model)
            part = mm(low, w_ref[:, cols]).astype(BF)
            qkv_ref[:, r, :, cols] = part.reshape(heads, length, model)
    for copy in sends.values():
        copy.wait_send()


def enter(tokens, modality, gain, shift, weight):
    heads, rows, _, model = tokens.shape
    assert heads == 4
    vmem = pl.BlockSpec(memory_space=pltpu.VMEM)
    sems = 3 * rows + 3
    return pl.pallas_call(
        enter_kernel,
        in_specs=[pl.BlockSpec(memory_space=pl.ANY)] + [vmem] * 4,
        out_specs=[vmem] * 5,
        out_shape=[
            jax.ShapeDtypeStruct(tokens.shape, BF),
            jax.ShapeDtypeStruct((heads,) + modality.shape[1:], jnp.int32),
            jax.ShapeDtypeStruct(tokens.shape[:3] + (1,), F32),
            jax.ShapeDtypeStruct(tokens.shape, BF),
            jax.ShapeDtypeStruct(tokens.shape[:3] + weight.shape[1:], BF),
        ],
        scratch_shapes=[
            pltpu.VMEM(tokens.shape, F32),
            pltpu.VMEM(tokens.shape, BF),
            pltpu.SemaphoreType.DMA((sems,)),
            pltpu.SemaphoreType.DMA((sems,)),
            pltpu.SemaphoreType.DMA((4 * rows,)),
        ],
        compiler_params=pltpu.CompilerParams(
            collective_id=2, has_side_effects=True, vmem_limit_bytes=VMEM_BYTES
        ),
        cost_estimate=pl.CostEstimate(
            flops=2 * tokens.size * weight.shape[1], bytes_accessed=40 * 1024 * 1024,
            transcendentals=0,
        ),
        name="enter",
    )(tokens, modality, gain, shift, weight)


def norm(values):
    mean = jnp.mean(values, axis=-1, keepdims=True)
    centered = values - mean
    rstd = lax.rsqrt(jnp.mean(centered * centered, axis=-1, keepdims=True) + EPS)
    return centered * rstd, rstd


def pick(table, kind):
    return jnp.where(kind == 0, table[0], table[1])


def norm_back(grad, gains, z, rstd):
    q = grad * gains
    return rstd * (
        q
        - jnp.mean(q, axis=-1, keepdims=True)
        - z * jnp.mean(q * z, axis=-1, keepdims=True)
    )


def by_expert(values, kind):
    first = jnp.sum(jnp.where(kind == 0, values, 0.0), axis=0)
    second = jnp.sum(jnp.where(kind == 0, 0.0, values), axis=0)
    return jnp.stack([first, second])


def flip(axis, size, bit):
    return functools.partial(
        lax.ppermute, axis_name=axis, perm=[(i, i ^ (1 << bit)) for i in range(size)]
    )


def take(values, dim, index):
    return lax.dynamic_index_in_dim(values, index, dim, keepdims=False)


def body(sizes, tokens, segment, modality, first_gain, first_shift, project_in, project_out,
         second_gain, second_shift, up_weight, down_weight, cotangent):
    heads, groups = sizes["head"], sizes["dp"]
    row_count, length, model = tokens.shape
    rows = row_count // heads
    count = row_count * length
    hidden = up_weight.shape[-1]
    me_h, me_d = lax.axis_index("head"), lax.axis_index("dp")
    core = me_h % 2
    head_bits = heads.bit_length() - 1
    dp_bits = groups.bit_length() - 1
    assert heads == 1 << head_bits and groups == 1 << dp_bits and head_bits >= 2
    hflip = [flip("head", heads, b) for b in range(head_bits)]
    dflip = [flip("dp", groups, b) for b in range(dp_bits)]

    grid = (heads, rows, length)
    tok, kinds, col, low1, qkv = enter(
        tokens.reshape(*grid, model), modality.reshape(heads // 2, 2, rows, length),
        first_gain, first_shift, project_in,
    )
    seg = lax.dynamic_slice_in_dim(segment, me_h * rows, rows, 0)
    kind = take(kinds, 1, core).reshape(count)
    kcol = col.reshape(count, 1)

    flat = tok.astype(F32).reshape(count, model)
    context, lse, cot = attention_forward(seg, qkv, cotangent.reshape(*grid, model))
    cot = cot.reshape(count, model)
    ctx = context.reshape(count, model)
    attention = mm(ctx, project_out)
    residual = flat + attention
    z2, rstd2 = norm(residual)
    gain2 = pick(second_gain, kcol)
    low2 = (z2 * gain2 + pick(second_shift, kcol)).astype(BF)

    slots = count + BLK
    is0 = (kind == 0).astype(F32).reshape(count // BLK, BLK)
    tri = jnp.triu(jnp.ones((BLK, BLK), F32))
    inner = mm(is0, tri)
    ends = jnp.cumsum(inner[:, -1])
    before = (inner + (ends - inner[:, -1])[:, None]).reshape(count).astype(jnp.int32)
    n0 = ends[-1].astype(jnp.int32)
    blocks0 = (n0 + BLK - 1) // BLK
    blocks1 = (count - n0 + BLK - 1) // BLK
    rank1 = jnp.arange(count, dtype=jnp.int32) - before
    slot = jnp.where(kind == 0, before - 1, blocks0 * BLK + rank1)
    place = (slot[None, :] == jnp.arange(slots, dtype=jnp.int32)[:, None]).astype(BF)

    near = hflip[0]
    g_mine = mm(place, cot).astype(BF)
    g_other = near(g_mine)
    zeros = jnp.sum(kinds == 0, axis=(0, 2, 3))
    full = jnp.stack([(zeros + BLK - 1) // BLK, (count - zeros + BLK - 1) // BLK], axis=1)
    blocks, blocks_other = take(full, 0, core), take(full, 0, 1 - core)
    xbit = (me_h // 2) % 2
    ybit = me_d % 2
    info = jnp.concatenate([blocks, blocks_other, jnp.stack([xbit, ybit, core])]).astype(jnp.int32)
    x_mine = mm(place, low2).astype(BF)
    x_other = near(x_mine)

    partial, kept, came = None, ([], []), ([], [])
    for call in range(CALLS):
        *partial, up_keep, up_send, down_keep, down_send = ffn(
            call, info, x_mine, x_other, g_mine, g_other, up_weight, down_weight, partial, groups
        )
        kept[0].append(up_keep)
        kept[1].append(down_keep)
        came[0].append(hflip[1](up_send))
        came[1].append(dflip[0](down_send))

    partial, early = lax.optimization_barrier((partial, [c[:-1] for c in came]))
    came = [e + c[-1:] for e, c in zip(early, came)]
    branch_mine, branch_other, dx_mine, dx_other = partial
    dx = dx_mine + near(dx_other)
    second_grad = mm_tn(place, dx)
    branch = mm_tn(place, branch_mine + near(branch_other))
    leaving = (attention + branch).astype(BF).reshape(*grid, model)

    cot32 = cot.astype(F32)
    gain2_term = by_expert(second_grad * z2, kcol)
    shift2_term = by_expert(second_grad, kcol)
    extra = norm_back(second_grad, gain2, z2, rstd2)
    attention_low = (cot32 + extra).astype(BF)
    out_term = mm_tn(ctx, attention_low)
    context_grad = mm_nt(attention_low, project_out).astype(BF)
    in_term, table1, tail, up_sum, down_sum, back, home0 = attention_backward(
        seg, qkv, context_grad.reshape(context.shape), lse, low1, project_in,
        tok, extra.reshape(*grid, model), col, first_gain,
        kept[0], came[0], kept[1], came[1], leaving, dp_bits,
    )
    output = tokens + back.reshape(row_count, length, model).astype(F32)
    att_sum, up_sum, down_sum, table, home = finish(
        dp_bits, up_sum, down_sum, in_term,
        out_term.astype(BF).reshape(groups, model // groups, model),
        (table1, gain2_term, shift2_term), tail,
    )
    home = jnp.concatenate([home0, home], axis=1)
    input_grad = cotangent + home.reshape(row_count, length, model).astype(F32)

    up_grad, down_grad = up_sum.astype(F32), down_sum.astype(F32)
    in_grad = att_sum[:, : 3 * model].astype(F32)
    out_grad = att_sum[:, 3 * model :].astype(F32)
    tables = lax.dynamic_slice_in_dim(table, me_d * (model // groups), model // groups, 1)
    tables = tables.reshape(4, EXPERTS, model // groups)
    return (
        output, input_grad, tables[0], tables[1], in_grad, out_grad, tables[2], tables[3],
        up_grad, down_grad,
    )


def solution(mesh):
    return jax.shard_map(
        functools.partial(body, dict(mesh.shape)),
        mesh=mesh,
        in_specs=(
            P("dp", "head", None),
            P("dp", None),
            P("dp", "head"),
            P(),
            P(),
            P(),
            P(),
            P(),
            P(),
            P(),
            P(),
            P("dp", "head", None),
        ),
        out_specs=(
            P("dp", "head", None),
            P("dp", "head", None),
            P(None, "dp"),
            P(None, "dp"),
            P("dp", None),
            P("dp", None),
            P(None, "dp"),
            P(None, "dp"),
            P(None, "dp", None),
            P(None, "dp", None),
        ),
        check_vma=False,
    )
```

```python
import functools

import jax
import jax.numpy as jnp
from jax import lax
from jax.experimental import pallas as pl
from jax.experimental.pallas import tpu as pltpu
from jax.sharding import PartitionSpec as P

HEAD_DIM = 64
EXPERTS = 2
EPS = 1e-05
NEG = -1000000000.0
BLK = 128
CALLS = 2
VMEM_BYTES = 60 * 1024 * 1024
BF = jnp.bfloat16
F32 = jnp.float32
NT = (((1,), (1,)), ((), ()))
TN = (((0,), (0,)), ((), ()))


def mm(a, b):
    return jnp.dot(a, b, preferred_element_type=F32)


def mm_nt(a, b):
    return lax.dot_general(a, b, NT, preferred_element_type=F32)


def mm_tn(a, b):
    return lax.dot_general(a, b, TN, preferred_element_type=F32)


def bias_of(segc_ref, segr_ref, bias_ref):
    same = segc_ref[0] == segr_ref[0]
    bias_ref[...] = jnp.where(same, 0.0, NEG)


def attn_specs(sub, length, pairs):
    def part(i):
        return pl.BlockSpec((sub, 1, length, 128), lambda r, j, i=i: (0, r, 0, i * pairs + j))

    return part


def ffn_kernel(first, bits, info_ref, xm_ref, xo_ref, gm_ref, go_ref, u_ref, d_ref, *refs):
    refs = list(refs)
    prev = [] if first else draw(refs, 4)
    outs, grads = draw(refs, 4), draw(refs, 4)
    du_ref, dd_ref, act_ref, dh_ref, x_ref, g_ref = draw(refs, 6)
    held, up_ref, keep_ref, send_ref, sem = draw(refs, 2), *refs
    e = pl.program_id(0)
    slots, model = xm_ref.shape
    cols = u_ref.shape[-1]
    tile = 256
    down = d_ref[0]
    made = [0]

    def local(src, dst):
        made[0] += 1
        return pltpu.make_async_copy(src, dst, sem.at[made[0] - 1])

    loads = [
        [local(x, x_ref.at[i]), local(g, g_ref.at[i])]
        + [local(p, h.at[i]) for p, h in zip(prev[i::2], held)]
        for i, (x, g) in enumerate(((xm_ref, gm_ref), (xo_ref, go_ref)))
    ]
    stores = [[local(h.at[i], out) for h, out in zip(held, outs[i::2])] for i in range(2)]

    @pl.when(e == 0)
    def _():
        for copy in loads[0] + loads[1]:
            copy.start()
        if first:
            for h in held:
                for which in range(2):
                    h[which, slots - BLK :, :] = jnp.zeros((BLK, model), BF)

    du_ref[...] = jnp.zeros_like(du_ref)
    dd_ref[...] = jnp.zeros_like(dd_ref)

    def chunk(which, block, count):
        size = count * BLK
        rows = pl.ds(pl.multiple_of(block * BLK, BLK), size)
        x = x_ref[which, rows, :]
        g = g_ref[which, rows, :]
        for n in range(cols // tile):
            part = slice(n * tile, (n + 1) * tile)
            h = mm(x, u_ref[0, :, part])
            da = mm_nt(g, down[part, :])
            cdf = 0.5 + 0.5 * lax.erf(h * 0.7071067811865476)
            pdf = 0.3989422804014327 * jnp.exp(-0.5 * h * h)
            act_ref[:size, part] = (h * cdf).astype(BF)
            dh_ref[:size, part] = (da * (cdf + h * pdf)).astype(BF)
        act = act_ref[:size, :]
        dh = dh_ref[:size, :]
        for slot, value in enumerate((mm(act, down), mm_nt(dh, u_ref[0]))):
            if not first:
                value = value + held[slot][which, rows, :].astype(F32)
            held[slot][which, rows, :] = value.astype(BF)
        du_ref[...] += mm_tn(x, dh)
        dd_ref[...] += mm_tn(act, g)

    def side(which, carry):
        for i in range(2):

            @pl.when((e == 0) & (which == i))
            def _(i=i):
                for copy in loads[i]:
                    copy.wait()

        n0 = info_ref[2 * which]
        n1 = info_ref[2 * which + 1]
        start = jnp.where(e == 0, 0, n0)
        count = jnp.where(e == 0, n0, n1)
        fours = count // 4 - jnp.where((count % 4 == 1) & (count > 4), 1, 0)

        def four(i, carry):
            chunk(which, start + 4 * i, 4)
            return carry

        lax.fori_loop(0, fours, four, 0)
        for left in (1, 2, 3, 5):

            @pl.when(count - 4 * fours == left)
            def _(left=left):
                chunk(which, start + 4 * fours, left)

        for i in range(2):

            @pl.when((e == EXPERTS - 1) & (which == i))
            def _(i=i):
                for copy in stores[i]:
                    copy.start()

        return carry

    lax.fori_loop(0, 2, side, 0)

    up_keep, up_send, down_keep, down_send = grads
    groups = 1 << bits
    per = model // groups
    wide = keep_ref.shape[2]
    xbit, ybit = info_ref[4], info_ref[5]
    for p in range(groups):
        up_ref[e, spot(p, range(bits))] = du_ref[p * per : (p + 1) * per, :].astype(BF)
    for y in range(2):
        for ref, here in ((keep_ref, ybit == y), (send_ref, ybit != y)):

            @pl.when(here)
            def _(ref=ref, y=y):
                for p in range(y, cols // wide, 2):
                    at = spot(p >> 1, range(bits - 3))
                    ref[at, e] = dd_ref[p * wide : (p + 1) * wide, :].astype(BF)

    sends = []
    for i in range(EXPERTS):
        ups = local(up_ref.at[i], up_keep), local(up_ref.at[i], up_send)
        downs = [
            local(src.at[:, i], dst.at[:, i])
            for src, dst in ((keep_ref, down_keep), (send_ref, down_send))
        ]
        sends.append((ups, downs))

        @pl.when(e == i)
        def _(ups=ups, downs=downs, i=i):
            for copy in downs:
                copy.start()
            for copy, here in zip(ups, (xbit == i, xbit != i)):

                @pl.when(here)
                def _(copy=copy):
                    copy.start()

    @pl.when(e == EXPERTS - 1)
    def _():
        for copy in stores[0] + stores[1]:
            copy.wait()
        for i, (ups, downs) in enumerate(sends):
            for copy in downs:
                copy.wait()
            for copy, here in zip(ups, (xbit == i, xbit != i)):

                @pl.when(here)
                def _(copy=copy):
                    copy.wait()


def spot(index, order):
    return functools.reduce(lambda acc, bit: 2 * acc + (index >> bit & 1), order, 0)


def ffn(call, info, x_mine, x_other, g_mine, g_other, up, down, partial, groups):
    slots, model = x_mine.shape
    hidden = up.shape[-1]
    cols = hidden // (2 * CALLS)
    bits = groups.bit_length() - 1
    hbm = pl.BlockSpec(memory_space=pl.ANY)
    first = partial is None
    extra = () if first else tuple(partial)
    grads = [(groups, model // groups, model)] * 2
    grads += [(groups // 8, EXPERTS, hidden // groups, model)] * 2
    return pl.pallas_call(
        functools.partial(ffn_kernel, first, bits),
        grid_spec=pltpu.PrefetchScalarGridSpec(
            num_scalar_prefetch=1,
            grid=(EXPERTS,),
            in_specs=[hbm] * 4
            + [
                pl.BlockSpec((1, model, cols), lambda e, i: (e, 0, i[6] * CALLS + call)),
                pl.BlockSpec((1, cols, model), lambda e, i: (e, i[6] * CALLS + call, 0)),
            ]
            + [hbm] * len(extra),
            out_specs=[hbm] * 8,
            scratch_shapes=[
                pltpu.VMEM((model, cols), F32),
                pltpu.VMEM((cols, model), F32),
                pltpu.VMEM((5 * BLK, cols), BF),
                pltpu.VMEM((5 * BLK, cols), BF),
                pltpu.VMEM((2, slots, model), BF),
                pltpu.VMEM((2, slots, model), BF),
                pltpu.VMEM((2, slots, model), BF),
                pltpu.VMEM((2, slots, model), BF),
                pltpu.VMEM((EXPERTS,) + grads[0], BF),
                pltpu.VMEM(grads[2], BF),
                pltpu.VMEM(grads[2], BF),
                pltpu.SemaphoreType.DMA((24,)),
            ],
        ),
        out_shape=[jax.ShapeDtypeStruct((slots, model), BF)] * 4
        + [jax.ShapeDtypeStruct(g, BF) for g in grads],
        compiler_params=pltpu.CompilerParams(vmem_limit_bytes=VMEM_BYTES),
        cost_estimate=pl.CostEstimate(
            flops=12 * 2 * slots * model * cols, bytes_accessed=40 * 1024 * 1024,
            transcendentals=2 * 2 * slots * cols,
        ),
        name="ffn",
    )(info, x_mine, x_other, g_mine, g_other, up, down, *extra)


def peers():
    out = {}
    for axis in ("head", "dp"):
        me = lax.axis_index(axis)
        for b in range(lax.axis_size(axis).bit_length() - 1):
            bit = (me // (1 << b)) % 2
            out[axis, b] = bit, {axis: me + (1 - 2 * bit) * (1 << b)}
    return out


class Halving:
    def __init__(self, env, order, buf, gots, first, remote):
        self.rounds, path, prev = [], (), first
        for o, got in zip(order, gots):
            bit, partner = env[o]
            view = buf.at[path] if path else buf
            away, stay = view.at[1 - bit], view.at[bit]
            halves = (None, None) if prev is None else (prev.at[1 - bit], prev.at[bit])
            self.rounds.append((away, stay, *halves, remote(away, got, partner)))
            path, prev = path + (bit,), got
        self.result, self.last, self.at = buf.at[path], prev, 0
        self.done = False

    def send(self):
        away, stay, got_away, got_stay, copy = self.rounds[self.at]
        accumulate(away, got_away)
        copy.start()
        accumulate(stay, got_stay)

    def step(self):
        self.rounds[self.at][-1].wait_recv()
        self.at += 1
        if self.at < len(self.rounds):
            self.send()
        else:
            accumulate(self.result, self.last)
            self.done = True

    def close(self):
        for *_, copy in self.rounds:
            copy.wait_send()


def spots(ref):
    lead = len(ref.shape) - 2
    return [tuple(i >> b & 1 for b in range(lead)) for i in range(1 << lead)]


def accumulate(into, got):
    if got is not None:
        for at in spots(into):
            at = at or ...
            into[at] = into[at] + got[at]


def neighbours(env):
    me = lax.axis_index("head")
    out = [partner for _, partner in env.values()]
    for o in range(1, lax.axis_size("head")):
        if o & (o - 1):
            out.append({"head": (me // 4) * 4 + flipped(me % 4, o)})
    return out


def greet(env):
    barrier = pltpu.get_barrier_semaphore()
    partners = neighbours(env)
    for partner in partners:
        pl.semaphore_signal(barrier, inc=1, device_id=partner, device_id_type=pl.DeviceIdType.MESH)
    pl.semaphore_wait(barrier, len(partners))


class Copies:
    def __init__(self, send_sem, recv_sem, load_sem):
        self.send_sem, self.recv_sem, self.load_sem = send_sem, recv_sem, load_sem
        self.used, self.loads = 0, 0

    def remote(self, src, dst, to):
        s = self.used
        self.used += 1
        return pltpu.make_async_remote_copy(
            src_ref=src, dst_ref=dst, send_sem=self.send_sem.at[s], recv_sem=self.recv_sem.at[s],
            device_id=to, device_id_type=pl.DeviceIdType.MESH,
        )

    def local(self, src, dst):
        self.loads += 1
        return pltpu.make_async_copy(src, dst, self.load_sem.at[self.loads - 1])


def draw(refs, k):
    out = refs[:k]
    del refs[:k]
    return out


def others():
    me = lax.axis_index("head")
    return [(me // 4) * 4 + flipped(me % 4, o) for o in (3, 2, 1)]


def attn_fwd_kernel(
    segc_ref, segr_ref, q_ref, k_ref, v_ref, cot_ref, o_ref, lse_ref, got_ref,
    bias_ref, wide_ref, send_ref, *sems,
):
    sub, _, length, width = q_ref.shape
    seq = sub * length
    copies = Copies(*sems)
    me = lax.axis_index("head")
    targets = others()
    order = [*targets, me]
    loads = [copies.local(cot_ref.at[to], wide_ref.at[to]) for to in order]
    sends = [copies.remote(send_ref.at[to], got_ref.at[me], {"head": to}) for to in targets]
    stays = copies.local(send_ref.at[me], got_ref.at[me])
    barrier = pltpu.get_barrier_semaphore()
    at = pl.program_id(0) * pl.num_programs(1) + pl.program_id(1)

    @pl.when(at == 0)
    def _():
        for copy in loads:
            copy.start()
        for to in targets:
            pl.semaphore_signal(
                barrier, inc=1, device_id={"head": to}, device_id_type=pl.DeviceIdType.MESH
            )

    @pl.when(at == 1)
    def _():
        pl.semaphore_wait(barrier, len(targets))
        for to, load, copy in zip(order, loads, [*sends, stays]):
            load.wait()
            send_ref[to] = wide_ref[to].astype(BF)
            copy.start()

    @pl.when(at == pl.num_programs(0) * pl.num_programs(1) - 1)
    def _():
        for copy in [*sends, stays]:
            copy.wait()

    @pl.when(pl.program_id(1) == 0)
    def _():
        bias_of(segc_ref, segr_ref, bias_ref)

    q = q_ref[...].reshape(seq, width) * jnp.asarray(HEAD_DIM**-0.5, BF)
    k = k_ref[...].reshape(seq, width)
    vt = v_ref[...].reshape(seq, width).T
    lane = lax.broadcasted_iota(jnp.int32, (1, width), 1) // HEAD_DIM
    zero = jnp.zeros((), BF)
    per = width // HEAD_DIM
    step = seq
    ks = [jnp.where(lane == h, k, zero) for h in range(per)]
    for b in range(seq // step):
        cols = slice(b * step, (b + 1) * step)
        parts = []
        for h in range(per):
            s = mm_nt(ks[h], q[cols]) + bias_ref[:, cols]
            top = jnp.max(s, axis=0, keepdims=True)
            e = jnp.exp(s - top)
            total = jnp.sum(e, axis=0, keepdims=True)
            parts.append(mm(vt[h * HEAD_DIM : (h + 1) * HEAD_DIM], e.astype(BF)) * (1.0 / total))
            lse_ref[0, 0, h : h + 1, cols] = top + jnp.log(total)
        out = jnp.concatenate(parts, axis=0).T.astype(BF)
        o_ref[:, 0] = out.reshape(sub, length, width)


def attention_forward(segment, qkv, cotangent):
    sub, rows, length, wide = qkv.shape
    seq = sub * length
    model = wide // 3
    pairs = model // 128
    part = attn_specs(sub, length, pairs)
    hbm = pl.BlockSpec(memory_space=pl.ANY)
    return pl.pallas_call(
        attn_fwd_kernel,
        grid=(rows, pairs),
        in_specs=[
            pl.BlockSpec((1, seq, 1), lambda r, j: (r, 0, 0)),
            pl.BlockSpec((1, 1, seq), lambda r, j: (r, 0, 0)),
            part(0),
            part(1),
            part(2),
            hbm,
        ],
        out_specs=[part(0), pl.BlockSpec((1, 1, 2, seq), lambda r, j: (r, j, 0, 0)), hbm],
        out_shape=[
            jax.ShapeDtypeStruct((sub, rows, length, model), BF),
            jax.ShapeDtypeStruct((rows, pairs, 2, seq), F32),
            jax.ShapeDtypeStruct(cotangent.shape, BF),
        ],
        scratch_shapes=[
            pltpu.VMEM((seq, seq), F32),
            pltpu.VMEM(cotangent.shape, F32),
            pltpu.VMEM(cotangent.shape, BF),
            pltpu.SemaphoreType.DMA((3,)),
            pltpu.SemaphoreType.DMA((3,)),
            pltpu.SemaphoreType.DMA((5,)),
        ],
        compiler_params=pltpu.CompilerParams(
            collective_id=3, has_side_effects=True, vmem_limit_bytes=VMEM_BYTES
        ),
        cost_estimate=pl.CostEstimate(
            flops=8 * rows * seq * seq * model, bytes_accessed=8 * rows * seq * model,
            transcendentals=rows * seq * seq * model // HEAD_DIM,
        ),
        name="attn_fwd",
    )(segment[:, :, None], segment[:, None, :], qkv, qkv, qkv, cotangent)


def up_order(dp_bits):
    return [("dp", b) for b in range(dp_bits)]


def down_order(dp_bits):
    return [("dp", b) for b in range(1, dp_bits - 1)] + [("head", 1)]


def attention_orders(dp_bits):
    rest = [("dp", b) for b in range(2, dp_bits)]
    core, x, y, z = ("head", 0), ("head", 1), ("dp", 0), ("dp", 1)
    return [core, y, z, x] + rest, [core, x, y, z] + rest


def stream_scratch(order, tail, first):
    sizes = [len(order)] * (2 if first else 1) + [len(order) - r for r in range(1, len(order) + 1)]
    return [pltpu.VMEM((2,) * k + tail, BF) for k in sizes]


def attn_bwd_kernel(calls, dp_bits, *refs):
    refs = list(refs)
    segc_ref, segr_ref, q_ref, k_ref, v_ref, do_ref, lse_ref, low_ref, w_ref = draw(refs, 9)
    tok_ref, extra_ref, col_ref, gain_ref = draw(refs, 4)
    up_kept, up_came, down_kept, down_came = (draw(refs, calls) for _ in range(4))
    leaving_ref, in_ref, table_ref, tail_ref, up_ref, down_ref, back_ref, home_ref = draw(refs, 8)
    bias_ref, dqkv_ref, lowt_ref, acc_ref, first_ref, rows_ref = draw(refs, 6)
    env = peers()
    copies = Copies(*refs[-3:])
    r, j = pl.program_id(0), pl.program_id(1)
    rows, pairs = pl.num_programs(0), pl.num_programs(1)
    me = lax.axis_index("head")

    streams, loads = [], []
    order = up_order(dp_bits)[:2]
    for i in range(calls):
        buf, first, *gots = draw(refs, 2 + len(order))
        loads.append([copies.local(up_kept[i], buf), copies.local(up_came[i], first)])
        streams.append(Halving(env, order, buf, gots, first, copies.remote))
    order = down_order(dp_bits)
    buf, first, *gots = draw(refs, 2 + len(order))
    lead = dp_bits - 3
    loads.append([])
    for i in range(calls):
        for p in range(1 << lead):
            at = tuple(p >> (lead - 1 - b) & 1 for b in range(lead)) + (i,)
            loads[-1].append(copies.local(down_kept[i].at[p], buf.at[at]))
            loads[-1].append(copies.local(down_came[i].at[p], first.at[at]))
    streams.append(Halving(env, order, buf, gots, first, copies.remote))
    moves = []
    for o in range(1, 4):
        to = (me // 4) * 4 + flipped(me % 4, o)
        moves.append(copies.remote(leaving_ref.at[to], back_ref.at[me], {"head": to}))
    stays = [copies.local(leaving_ref.at[me], back_ref.at[me])]
    early = rows_ref.shape[1]
    homes = []
    for i in range(early):
        homes.append([copies.local(rows_ref.at[me, i], home_ref.at[me, i])])
        for to in others():
            homes[i].append(copies.remote(rows_ref.at[to, i], home_ref.at[me, i], {"head": to}))

    @pl.when((r == 0) & (j == 0))
    def _():
        for group in loads:
            for copy in group:
                copy.start()
        stays[0].start()
        greet(env)
        for stream, group in zip(reversed(streams), reversed(loads)):
            for copy in group:
                copy.wait()
            stream.send()
        for copy in moves:
            copy.start()

    @pl.when((r == rows - 1) & (j == pairs // 2))
    def _():
        for stream in reversed(streams):
            stream.step()

    sub, _, length, width = q_ref.shape
    seq = sub * length
    model = dqkv_ref.shape[-1] // 3

    @pl.when(j == 0)
    def _():
        bias_of(segc_ref, segr_ref, bias_ref)

    scale = HEAD_DIM**-0.5
    q = q_ref[...].reshape(seq, width) * jnp.asarray(scale, BF)
    k = k_ref[...].reshape(seq, width)
    kt = k.T
    v = v_ref[...].reshape(seq, width)
    do = do_ref[...].reshape(seq, width)
    lane = lax.broadcasted_iota(jnp.int32, (1, width), 1) // HEAD_DIM
    zero = jnp.zeros((), BF)
    per = width // HEAD_DIM
    step = seq
    dk = jnp.zeros((seq, width), F32)
    dv = jnp.zeros((seq, width), F32)
    dqs = [[] for _ in range(seq // step)]
    for h in range(per):
        kh = jnp.where(lane == h, k, zero)
        vh = jnp.where(lane == h, v, zero)
        qh = jnp.where(lane == h, q, zero)
        doh = jnp.where(lane == h, do, zero)
        for b in range(seq // step):
            cols = slice(b * step, (b + 1) * step)
            s = mm_nt(kh, q[cols]) + bias_ref[:, cols]
            p = jnp.exp(s - lse_ref[0, 0, h : h + 1, cols])
            dp = mm_nt(vh, do[cols])
            ds = (p * (dp - jnp.sum(p * dp, axis=0, keepdims=True))).astype(BF)
            dv = dv + mm(p.astype(BF), doh[cols])
            dk = dk + mm(ds, qh[cols])
            dqs[b].append(mm(kt[h * HEAD_DIM : (h + 1) * HEAD_DIM], ds) * scale)
    dq = jnp.concatenate([jnp.concatenate(d, axis=0).T for d in dqs], axis=0)
    for i, g in enumerate((dq, dk, dv)):
        at = pl.multiple_of(i * model + j * width, width)
        dqkv_ref[:, pl.ds(at, width)] = g.astype(BF)

    @pl.when(j == pairs - 1)
    def _():
        tile = 256
        lowt_ref[...] = low_ref[...].reshape(seq, model).T
        first_ref[...] = jnp.zeros_like(first_ref)

        @pl.when(r == 0)
        def _():
            acc_ref[...] = jnp.zeros_like(acc_ref)
            table_ref[...] = jnp.zeros_like(table_ref)

        def piece(n, carry):
            cols = pl.ds(pl.multiple_of(n * tile, tile), tile)
            part = dqkv_ref[:, cols]
            acc_ref[:, cols] += mm(lowt_ref[...], part)
            first_ref[...] += mm_nt(part, w_ref[:, cols])
            return carry

        lax.fori_loop(0, 3 * model // tile, piece, 0)
        for h in range(sub):
            grad = first_ref[h * length : (h + 1) * length, :]
            vision = col_ref[h, 0] > 0.5
            z, rstd = norm(tok_ref[h, 0].astype(F32))
            gain = jnp.where(vision, gain_ref[1:2], gain_ref[0:1])
            for i, term in enumerate((grad * z, grad)):
                for e, part in enumerate((jnp.where(vision, 0.0, term), jnp.where(vision, term, 0.0))):
                    at = 2 * i + e
                    table_ref[at : at + 1, :] += jnp.sum(part, axis=0, keepdims=True)
            tail = (extra_ref[h, 0] + norm_back(grad, gain, z, rstd)).astype(BF)

            @pl.when(r < early)
            def _(h=h, tail=tail):
                rows_ref[h, jnp.minimum(r, early - 1)] = tail

            @pl.when(r == early)
            def _(h=h, tail=tail):
                tail_ref[h, 0] = tail

        for i in range(early):

            @pl.when(r == i)
            def _(i=i):
                for copy in homes[i]:
                    copy.start()

    @pl.when((r == rows - 1) & (j == pairs - 1))
    def _():
        height = in_ref.shape[1]
        for p in range(in_ref.shape[0]):
            in_ref[p] = acc_ref[p * height : (p + 1) * height, :].astype(BF)
        while not all(stream.done for stream in streams):
            for stream in streams:
                if not stream.done:
                    stream.step()
        for i in range(calls):
            for at in spots(streams[i].result):
                up_ref[(i, *at)] = streams[i].result[at or ...]
        down_ref[...] = streams[-1].result[...]
        for copy in [*stays, *moves, *sum(homes, [])]:
            copy.wait()
        for stream in streams:
            stream.close()


def attention_backward(
    segment, qkv, grad, lse, low, weight, tok, extra, col, gain, up_kept, up_came, down_kept, down_came, leaving, dp_bits
):
    sub, rows, length, wide = qkv.shape
    seq = sub * length
    model = wide // 3
    pairs = model // 128
    groups = 1 << dp_bits
    calls = len(up_kept)
    part = attn_specs(sub, length, pairs)
    per, high = model // groups, down_kept[0].shape[2]
    row = pl.BlockSpec((sub, 1, length, model), lambda r, j: (0, r, 0, 0))
    hbm = pl.BlockSpec(memory_space=pl.ANY)

    def fixed(*shape):
        return pl.BlockSpec(shape, lambda r, j: (0,) * len(shape), pipeline_mode=pl.Buffered(1))

    up_kept, up_came = (
        [k.reshape((2,) * dp_bits + (per, model)) for k in ks] for ks in (up_kept, up_came)
    )
    ups, downs = up_order(dp_bits), down_order(dp_bits)
    scratch = [
        s
        for _ in range(calls)
        for s in [pltpu.VMEM((2,) * dp_bits + (per, model), BF)] * 2
        + [pltpu.VMEM((2,) * (dp_bits - 1 - i) + (per, model), BF) for i in range(2)]
    ]
    scratch += stream_scratch(downs, (high, model), True)
    sems = 2 * calls + len(downs) + 3 * rows
    loads = 2 * calls + 2 * calls * (groups // 8) + rows
    up_tail = (calls,) + (2,) * (dp_bits - 2) + (per, model)
    return pl.pallas_call(
        functools.partial(attn_bwd_kernel, calls, dp_bits),
        grid=(rows, pairs),
        in_specs=[
            pl.BlockSpec((1, seq, 1), lambda r, j: (r, 0, 0)),
            pl.BlockSpec((1, 1, seq), lambda r, j: (r, 0, 0)),
            part(0),
            part(1),
            part(2),
            part(0),
            pl.BlockSpec((1, 1, 2, seq), lambda r, j: (r, j, 0, 0)),
            row,
            fixed(*weight.shape),
            row,
            row,
            pl.BlockSpec((sub, 1, length, 1), lambda r, j: (0, r, 0, 0)),
            fixed(*gain.shape),
        ]
        + [hbm] * (4 * calls + 1),
        out_specs=[
            fixed(groups, per, wide), fixed(4, model), fixed(sub, 1, length, model),
            fixed(*up_tail), fixed(high, model), hbm, hbm,
        ],
        out_shape=[
            jax.ShapeDtypeStruct((groups, per, wide), BF),
            jax.ShapeDtypeStruct((4, model), F32),
            jax.ShapeDtypeStruct((sub, 1, length, model), BF),
            jax.ShapeDtypeStruct(up_tail, BF),
            jax.ShapeDtypeStruct((high, model), BF),
            jax.ShapeDtypeStruct(leaving.shape, BF),
            jax.ShapeDtypeStruct((sub, rows - 1, length, model), BF),
        ],
        scratch_shapes=[
            pltpu.VMEM((seq, seq), F32),
            pltpu.VMEM((seq, wide), BF),
            pltpu.VMEM((model, seq), BF),
            pltpu.VMEM((model, wide), F32),
            pltpu.VMEM((seq, model), F32),
            pltpu.VMEM((sub, rows - 1, length, model), BF),
        ]
        + scratch
        + [
            pltpu.SemaphoreType.DMA((sems,)),
            pltpu.SemaphoreType.DMA((sems,)),
            pltpu.SemaphoreType.DMA((loads,)),
        ],
        compiler_params=pltpu.CompilerParams(
            collective_id=1, has_side_effects=True, vmem_limit_bytes=VMEM_BYTES
        ),
        cost_estimate=pl.CostEstimate(
            flops=20 * rows * seq * seq * model + 4 * rows * seq * model * wide,
            bytes_accessed=100 * 1024 * 1024,
            transcendentals=rows * seq * seq * model // HEAD_DIM,
        ),
        name="attn_bwd",
    )(
        segment[:, :, None], segment[:, None, :], qkv, qkv, qkv, grad, lse, low, weight,
        tok, extra, col, gain,
        *up_kept, *up_came, *down_kept, *down_came, leaving,
    )


def finish_kernel(calls, dp_bits, *refs):
    refs = list(refs)
    up_ref, in_ref, out_ref = draw(refs, 3)
    tables = draw(refs, 3)
    last_ref, rows_ref, att_ref, up_out, down_ref, table_ref, home_ref = draw(refs, 7)
    env = peers()
    copies = Copies(*refs[-3:])
    remote = copies.remote
    core, x = env["head", 0][0], env["head", 1][0]
    me = lax.axis_index("head")
    groups = 1 << dp_bits
    model = home_ref.shape[-1]
    x_partner, core_partner = env["head", 1][1], env["head", 0][1]

    streams, loads = [], []
    for half, order in enumerate(attention_orders(dp_bits)):
        buf, *gots = draw(refs, 1 + len(order))
        loads.append([])
        lanes = buf.shape[-1]
        for i in range(4):
            ref, start = (out_ref, 0) if i == 3 else (in_ref, i * model)
            for p in range(groups):
                spot_of = {("head", 0): i >> 1, ("head", 1): i & 1}
                spot_of.update({("dp", b): p >> b & 1 for b in range(dp_bits)})
                cols = pl.ds(start + half * lanes, lanes)
                loads[-1].append(
                    copies.local(ref.at[p, :, cols], buf.at[tuple(spot_of[o] for o in order)])
                )
        streams.append(Halving(env, order, buf, gots, None, remote))
    order = up_order(dp_bits)[2:]
    for i in range(calls):
        buf, *gots = draw(refs, 1 + len(order))
        loads.append([copies.local(up_ref.at[i], buf)])
        streams.append(Halving(env, order, buf, gots, None, remote))
    (last_got,) = draw(refs, 1)
    sbuf, *sgots = draw(refs, 3 + dp_bits)

    for group in loads:
        for copy in group:
            copy.start()
    moves = []
    for o in range(1, 4):
        to = (me // 4) * 4 + flipped(me % 4, o)
        moves.append(remote(rows_ref.at[to], home_ref.at[me], {"head": to}))

    top, beyond = env["dp", dp_bits - 1]
    here, over = down_ref.at[x], down_ref.at[1 - x]
    last = remote(last_ref, last_got, beyond)
    to_x, to_core = remote(here, here, x_partner), remote(here, here, core_partner)
    forward = remote(over, over, core_partner)
    greet(env)

    for copy in moves:
        copy.start()

    @pl.when(top != core)
    def _():
        last.start()

    for i, (stream, group) in enumerate(zip(streams, loads)):
        for copy in group:
            copy.wait()
        if i < 2:
            stream.send()

    for at, ref in zip((0, 4, 6), tables):
        sbuf[at : at + ref.shape[0], :] = ref[...]
    sorder = [("head", 0), ("head", 1)] + [("dp", b) for b in range(dp_bits)]
    scopies = [remote(sbuf, got, env[o][1]) for o, got in zip(sorder, sgots)]
    scopies[0].start()
    home_ref[me] = rows_ref[me]

    gathers, after = [], []

    def spread(place, value):
        mine = place(x)
        mine[...] = value[...]
        for to, where in ((x_partner, after), (core_partner, gathers)):
            copy = remote(mine, mine, to)
            copy.start()
            where.append((copy, place))

    def att_place(half, side):
        at = (2 * core + side) * model + half * (model // 2)
        return att_ref.at[:, pl.ds(pl.multiple_of(at, 128), model // 2)]

    def up_place(call, side):
        at = (core * calls + call) * model
        return up_out.at[side, :, pl.ds(pl.multiple_of(at, 128), model)]

    rounds = max(len(sorder), max(len(stream.rounds) for stream in streams))
    for r in range(rounds):
        for i, stream in enumerate(streams):
            if not stream.done and (i < 2 or r >= 3):
                stream.step()
                if stream.done:
                    if i < 2:
                        spread(functools.partial(att_place, i), stream.result)
                    else:
                        spread(functools.partial(up_place, i - 2), stream.result)
        if r < len(sorder):
            scopies[r].wait()
            sbuf[...] = sbuf[...] + sgots[r][...]
            if r + 1 < len(sorder):
                scopies[r + 1].start()
        if r == 1:
            for stream in streams[2:]:
                stream.send()
        if r == 1:

            @pl.when(top == core)
            def _():
                last.wait_recv()
                here[...] = last_ref[...] + last_got[...]
                to_x.start()
                to_core.start()

    table_ref[...] = sbuf[...]
    forwards = []
    for copy, place in after:
        copy.wait_recv()
        other = place(1 - x)
        forwards.append(remote(other, other, core_partner))
        forwards[-1].start()

    @pl.when(top == core)
    def _():
        to_x.wait_recv()
        forward.start()
        to_core.wait_send()
        to_x.wait_send()
        forward.wait_send()

    @pl.when(top != core)
    def _():
        last.wait_send()
        to_core.wait_recv()
        forward.wait_recv()

    for copy, _ in gathers:
        copy.wait()
    for copy in forwards:
        copy.wait()
    for copy, _ in after:
        copy.wait_send()
    for stream in streams:
        stream.close()
    for copy in moves:
        copy.wait()


def flipped(index, offset):
    low, high = index % 2, index // 2
    if offset & 1:
        low = 1 - low
    if offset & 2:
        high = 1 - high
    return 2 * high + low


def finish(dp_bits, up, down, in_term, out_term, tables, rows):
    assert rows.shape[0] == 4
    calls = up.shape[0]
    groups, per, model = out_term.shape
    high = down.shape[0]
    orders = attention_orders(dp_bits)
    ups = up_order(dp_bits)[2:]
    scratch = [s for o in orders for s in stream_scratch(o, (per, model // 2), False)]
    scratch += [s for _ in range(calls) for s in stream_scratch(ups, (per, model), False)]
    scratch.append(pltpu.VMEM((high, model), BF))
    scratch += [pltpu.VMEM((8, model), F32)] * (3 + dp_bits)
    sems = sum(map(len, orders)) + calls * len(ups) + 3 + 4 + 2 + dp_bits + 3 * (calls + 2)
    loads = 2 * 4 * groups + calls
    hbm = pl.BlockSpec(memory_space=pl.ANY)
    vmem = pl.BlockSpec(memory_space=pltpu.VMEM)
    return pl.pallas_call(
        functools.partial(finish_kernel, calls, dp_bits),
        in_specs=[hbm] * 3 + [vmem] * 5,
        out_specs=[vmem] * 5,
        out_shape=[
            jax.ShapeDtypeStruct((per, 4 * model), BF),
            jax.ShapeDtypeStruct((2, per, 2 * calls * model), BF),
            jax.ShapeDtypeStruct((2, high, model), BF),
            jax.ShapeDtypeStruct((8, model), F32),
            jax.ShapeDtypeStruct(rows.shape, BF),
        ],
        scratch_shapes=scratch
        + [
            pltpu.SemaphoreType.DMA((sems,)),
            pltpu.SemaphoreType.DMA((sems,)),
            pltpu.SemaphoreType.DMA((loads,)),
        ],
        compiler_params=pltpu.CompilerParams(
            collective_id=0, has_side_effects=True, vmem_limit_bytes=VMEM_BYTES
        ),
        cost_estimate=pl.CostEstimate(
            flops=0, bytes_accessed=100 * 1024 * 1024, transcendentals=0
        ),
        name="finish",
    )(up, in_term, out_term, *tables, down, rows)


def enter_kernel(tokens_ref, modality_ref, gain_ref, shift_ref, w_ref, *refs):
    refs = list(refs)
    tok_ref, kind_ref, col_ref, low_ref, qkv_ref, wide_ref, send_ref = draw(refs, 7)
    copies = Copies(*refs)
    me = lax.axis_index("head")
    heads, rows, length, model = tok_ref.shape
    core = me % 2
    targets = others()
    loads = {
        (o, r): copies.local(tokens_ref.at[to, r], wide_ref.at[to, r])
        for r in range(rows)
        for o, to in enumerate([*targets, me])
    }
    kinds = [copies.remote(modality_ref.at[to // 2], kind_ref.at[me], {"head": to}) for to in targets]
    sends = {
        (o, r): copies.remote(send_ref.at[to, r], tok_ref.at[me, r], {"head": to})
        for r in range(rows)
        for o, to in enumerate(targets)
    }
    for copy in loads.values():
        copy.start()
    barrier = pltpu.get_barrier_semaphore()
    for to in targets:
        pl.semaphore_signal(
            barrier, inc=1, device_id={"head": to}, device_id_type=pl.DeviceIdType.MESH
        )
    pl.semaphore_wait(barrier, len(targets))
    for copy in kinds:
        copy.start()
    kind_ref[me] = modality_ref[me // 2]
    for r in range(rows):
        for o, to in enumerate(targets):
            loads[o, r].wait()
            send_ref[to, r] = wide_ref[to, r].astype(BF)
            sends[o, r].start()
        loads[len(targets), r].wait()
        tok_ref[me, r] = wide_ref[me, r].astype(BF)
    for copy in kinds:
        copy.wait()
    ones = jnp.ones((8, length), BF)
    row = lax.broadcasted_iota(jnp.int32, (8, length), 0)
    for r in range(rows):
        for o in range(len(targets)):
            sends[o, r].wait_recv()
        for h in range(heads):
            kind = kind_ref[h, core, r : r + 1, :].astype(F32)
            kind = jnp.where(row == 0, jnp.broadcast_to(kind, (8, length)), 0.0).astype(BF)
            kind = mm_tn(kind, ones)[:, :1]
            col_ref[h, r] = kind
            z, _ = norm(tok_ref[h, r].astype(F32))
            low = z * jnp.where(kind < 0.5, gain_ref[0:1], gain_ref[1:2])
            low_ref[h, r] = (low + jnp.where(kind < 0.5, shift_ref[0:1], shift_ref[1:2])).astype(BF)
        low = low_ref[:, r].reshape(heads * length, model)
        for n in range(w_ref.shape[1] // model):
            cols = slice(n * model, (n + 1) * model)
            part = mm(low, w_ref[:, cols]).astype(BF)
            qkv_ref[:, r, :, cols] = part.reshape(heads, length, model)
    for copy in sends.values():
        copy.wait_send()


def enter(tokens, modality, gain, shift, weight):
    heads, rows, _, model = tokens.shape
    assert heads == 4
    vmem = pl.BlockSpec(memory_space=pltpu.VMEM)
    sems = 3 * rows + 3
    return pl.pallas_call(
        enter_kernel,
        in_specs=[pl.BlockSpec(memory_space=pl.ANY)] + [vmem] * 4,
        out_specs=[vmem] * 5,
        out_shape=[
            jax.ShapeDtypeStruct(tokens.shape, BF),
            jax.ShapeDtypeStruct((heads,) + modality.shape[1:], jnp.int32),
            jax.ShapeDtypeStruct(tokens.shape[:3] + (1,), F32),
            jax.ShapeDtypeStruct(tokens.shape, BF),
            jax.ShapeDtypeStruct(tokens.shape[:3] + weight.shape[1:], BF),
        ],
        scratch_shapes=[
            pltpu.VMEM(tokens.shape, F32),
            pltpu.VMEM(tokens.shape, BF),
            pltpu.SemaphoreType.DMA((sems,)),
            pltpu.SemaphoreType.DMA((sems,)),
            pltpu.SemaphoreType.DMA((4 * rows,)),
        ],
        compiler_params=pltpu.CompilerParams(
            collective_id=2, has_side_effects=True, vmem_limit_bytes=VMEM_BYTES
        ),
        cost_estimate=pl.CostEstimate(
            flops=2 * tokens.size * weight.shape[1], bytes_accessed=40 * 1024 * 1024,
            transcendentals=0,
        ),
        name="enter",
    )(tokens, modality, gain, shift, weight)


def norm(values):
    mean = jnp.mean(values, axis=-1, keepdims=True)
    centered = values - mean
    rstd = lax.rsqrt(jnp.mean(centered * centered, axis=-1, keepdims=True) + EPS)
    return centered * rstd, rstd


def pick(table, kind):
    return jnp.where(kind == 0, table[0], table[1])


def norm_back(grad, gains, z, rstd):
    q = grad * gains
    return rstd * (
        q
        - jnp.mean(q, axis=-1, keepdims=True)
        - z * jnp.mean(q * z, axis=-1, keepdims=True)
    )


def by_expert(values, kind):
    first = jnp.sum(jnp.where(kind == 0, values, 0.0), axis=0)
    second = jnp.sum(jnp.where(kind == 0, 0.0, values), axis=0)
    return jnp.stack([first, second])


def flip(axis, size, bit):
    return functools.partial(
        lax.ppermute, axis_name=axis, perm=[(i, i ^ (1 << bit)) for i in range(size)]
    )


def take(values, dim, index):
    return lax.dynamic_index_in_dim(values, index, dim, keepdims=False)


def body(sizes, tokens, segment, modality, first_gain, first_shift, project_in, project_out,
         second_gain, second_shift, up_weight, down_weight, cotangent):
    heads, groups = sizes["head"], sizes["dp"]
    row_count, length, model = tokens.shape
    rows = row_count // heads
    count = row_count * length
    hidden = up_weight.shape[-1]
    me_h, me_d = lax.axis_index("head"), lax.axis_index("dp")
    core = me_h % 2
    head_bits = heads.bit_length() - 1
    dp_bits = groups.bit_length() - 1
    assert heads == 1 << head_bits and groups == 1 << dp_bits and head_bits >= 2
    hflip = [flip("head", heads, b) for b in range(head_bits)]
    dflip = [flip("dp", groups, b) for b in range(dp_bits)]

    grid = (heads, rows, length)
    tok, kinds, col, low1, qkv = enter(
        tokens.reshape(*grid, model), modality.reshape(heads // 2, 2, rows, length),
        first_gain, first_shift, project_in,
    )
    seg = lax.dynamic_slice_in_dim(segment, me_h * rows, rows, 0)
    kind = take(kinds, 1, core).reshape(count)
    kcol = col.reshape(count, 1)

    flat = tok.astype(F32).reshape(count, model)
    context, lse, cot = attention_forward(seg, qkv, cotangent.reshape(*grid, model))
    cot = cot.reshape(count, model)
    ctx = context.reshape(count, model)
    attention = mm(ctx, project_out)
    residual = flat + attention
    z2, rstd2 = norm(residual)
    gain2 = pick(second_gain, kcol)
    low2 = (z2 * gain2 + pick(second_shift, kcol)).astype(BF)

    slots = count + BLK
    is0 = (kind == 0).astype(F32).reshape(count // BLK, BLK)
    tri = jnp.triu(jnp.ones((BLK, BLK), F32))
    inner = mm(is0, tri)
    ends = jnp.cumsum(inner[:, -1])
    before = (inner + (ends - inner[:, -1])[:, None]).reshape(count).astype(jnp.int32)
    n0 = ends[-1].astype(jnp.int32)
    blocks0 = (n0 + BLK - 1) // BLK
    blocks1 = (count - n0 + BLK - 1) // BLK
    rank1 = jnp.arange(count, dtype=jnp.int32) - before
    slot = jnp.where(kind == 0, before - 1, blocks0 * BLK + rank1)
    place = (slot[None, :] == jnp.arange(slots, dtype=jnp.int32)[:, None]).astype(BF)

    near = hflip[0]
    g_mine = mm(place, cot).astype(BF)
    g_other = near(g_mine)
    zeros = jnp.sum(kinds == 0, axis=(0, 2, 3))
    full = jnp.stack([(zeros + BLK - 1) // BLK, (count - zeros + BLK - 1) // BLK], axis=1)
    blocks, blocks_other = take(full, 0, core), take(full, 0, 1 - core)
    xbit = (me_h // 2) % 2
    ybit = me_d % 2
    info = jnp.concatenate([blocks, blocks_other, jnp.stack([xbit, ybit, core])]).astype(jnp.int32)
    x_mine = mm(place, low2).astype(BF)
    x_other = near(x_mine)

    partial, kept, came = None, ([], []), ([], [])
    for call in range(CALLS):
        *partial, up_keep, up_send, down_keep, down_send = ffn(
            call, info, x_mine, x_other, g_mine, g_other, up_weight, down_weight, partial, groups
        )
        kept[0].append(up_keep)
        kept[1].append(down_keep)
        came[0].append(hflip[1](up_send))
        came[1].append(dflip[0](down_send))

    partial, early = lax.optimization_barrier((partial, [c[:-1] for c in came]))
    came = [e + c[-1:] for e, c in zip(early, came)]
    branch_mine, branch_other, dx_mine, dx_other = partial
    dx = dx_mine + near(dx_other)
    second_grad = mm_tn(place, dx)
    branch = mm_tn(place, branch_mine + near(branch_other))
    leaving = (attention + branch).astype(BF).reshape(*grid, model)

    cot32 = cot.astype(F32)
    gain2_term = by_expert(second_grad * z2, kcol)
    shift2_term = by_expert(second_grad, kcol)
    extra = norm_back(second_grad, gain2, z2, rstd2)
    attention_low = (cot32 + extra).astype(BF)
    out_term = mm_tn(ctx, attention_low)
    context_grad = mm_nt(attention_low, project_out).astype(BF)
    in_term, table1, tail, up_sum, down_sum, back, home0 = attention_backward(
        seg, qkv, context_grad.reshape(context.shape), lse, low1, project_in,
        tok, extra.reshape(*grid, model), col, first_gain,
        kept[0], came[0], kept[1], came[1], leaving, dp_bits,
    )
    output = tokens + back.reshape(row_count, length, model).astype(F32)
    att_sum, up_sum, down_sum, table, home = finish(
        dp_bits, up_sum, down_sum, in_term,
        out_term.astype(BF).reshape(groups, model // groups, model),
        (table1, gain2_term, shift2_term), tail,
    )
    home = jnp.concatenate([home0, home], axis=1)
    input_grad = cotangent + home.reshape(row_count, length, model).astype(F32)

    up_grad, down_grad = up_sum.astype(F32), down_sum.astype(F32)
    in_grad = att_sum[:, : 3 * model].astype(F32)
    out_grad = att_sum[:, 3 * model :].astype(F32)
    tables = lax.dynamic_slice_in_dim(table, me_d * (model // groups), model // groups, 1)
    tables = tables.reshape(4, EXPERTS, model // groups)
    return (
        output, input_grad, tables[0], tables[1], in_grad, out_grad, tables[2], tables[3],
        up_grad, down_grad,
    )


def solution(mesh):
    return jax.shard_map(
        functools.partial(body, dict(mesh.shape)),
        mesh=mesh,
        in_specs=(
            P("dp", "head", None),
            P("dp", None),
            P("dp", "head"),
            P(),
            P(),
            P(),
            P(),
            P(),
            P(),
            P(),
            P(),
            P("dp", "head", None),
        ),
        out_specs=(
            P("dp", "head", None),
            P("dp", "head", None),
            P(None, "dp"),
            P(None, "dp"),
            P("dp", None),
            P("dp", None),
            P(None, "dp"),
            P(None, "dp"),
            P(None, "dp", None),
            P(None, "dp", None),
        ),
        check_vma=False,
    )
```

```python
import functools

import jax
import jax.numpy as jnp
from jax import lax
from jax.experimental import pallas as pl
from jax.experimental.pallas import tpu as pltpu
from jax.sharding import PartitionSpec as P

HEAD_DIM = 64
EXPERTS = 2
EPS = 1e-05
NEG = -1000000000.0
BLK = 128
CALLS = 2
VMEM_BYTES = 60 * 1024 * 1024
BF = jnp.bfloat16
F32 = jnp.float32
NT = (((1,), (1,)), ((), ()))
TN = (((0,), (0,)), ((), ()))


def mm(a, b):
    return jnp.dot(a, b, preferred_element_type=F32)


def mm_nt(a, b):
    return lax.dot_general(a, b, NT, preferred_element_type=F32)


def mm_tn(a, b):
    return lax.dot_general(a, b, TN, preferred_element_type=F32)


def bias_of(segc_ref, segr_ref, bias_ref):
    same = segc_ref[0] == segr_ref[0]
    bias_ref[...] = jnp.where(same, 0.0, NEG)


def attn_specs(sub, length, pairs):
    def part(i):
        return pl.BlockSpec((sub, 1, length, 128), lambda r, j, i=i: (0, r, 0, i * pairs + j))

    return part


def ffn_kernel(first, bits, info_ref, xm_ref, xo_ref, gm_ref, go_ref, u_ref, d_ref, *refs):
    refs = list(refs)
    prev = [] if first else draw(refs, 4)
    outs, grads = draw(refs, 4), draw(refs, 4)
    du_ref, dd_ref, act_ref, dh_ref, x_ref, g_ref = draw(refs, 6)
    held, up_ref, keep_ref, send_ref, sem = draw(refs, 2), *refs
    e = pl.program_id(0)
    slots, model = xm_ref.shape
    cols = u_ref.shape[-1]
    tile = 256
    down = d_ref[0]
    made = [0]

    def local(src, dst):
        made[0] += 1
        return pltpu.make_async_copy(src, dst, sem.at[made[0] - 1])

    loads = [
        [local(x, x_ref.at[i]), local(g, g_ref.at[i])]
        + [local(p, h.at[i]) for p, h in zip(prev[i::2], held)]
        for i, (x, g) in enumerate(((xm_ref, gm_ref), (xo_ref, go_ref)))
    ]
    stores = [[local(h.at[i], out) for h, out in zip(held, outs[i::2])] for i in range(2)]

    @pl.when(e == 0)
    def _():
        for copy in loads[0] + loads[1]:
            copy.start()
        if first:
            for h in held:
                for which in range(2):
                    h[which, slots - BLK :, :] = jnp.zeros((BLK, model), BF)

    du_ref[...] = jnp.zeros_like(du_ref)
    dd_ref[...] = jnp.zeros_like(dd_ref)

    def chunk(which, block, count):
        size = count * BLK
        rows = pl.ds(pl.multiple_of(block * BLK, BLK), size)
        x = x_ref[which, rows, :]
        g = g_ref[which, rows, :]
        for n in range(cols // tile):
            part = slice(n * tile, (n + 1) * tile)
            h = mm(x, u_ref[0, :, part])
            da = mm_nt(g, down[part, :])
            cdf = 0.5 + 0.5 * lax.erf(h * 0.7071067811865476)
            pdf = 0.3989422804014327 * jnp.exp(-0.5 * h * h)
            act_ref[:size, part] = (h * cdf).astype(BF)
            dh_ref[:size, part] = (da * (cdf + h * pdf)).astype(BF)
        act = act_ref[:size, :]
        dh = dh_ref[:size, :]
        for slot, value in enumerate((mm(act, down), mm_nt(dh, u_ref[0]))):
            if not first:
                value = value + held[slot][which, rows, :].astype(F32)
            held[slot][which, rows, :] = value.astype(BF)
        du_ref[...] += mm_tn(x, dh)
        dd_ref[...] += mm_tn(act, g)

    def side(which, carry):
        for i in range(2):

            @pl.when((e == 0) & (which == i))
            def _(i=i):
                for copy in loads[i]:
                    copy.wait()

        n0 = info_ref[2 * which]
        n1 = info_ref[2 * which + 1]
        start = jnp.where(e == 0, 0, n0)
        count = jnp.where(e == 0, n0, n1)
        fours = count // 4 - jnp.where((count % 4 == 1) & (count > 4), 1, 0)

        def four(i, carry):
            chunk(which, start + 4 * i, 4)
            return carry

        lax.fori_loop(0, fours, four, 0)
        for left in (1, 2, 3, 5):

            @pl.when(count - 4 * fours == left)
            def _(left=left):
                chunk(which, start + 4 * fours, left)

        for i in range(2):

            @pl.when((e == EXPERTS - 1) & (which == i))
            def _(i=i):
                for copy in stores[i]:
                    copy.start()

        return carry

    lax.fori_loop(0, 2, side, 0)

    up_keep, up_send, down_keep, down_send = grads
    groups = 1 << bits
    per = model // groups
    wide = keep_ref.shape[2]
    xbit, ybit = info_ref[4], info_ref[5]
    for p in range(groups):
        up_ref[e, spot(p, range(bits))] = du_ref[p * per : (p + 1) * per, :].astype(BF)
    for y in range(2):
        for ref, here in ((keep_ref, ybit == y), (send_ref, ybit != y)):

            @pl.when(here)
            def _(ref=ref, y=y):
                for p in range(y, cols // wide, 2):
                    at = spot(p >> 1, range(bits - 3))
                    ref[at, e] = dd_ref[p * wide : (p + 1) * wide, :].astype(BF)

    sends = []
    for i in range(EXPERTS):
        ups = local(up_ref.at[i], up_keep), local(up_ref.at[i], up_send)
        downs = [
            local(src.at[:, i], dst.at[:, i])
            for src, dst in ((keep_ref, down_keep), (send_ref, down_send))
        ]
        sends.append((ups, downs))

        @pl.when(e == i)
        def _(ups=ups, downs=downs, i=i):
            for copy in downs:
                copy.start()
            for copy, here in zip(ups, (xbit == i, xbit != i)):

                @pl.when(here)
                def _(copy=copy):
                    copy.start()

    @pl.when(e == EXPERTS - 1)
    def _():
        for copy in stores[0] + stores[1]:
            copy.wait()
        for i, (ups, downs) in enumerate(sends):
            for copy in downs:
                copy.wait()
            for copy, here in zip(ups, (xbit == i, xbit != i)):

                @pl.when(here)
                def _(copy=copy):
                    copy.wait()


def spot(index, order):
    return functools.reduce(lambda acc, bit: 2 * acc + (index >> bit & 1), order, 0)


def ffn(call, info, x_mine, x_other, g_mine, g_other, up, down, partial, groups):
    slots, model = x_mine.shape
    hidden = up.shape[-1]
    cols = hidden // (2 * CALLS)
    bits = groups.bit_length() - 1
    hbm = pl.BlockSpec(memory_space=pl.ANY)
    first = partial is None
    extra = () if first else tuple(partial)
    grads = [(groups, model // groups, model)] * 2
    grads += [(groups // 8, EXPERTS, hidden // groups, model)] * 2
    return pl.pallas_call(
        functools.partial(ffn_kernel, first, bits),
        grid_spec=pltpu.PrefetchScalarGridSpec(
            num_scalar_prefetch=1,
            grid=(EXPERTS,),
            in_specs=[hbm] * 4
            + [
                pl.BlockSpec((1, model, cols), lambda e, i: (e, 0, i[6] * CALLS + call)),
                pl.BlockSpec((1, cols, model), lambda e, i: (e, i[6] * CALLS + call, 0)),
            ]
            + [hbm] * len(extra),
            out_specs=[hbm] * 8,
            scratch_shapes=[
                pltpu.VMEM((model, cols), F32),
                pltpu.VMEM((cols, model), F32),
                pltpu.VMEM((5 * BLK, cols), BF),
                pltpu.VMEM((5 * BLK, cols), BF),
                pltpu.VMEM((2, slots, model), BF),
                pltpu.VMEM((2, slots, model), BF),
                pltpu.VMEM((2, slots, model), BF),
                pltpu.VMEM((2, slots, model), BF),
                pltpu.VMEM((EXPERTS,) + grads[0], BF),
                pltpu.VMEM(grads[2], BF),
                pltpu.VMEM(grads[2], BF),
                pltpu.SemaphoreType.DMA((24,)),
            ],
        ),
        out_shape=[jax.ShapeDtypeStruct((slots, model), BF)] * 4
        + [jax.ShapeDtypeStruct(g, BF) for g in grads],
        compiler_params=pltpu.CompilerParams(vmem_limit_bytes=VMEM_BYTES),
        cost_estimate=pl.CostEstimate(
            flops=12 * 2 * slots * model * cols, bytes_accessed=40 * 1024 * 1024,
            transcendentals=2 * 2 * slots * cols,
        ),
        name="ffn",
    )(info, x_mine, x_other, g_mine, g_other, up, down, *extra)


def peers():
    out = {}
    for axis in ("head", "dp"):
        me = lax.axis_index(axis)
        for b in range(lax.axis_size(axis).bit_length() - 1):
            bit = (me // (1 << b)) % 2
            out[axis, b] = bit, {axis: me + (1 - 2 * bit) * (1 << b)}
    return out


class Halving:
    def __init__(self, env, order, buf, gots, first, remote):
        self.rounds, path, prev = [], (), first
        for o, got in zip(order, gots):
            bit, partner = env[o]
            view = buf.at[path] if path else buf
            away, stay = view.at[1 - bit], view.at[bit]
            halves = (None, None) if prev is None else (prev.at[1 - bit], prev.at[bit])
            self.rounds.append((away, stay, *halves, remote(away, got, partner)))
            path, prev = path + (bit,), got
        self.result, self.last, self.at = buf.at[path], prev, 0
        self.done = False

    def send(self):
        away, stay, got_away, got_stay, copy = self.rounds[self.at]
        accumulate(away, got_away)
        copy.start()
        accumulate(stay, got_stay)

    def step(self):
        self.rounds[self.at][-1].wait_recv()
        self.at += 1
        if self.at < len(self.rounds):
            self.send()
        else:
            accumulate(self.result, self.last)
            self.done = True

    def close(self):
        for *_, copy in self.rounds:
            copy.wait_send()


def spots(ref):
    lead = len(ref.shape) - 2
    return [tuple(i >> b & 1 for b in range(lead)) for i in range(1 << lead)]


def accumulate(into, got):
    if got is not None:
        for at in spots(into):
            at = at or ...
            into[at] = into[at] + got[at]


def neighbours(env):
    me = lax.axis_index("head")
    out = [partner for _, partner in env.values()]
    for o in range(1, lax.axis_size("head")):
        if o & (o - 1):
            out.append({"head": (me // 4) * 4 + flipped(me % 4, o)})
    return out


def greet(env):
    barrier = pltpu.get_barrier_semaphore()
    partners = neighbours(env)
    for partner in partners:
        pl.semaphore_signal(barrier, inc=1, device_id=partner, device_id_type=pl.DeviceIdType.MESH)
    pl.semaphore_wait(barrier, len(partners))


class Copies:
    def __init__(self, send_sem, recv_sem, load_sem):
        self.send_sem, self.recv_sem, self.load_sem = send_sem, recv_sem, load_sem
        self.used, self.loads = 0, 0

    def remote(self, src, dst, to):
        s = self.used
        self.used += 1
        return pltpu.make_async_remote_copy(
            src_ref=src, dst_ref=dst, send_sem=self.send_sem.at[s], recv_sem=self.recv_sem.at[s],
            device_id=to, device_id_type=pl.DeviceIdType.MESH,
        )

    def local(self, src, dst):
        self.loads += 1
        return pltpu.make_async_copy(src, dst, self.load_sem.at[self.loads - 1])


def draw(refs, k):
    out = refs[:k]
    del refs[:k]
    return out


def others():
    me = lax.axis_index("head")
    return [(me // 4) * 4 + flipped(me % 4, o) for o in (3, 2, 1)]


def attn_fwd_kernel(
    segc_ref, segr_ref, q_ref, k_ref, v_ref, cot_ref, o_ref, lse_ref, got_ref,
    bias_ref, *sems,
):
    sub, _, length, width = q_ref.shape
    seq = sub * length
    copies = Copies(*sems)
    me = lax.axis_index("head")
    targets = others()
    sends = [copies.remote(cot_ref.at[to], got_ref.at[me], {"head": to}) for to in targets]
    stays = copies.local(cot_ref.at[me], got_ref.at[me])
    barrier = pltpu.get_barrier_semaphore()
    at = pl.program_id(0) * pl.num_programs(1) + pl.program_id(1)

    @pl.when(at == 0)
    def _():
        for to in targets:
            pl.semaphore_signal(
                barrier, inc=1, device_id={"head": to}, device_id_type=pl.DeviceIdType.MESH
            )
        pl.semaphore_wait(barrier, len(targets))
        for copy in [*sends, stays]:
            copy.start()

    @pl.when(at == pl.num_programs(0) * pl.num_programs(1) - 1)
    def _():
        for copy in [*sends, stays]:
            copy.wait()

    @pl.when(pl.program_id(1) == 0)
    def _():
        bias_of(segc_ref, segr_ref, bias_ref)

    q = q_ref[...].reshape(seq, width) * jnp.asarray(HEAD_DIM**-0.5, BF)
    k = k_ref[...].reshape(seq, width)
    vt = v_ref[...].reshape(seq, width).T
    lane = lax.broadcasted_iota(jnp.int32, (1, width), 1) // HEAD_DIM
    zero = jnp.zeros((), BF)
    per = width // HEAD_DIM
    step = seq
    ks = [jnp.where(lane == h, k, zero) for h in range(per)]
    for b in range(seq // step):
        cols = slice(b * step, (b + 1) * step)
        parts = []
        for h in range(per):
            s = mm_nt(ks[h], q[cols]) + bias_ref[:, cols]
            top = jnp.max(s, axis=0, keepdims=True)
            e = jnp.exp(s - top)
            total = jnp.sum(e, axis=0, keepdims=True)
            parts.append(mm(vt[h * HEAD_DIM : (h + 1) * HEAD_DIM], e.astype(BF)) * (1.0 / total))
            lse_ref[0, 0, h : h + 1, cols] = top + jnp.log(total)
        out = jnp.concatenate(parts, axis=0).T.astype(BF)
        o_ref[:, 0] = out.reshape(sub, length, width)


def attention_forward(segment, qkv, cotangent):
    sub, rows, length, wide = qkv.shape
    seq = sub * length
    model = wide // 3
    pairs = model // 128
    part = attn_specs(sub, length, pairs)
    hbm = pl.BlockSpec(memory_space=pl.ANY)
    return pl.pallas_call(
        attn_fwd_kernel,
        grid=(rows, pairs),
        in_specs=[
            pl.BlockSpec((1, seq, 1), lambda r, j: (r, 0, 0)),
            pl.BlockSpec((1, 1, seq), lambda r, j: (r, 0, 0)),
            part(0),
            part(1),
            part(2),
            hbm,
        ],
        out_specs=[part(0), pl.BlockSpec((1, 1, 2, seq), lambda r, j: (r, j, 0, 0)), hbm],
        out_shape=[
            jax.ShapeDtypeStruct((sub, rows, length, model), BF),
            jax.ShapeDtypeStruct((rows, pairs, 2, seq), F32),
            jax.ShapeDtypeStruct(cotangent.shape, BF),
        ],
        scratch_shapes=[
            pltpu.VMEM((seq, seq), F32),
            pltpu.SemaphoreType.DMA((3,)),
            pltpu.SemaphoreType.DMA((3,)),
            pltpu.SemaphoreType.DMA((1,)),
        ],
        compiler_params=pltpu.CompilerParams(
            collective_id=3, has_side_effects=True, vmem_limit_bytes=VMEM_BYTES
        ),
        cost_estimate=pl.CostEstimate(
            flops=8 * rows * seq * seq * model, bytes_accessed=8 * rows * seq * model,
            transcendentals=rows * seq * seq * model // HEAD_DIM,
        ),
        name="attn_fwd",
    )(segment[:, :, None], segment[:, None, :], qkv, qkv, qkv, cotangent)


def up_order(dp_bits):
    return [("dp", b) for b in range(dp_bits)]


def down_order(dp_bits):
    return [("dp", b) for b in range(1, dp_bits - 1)] + [("head", 1)]


def attention_orders(dp_bits):
    rest = [("dp", b) for b in range(2, dp_bits)]
    core, x, y, z = ("head", 0), ("head", 1), ("dp", 0), ("dp", 1)
    return [core, y, z, x] + rest, [core, x, y, z] + rest


def stream_scratch(order, tail, first):
    sizes = [len(order)] * (2 if first else 1) + [len(order) - r for r in range(1, len(order) + 1)]
    return [pltpu.VMEM((2,) * k + tail, BF) for k in sizes]


def attn_bwd_kernel(calls, dp_bits, *refs):
    refs = list(refs)
    segc_ref, segr_ref, q_ref, k_ref, v_ref, do_ref, lse_ref, low_ref, w_ref = draw(refs, 9)
    tok_ref, extra_ref, col_ref, gain_ref = draw(refs, 4)
    up_kept, up_came, down_kept, down_came = (draw(refs, calls) for _ in range(4))
    leaving_ref, in_ref, table_ref, tail_ref, up_ref, down_ref, back_ref, home_ref = draw(refs, 8)
    bias_ref, dqkv_ref, lowt_ref, acc_ref, first_ref, rows_ref = draw(refs, 6)
    env = peers()
    copies = Copies(*refs[-3:])
    r, j = pl.program_id(0), pl.program_id(1)
    rows, pairs = pl.num_programs(0), pl.num_programs(1)
    me = lax.axis_index("head")

    streams, loads = [], []
    order = up_order(dp_bits)[:2]
    for i in range(calls):
        buf, first, *gots = draw(refs, 2 + len(order))
        loads.append([copies.local(up_kept[i], buf), copies.local(up_came[i], first)])
        streams.append(Halving(env, order, buf, gots, first, copies.remote))
    order = down_order(dp_bits)
    buf, first, *gots = draw(refs, 2 + len(order))
    lead = dp_bits - 3
    loads.append([])
    for i in range(calls):
        for p in range(1 << lead):
            at = tuple(p >> (lead - 1 - b) & 1 for b in range(lead)) + (i,)
            loads[-1].append(copies.local(down_kept[i].at[p], buf.at[at]))
            loads[-1].append(copies.local(down_came[i].at[p], first.at[at]))
    streams.append(Halving(env, order, buf, gots, first, copies.remote))
    moves = []
    for o in range(1, 4):
        to = (me // 4) * 4 + flipped(me % 4, o)
        moves.append(copies.remote(leaving_ref.at[to], back_ref.at[me], {"head": to}))
    stays = [copies.local(leaving_ref.at[me], back_ref.at[me])]
    early = rows_ref.shape[1]
    homes = []
    for i in range(early):
        homes.append([copies.local(rows_ref.at[me, i], home_ref.at[me, i])])
        for to in others():
            homes[i].append(copies.remote(rows_ref.at[to, i], home_ref.at[me, i], {"head": to}))

    @pl.when((r == 0) & (j == 0))
    def _():
        for group in loads:
            for copy in group:
                copy.start()
        stays[0].start()
        greet(env)
        for stream, group in zip(reversed(streams), reversed(loads)):
            for copy in group:
                copy.wait()
            stream.send()
        for copy in moves:
            copy.start()

    @pl.when((r == rows - 1) & (j == pairs // 2))
    def _():
        for stream in reversed(streams):
            stream.step()

    sub, _, length, width = q_ref.shape
    seq = sub * length
    model = dqkv_ref.shape[-1] // 3

    @pl.when(j == 0)
    def _():
        bias_of(segc_ref, segr_ref, bias_ref)

    scale = HEAD_DIM**-0.5
    q = q_ref[...].reshape(seq, width) * jnp.asarray(scale, BF)
    k = k_ref[...].reshape(seq, width)
    kt = k.T
    v = v_ref[...].reshape(seq, width)
    do = do_ref[...].reshape(seq, width)
    lane = lax.broadcasted_iota(jnp.int32, (1, width), 1) // HEAD_DIM
    zero = jnp.zeros((), BF)
    per = width // HEAD_DIM
    step = seq
    dk = jnp.zeros((seq, width), F32)
    dv = jnp.zeros((seq, width), F32)
    dqs = [[] for _ in range(seq // step)]
    for h in range(per):
        kh = jnp.where(lane == h, k, zero)
        vh = jnp.where(lane == h, v, zero)
        qh = jnp.where(lane == h, q, zero)
        doh = jnp.where(lane == h, do, zero)
        for b in range(seq // step):
            cols = slice(b * step, (b + 1) * step)
            s = mm_nt(kh, q[cols]) + bias_ref[:, cols]
            p = jnp.exp(s - lse_ref[0, 0, h : h + 1, cols])
            dp = mm_nt(vh, do[cols])
            ds = (p * (dp - jnp.sum(p * dp, axis=0, keepdims=True))).astype(BF)
            dv = dv + mm(p.astype(BF), doh[cols])
            dk = dk + mm(ds, qh[cols])
            dqs[b].append(mm(kt[h * HEAD_DIM : (h + 1) * HEAD_DIM], ds) * scale)
    dq = jnp.concatenate([jnp.concatenate(d, axis=0).T for d in dqs], axis=0)
    for i, g in enumerate((dq, dk, dv)):
        at = pl.multiple_of(i * model + j * width, width)
        dqkv_ref[:, pl.ds(at, width)] = g.astype(BF)

    @pl.when(j == pairs - 1)
    def _():
        tile = 256
        lowt_ref[...] = low_ref[...].reshape(seq, model).T
        first_ref[...] = jnp.zeros_like(first_ref)

        @pl.when(r == 0)
        def _():
            acc_ref[...] = jnp.zeros_like(acc_ref)
            table_ref[...] = jnp.zeros_like(table_ref)

        def piece(n, carry):
            cols = pl.ds(pl.multiple_of(n * tile, tile), tile)
            part = dqkv_ref[:, cols]
            acc_ref[:, cols] += mm(lowt_ref[...], part)
            first_ref[...] += mm_nt(part, w_ref[:, cols])
            return carry

        lax.fori_loop(0, 3 * model // tile, piece, 0)
        for h in range(sub):
            grad = first_ref[h * length : (h + 1) * length, :]
            vision = col_ref[h, 0] > 0.5
            z, rstd = norm(tok_ref[h, 0].astype(F32))
            gain = jnp.where(vision, gain_ref[1:2], gain_ref[0:1])
            for i, term in enumerate((grad * z, grad)):
                for e, part in enumerate((jnp.where(vision, 0.0, term), jnp.where(vision, term, 0.0))):
                    at = 2 * i + e
                    table_ref[at : at + 1, :] += jnp.sum(part, axis=0, keepdims=True)
            tail = (extra_ref[h, 0] + norm_back(grad, gain, z, rstd)).astype(BF)

            @pl.when(r < early)
            def _(h=h, tail=tail):
                rows_ref[h, jnp.minimum(r, early - 1)] = tail

            @pl.when(r == early)
            def _(h=h, tail=tail):
                tail_ref[h, 0] = tail

        for i in range(early):

            @pl.when(r == i)
            def _(i=i):
                for copy in homes[i]:
                    copy.start()

    @pl.when((r == rows - 1) & (j == pairs - 1))
    def _():
        height = in_ref.shape[1]
        for p in range(in_ref.shape[0]):
            in_ref[p] = acc_ref[p * height : (p + 1) * height, :].astype(BF)
        while not all(stream.done for stream in streams):
            for stream in streams:
                if not stream.done:
                    stream.step()
        for i in range(calls):
            for at in spots(streams[i].result):
                up_ref[(i, *at)] = streams[i].result[at or ...]
        down_ref[...] = streams[-1].result[...]
        for copy in [*stays, *moves, *sum(homes, [])]:
            copy.wait()
        for stream in streams:
            stream.close()


def attention_backward(
    segment, qkv, grad, lse, low, weight, tok, extra, col, gain, up_kept, up_came, down_kept, down_came, leaving, dp_bits
):
    sub, rows, length, wide = qkv.shape
    seq = sub * length
    model = wide // 3
    pairs = model // 128
    groups = 1 << dp_bits
    calls = len(up_kept)
    part = attn_specs(sub, length, pairs)
    per, high = model // groups, down_kept[0].shape[2]
    row = pl.BlockSpec((sub, 1, length, model), lambda r, j: (0, r, 0, 0))
    hbm = pl.BlockSpec(memory_space=pl.ANY)

    def fixed(*shape):
        return pl.BlockSpec(shape, lambda r, j: (0,) * len(shape), pipeline_mode=pl.Buffered(1))

    up_kept, up_came = (
        [k.reshape((2,) * dp_bits + (per, model)) for k in ks] for ks in (up_kept, up_came)
    )
    ups, downs = up_order(dp_bits), down_order(dp_bits)
    scratch = [
        s
        for _ in range(calls)
        for s in [pltpu.VMEM((2,) * dp_bits + (per, model), BF)] * 2
        + [pltpu.VMEM((2,) * (dp_bits - 1 - i) + (per, model), BF) for i in range(2)]
    ]
    scratch += stream_scratch(downs, (high, model), True)
    sems = 2 * calls + len(downs) + 3 * rows
    loads = 2 * calls + 2 * calls * (groups // 8) + rows
    up_tail = (calls,) + (2,) * (dp_bits - 2) + (per, model)
    return pl.pallas_call(
        functools.partial(attn_bwd_kernel, calls, dp_bits),
        grid=(rows, pairs),
        in_specs=[
            pl.BlockSpec((1, seq, 1), lambda r, j: (r, 0, 0)),
            pl.BlockSpec((1, 1, seq), lambda r, j: (r, 0, 0)),
            part(0),
            part(1),
            part(2),
            part(0),
            pl.BlockSpec((1, 1, 2, seq), lambda r, j: (r, j, 0, 0)),
            row,
            fixed(*weight.shape),
            row,
            row,
            pl.BlockSpec((sub, 1, length, 1), lambda r, j: (0, r, 0, 0)),
            fixed(*gain.shape),
        ]
        + [hbm] * (4 * calls + 1),
        out_specs=[
            fixed(groups, per, wide), fixed(4, model), fixed(sub, 1, length, model),
            fixed(*up_tail), fixed(high, model), hbm, hbm,
        ],
        out_shape=[
            jax.ShapeDtypeStruct((groups, per, wide), BF),
            jax.ShapeDtypeStruct((4, model), F32),
            jax.ShapeDtypeStruct((sub, 1, length, model), BF),
            jax.ShapeDtypeStruct(up_tail, BF),
            jax.ShapeDtypeStruct((high, model), BF),
            jax.ShapeDtypeStruct(leaving.shape, BF),
            jax.ShapeDtypeStruct((sub, rows - 1, length, model), BF),
        ],
        scratch_shapes=[
            pltpu.VMEM((seq, seq), F32),
            pltpu.VMEM((seq, wide), BF),
            pltpu.VMEM((model, seq), BF),
            pltpu.VMEM((model, wide), F32),
            pltpu.VMEM((seq, model), F32),
            pltpu.VMEM((sub, rows - 1, length, model), BF),
        ]
        + scratch
        + [
            pltpu.SemaphoreType.DMA((sems,)),
            pltpu.SemaphoreType.DMA((sems,)),
            pltpu.SemaphoreType.DMA((loads,)),
        ],
        compiler_params=pltpu.CompilerParams(
            collective_id=1, has_side_effects=True, vmem_limit_bytes=VMEM_BYTES
        ),
        cost_estimate=pl.CostEstimate(
            flops=20 * rows * seq * seq * model + 4 * rows * seq * model * wide,
            bytes_accessed=100 * 1024 * 1024,
            transcendentals=rows * seq * seq * model // HEAD_DIM,
        ),
        name="attn_bwd",
    )(
        segment[:, :, None], segment[:, None, :], qkv, qkv, qkv, grad, lse, low, weight,
        tok, extra, col, gain,
        *up_kept, *up_came, *down_kept, *down_came, leaving,
    )


def finish_kernel(calls, dp_bits, *refs):
    refs = list(refs)
    up_ref, in_ref, out_ref = draw(refs, 3)
    tables = draw(refs, 3)
    last_ref, rows_ref, att_ref, up_out, down_ref, table_ref, home_ref = draw(refs, 7)
    env = peers()
    copies = Copies(*refs[-3:])
    remote = copies.remote
    core, x = env["head", 0][0], env["head", 1][0]
    me = lax.axis_index("head")
    groups = 1 << dp_bits
    model = home_ref.shape[-1]
    x_partner, core_partner = env["head", 1][1], env["head", 0][1]

    streams, loads = [], []
    for half, order in enumerate(attention_orders(dp_bits)):
        buf, *gots = draw(refs, 1 + len(order))
        loads.append([])
        lanes = buf.shape[-1]
        for i in range(4):
            ref, start = (out_ref, 0) if i == 3 else (in_ref, i * model)
            for p in range(groups):
                spot_of = {("head", 0): i >> 1, ("head", 1): i & 1}
                spot_of.update({("dp", b): p >> b & 1 for b in range(dp_bits)})
                cols = pl.ds(start + half * lanes, lanes)
                loads[-1].append(
                    copies.local(ref.at[p, :, cols], buf.at[tuple(spot_of[o] for o in order)])
                )
        streams.append(Halving(env, order, buf, gots, None, remote))
    order = up_order(dp_bits)[2:]
    for i in range(calls):
        buf, *gots = draw(refs, 1 + len(order))
        loads.append([copies.local(up_ref.at[i], buf)])
        streams.append(Halving(env, order, buf, gots, None, remote))
    (last_got,) = draw(refs, 1)
    sbuf, *sgots = draw(refs, 3 + dp_bits)

    for group in loads:
        for copy in group:
            copy.start()
    moves = []
    for o in range(1, 4):
        to = (me // 4) * 4 + flipped(me % 4, o)
        moves.append(remote(rows_ref.at[to], home_ref.at[me], {"head": to}))

    top, beyond = env["dp", dp_bits - 1]
    here, over = down_ref.at[x], down_ref.at[1 - x]
    last = remote(last_ref, last_got, beyond)
    to_x, to_core = remote(here, here, x_partner), remote(here, here, core_partner)
    forward = remote(over, over, core_partner)
    greet(env)

    for copy in moves:
        copy.start()

    @pl.when(top != core)
    def _():
        last.start()

    for i, (stream, group) in enumerate(zip(streams, loads)):
        for copy in group:
            copy.wait()
        if i < 2:
            stream.send()

    for at, ref in zip((0, 4, 6), tables):
        sbuf[at : at + ref.shape[0], :] = ref[...]
    sorder = [("head", 0), ("head", 1)] + [("dp", b) for b in range(dp_bits)]
    scopies = [remote(sbuf, got, env[o][1]) for o, got in zip(sorder, sgots)]
    scopies[0].start()
    home_ref[me] = rows_ref[me]

    gathers, after = [], []

    def spread(place, value):
        mine = place(x)
        mine[...] = value[...]
        for to, where in ((x_partner, after), (core_partner, gathers)):
            copy = remote(mine, mine, to)
            copy.start()
            where.append((copy, place))

    def att_place(half, side):
        at = (2 * core + side) * model + half * (model // 2)
        return att_ref.at[:, pl.ds(pl.multiple_of(at, 128), model // 2)]

    def up_place(call, side):
        at = (core * calls + call) * model
        return up_out.at[side, :, pl.ds(pl.multiple_of(at, 128), model)]

    rounds = max(len(sorder), max(len(stream.rounds) for stream in streams))
    for r in range(rounds):
        for i, stream in enumerate(streams):
            if not stream.done and (i < 2 or r >= 3):
                stream.step()
                if stream.done:
                    if i < 2:
                        spread(functools.partial(att_place, i), stream.result)
                    else:
                        spread(functools.partial(up_place, i - 2), stream.result)
        if r < len(sorder):
            scopies[r].wait()
            sbuf[...] = sbuf[...] + sgots[r][...]
            if r + 1 < len(sorder):
                scopies[r + 1].start()
        if r == 1:
            for stream in streams[2:]:
                stream.send()
        if r == 1:

            @pl.when(top == core)
            def _():
                last.wait_recv()
                here[...] = last_ref[...] + last_got[...]
                to_x.start()
                to_core.start()

    table_ref[...] = sbuf[...]
    forwards = []
    for copy, place in after:
        copy.wait_recv()
        other = place(1 - x)
        forwards.append(remote(other, other, core_partner))
        forwards[-1].start()

    @pl.when(top == core)
    def _():
        to_x.wait_recv()
        forward.start()
        to_core.wait_send()
        to_x.wait_send()
        forward.wait_send()

    @pl.when(top != core)
    def _():
        last.wait_send()
        to_core.wait_recv()
        forward.wait_recv()

    for copy, _ in gathers:
        copy.wait()
    for copy in forwards:
        copy.wait()
    for copy, _ in after:
        copy.wait_send()
    for stream in streams:
        stream.close()
    for copy in moves:
        copy.wait()


def flipped(index, offset):
    low, high = index % 2, index // 2
    if offset & 1:
        low = 1 - low
    if offset & 2:
        high = 1 - high
    return 2 * high + low


def finish(dp_bits, up, down, in_term, out_term, tables, rows):
    assert rows.shape[0] == 4
    calls = up.shape[0]
    groups, per, model = out_term.shape
    high = down.shape[0]
    orders = attention_orders(dp_bits)
    ups = up_order(dp_bits)[2:]
    scratch = [s for o in orders for s in stream_scratch(o, (per, model // 2), False)]
    scratch += [s for _ in range(calls) for s in stream_scratch(ups, (per, model), False)]
    scratch.append(pltpu.VMEM((high, model), BF))
    scratch += [pltpu.VMEM((8, model), F32)] * (3 + dp_bits)
    sems = sum(map(len, orders)) + calls * len(ups) + 3 + 4 + 2 + dp_bits + 3 * (calls + 2)
    loads = 2 * 4 * groups + calls
    hbm = pl.BlockSpec(memory_space=pl.ANY)
    vmem = pl.BlockSpec(memory_space=pltpu.VMEM)
    return pl.pallas_call(
        functools.partial(finish_kernel, calls, dp_bits),
        in_specs=[hbm] * 3 + [vmem] * 5,
        out_specs=[vmem] * 5,
        out_shape=[
            jax.ShapeDtypeStruct((per, 4 * model), BF),
            jax.ShapeDtypeStruct((2, per, 2 * calls * model), BF),
            jax.ShapeDtypeStruct((2, high, model), BF),
            jax.ShapeDtypeStruct((8, model), F32),
            jax.ShapeDtypeStruct(rows.shape, BF),
        ],
        scratch_shapes=scratch
        + [
            pltpu.SemaphoreType.DMA((sems,)),
            pltpu.SemaphoreType.DMA((sems,)),
            pltpu.SemaphoreType.DMA((loads,)),
        ],
        compiler_params=pltpu.CompilerParams(
            collective_id=0, has_side_effects=True, vmem_limit_bytes=VMEM_BYTES
        ),
        cost_estimate=pl.CostEstimate(
            flops=0, bytes_accessed=100 * 1024 * 1024, transcendentals=0
        ),
        name="finish",
    )(up, in_term, out_term, *tables, down, rows)


def enter_kernel(tokens_ref, cot_ref, modality_ref, gain_ref, shift_ref, w_ref, *refs):
    refs = list(refs)
    tok_ref, kind_ref, col_ref, low_ref, low_cot_ref, qkv_out = draw(refs, 6)
    wide_ref, send_ref, cot_wide, qkv_ref = draw(refs, 4)
    copies = Copies(*refs)
    me = lax.axis_index("head")
    heads, rows, length, model = tok_ref.shape
    core = me % 2
    targets = others()
    loads = {
        (o, r): copies.local(tokens_ref.at[to, r], wide_ref.at[to, r])
        for r in range(rows)
        for o, to in enumerate([*targets, me])
    }
    kinds = [copies.remote(modality_ref.at[to // 2], kind_ref.at[me], {"head": to}) for to in targets]
    sends = {
        (o, r): copies.remote(send_ref.at[to, r], tok_ref.at[me, r], {"head": to})
        for r in range(rows)
        for o, to in enumerate(targets)
    }
    cot_load = copies.local(cot_ref, cot_wide)
    for copy in loads.values():
        copy.start()
    cot_load.start()
    barrier = pltpu.get_barrier_semaphore()
    for to in targets:
        pl.semaphore_signal(
            barrier, inc=1, device_id={"head": to}, device_id_type=pl.DeviceIdType.MESH
        )
    pl.semaphore_wait(barrier, len(targets))
    for copy in kinds:
        copy.start()
    kind_ref[me] = modality_ref[me // 2]
    for r in range(rows):
        for o, to in enumerate(targets):
            loads[o, r].wait()
            send_ref[to, r] = wide_ref[to, r].astype(BF)
            sends[o, r].start()
        loads[len(targets), r].wait()
        tok_ref[me, r] = wide_ref[me, r].astype(BF)
    for copy in kinds:
        copy.wait()
    ones = jnp.ones((8, length), BF)
    row = lax.broadcasted_iota(jnp.int32, (8, length), 0)
    cot_load.wait()
    low_cot_ref[...] = cot_wide[...].astype(BF)
    leaves = []
    for r in range(rows):
        for group in ((3, 2), (1, 0)):
            lows = []
            for o in group:
                h = [*targets, me][o]
                if o < len(targets):
                    sends[o, r].wait_recv()
                kind = kind_ref[h, core, r : r + 1, :].astype(F32)
                kind = jnp.where(row == 0, jnp.broadcast_to(kind, (8, length)), 0.0).astype(BF)
                kind = mm_tn(kind, ones)[:, :1]
                col_ref[h, r] = kind
                z, _ = norm(tok_ref[h, r].astype(F32))
                low = z * jnp.where(kind < 0.5, gain_ref[0:1], gain_ref[1:2])
                low = (low + jnp.where(kind < 0.5, shift_ref[0:1], shift_ref[1:2])).astype(BF)
                low_ref[h, r] = low
                lows.append(low)
            low = jnp.concatenate(lows, axis=0)
            for n in range(w_ref.shape[1] // model):
                cols = slice(n * model, (n + 1) * model)
                part = mm(low, w_ref[:, cols]).astype(BF)
                for i, o in enumerate(group):
                    qkv_ref[[*targets, me][o], r, :, cols] = part[i * length : (i + 1) * length]
            for o in group:
                h = [*targets, me][o]
                leaves.append(copies.local(qkv_ref.at[h, r], qkv_out.at[h, r]))
                leaves[-1].start()
    for copy in leaves:
        copy.wait()
    for copy in sends.values():
        copy.wait_send()


def enter(tokens, cotangent, modality, gain, shift, weight):
    heads, rows, _, model = tokens.shape
    assert heads == 4
    vmem = pl.BlockSpec(memory_space=pltpu.VMEM)
    hbm = pl.BlockSpec(memory_space=pl.ANY)
    sems = 3 * rows + 3
    return pl.pallas_call(
        enter_kernel,
        in_specs=[hbm] * 2 + [vmem] * 4,
        out_specs=[vmem] * 5 + [hbm],
        out_shape=[
            jax.ShapeDtypeStruct(tokens.shape, BF),
            jax.ShapeDtypeStruct((heads,) + modality.shape[1:], jnp.int32),
            jax.ShapeDtypeStruct(tokens.shape[:3] + (1,), F32),
            jax.ShapeDtypeStruct(tokens.shape, BF),
            jax.ShapeDtypeStruct(tokens.shape, BF),
            jax.ShapeDtypeStruct(tokens.shape[:3] + weight.shape[1:], BF),
        ],
        scratch_shapes=[
            pltpu.VMEM(tokens.shape, F32),
            pltpu.VMEM(tokens.shape, BF),
            pltpu.VMEM(tokens.shape, F32),
            pltpu.VMEM(tokens.shape[:3] + weight.shape[1:], BF),
            pltpu.SemaphoreType.DMA((sems,)),
            pltpu.SemaphoreType.DMA((sems,)),
            pltpu.SemaphoreType.DMA((8 * rows + 1,)),
        ],
        compiler_params=pltpu.CompilerParams(
            collective_id=2, has_side_effects=True, vmem_limit_bytes=VMEM_BYTES
        ),
        cost_estimate=pl.CostEstimate(
            flops=2 * tokens.size * weight.shape[1], bytes_accessed=40 * 1024 * 1024,
            transcendentals=0,
        ),
        name="enter",
    )(tokens, cotangent, modality, gain, shift, weight)


def norm(values):
    mean = jnp.mean(values, axis=-1, keepdims=True)
    centered = values - mean
    rstd = lax.rsqrt(jnp.mean(centered * centered, axis=-1, keepdims=True) + EPS)
    return centered * rstd, rstd


def pick(table, kind):
    return jnp.where(kind == 0, table[0], table[1])


def norm_back(grad, gains, z, rstd):
    q = grad * gains
    return rstd * (
        q
        - jnp.mean(q, axis=-1, keepdims=True)
        - z * jnp.mean(q * z, axis=-1, keepdims=True)
    )


def by_expert(values, kind):
    first = jnp.sum(jnp.where(kind == 0, values, 0.0), axis=0)
    second = jnp.sum(jnp.where(kind == 0, 0.0, values), axis=0)
    return jnp.stack([first, second])


def flip(axis, size, bit):
    return functools.partial(
        lax.ppermute, axis_name=axis, perm=[(i, i ^ (1 << bit)) for i in range(size)]
    )


def take(values, dim, index):
    return lax.dynamic_index_in_dim(values, index, dim, keepdims=False)


def body(sizes, tokens, segment, modality, first_gain, first_shift, project_in, project_out,
         second_gain, second_shift, up_weight, down_weight, cotangent):
    heads, groups = sizes["head"], sizes["dp"]
    row_count, length, model = tokens.shape
    rows = row_count // heads
    count = row_count * length
    hidden = up_weight.shape[-1]
    me_h, me_d = lax.axis_index("head"), lax.axis_index("dp")
    core = me_h % 2
    head_bits = heads.bit_length() - 1
    dp_bits = groups.bit_length() - 1
    assert heads == 1 << head_bits and groups == 1 << dp_bits and head_bits >= 2
    hflip = [flip("head", heads, b) for b in range(head_bits)]
    dflip = [flip("dp", groups, b) for b in range(dp_bits)]

    grid = (heads, rows, length)
    tok, kinds, col, low1, low_cot, qkv = enter(
        tokens.reshape(*grid, model), cotangent.reshape(*grid, model), modality.reshape(heads // 2, 2, rows, length),
        first_gain, first_shift, project_in,
    )
    seg = lax.dynamic_slice_in_dim(segment, me_h * rows, rows, 0)
    kind = take(kinds, 1, core).reshape(count)
    kcol = col.reshape(count, 1)

    flat = tok.astype(F32).reshape(count, model)
    context, lse, cot = attention_forward(seg, qkv, low_cot)
    cot = cot.reshape(count, model)
    ctx = context.reshape(count, model)
    attention = mm(ctx, project_out)
    residual = flat + attention
    z2, rstd2 = norm(residual)
    gain2 = pick(second_gain, kcol)
    low2 = (z2 * gain2 + pick(second_shift, kcol)).astype(BF)

    slots = count + BLK
    is0 = (kind == 0).astype(F32).reshape(count // BLK, BLK)
    tri = jnp.triu(jnp.ones((BLK, BLK), F32))
    inner = mm(is0, tri)
    ends = jnp.cumsum(inner[:, -1])
    before = (inner + (ends - inner[:, -1])[:, None]).reshape(count).astype(jnp.int32)
    n0 = ends[-1].astype(jnp.int32)
    blocks0 = (n0 + BLK - 1) // BLK
    blocks1 = (count - n0 + BLK - 1) // BLK
    rank1 = jnp.arange(count, dtype=jnp.int32) - before
    slot = jnp.where(kind == 0, before - 1, blocks0 * BLK + rank1)
    place = (slot[None, :] == jnp.arange(slots, dtype=jnp.int32)[:, None]).astype(BF)

    near = hflip[0]
    g_mine = mm(place, cot).astype(BF)
    g_other = near(g_mine)
    zeros = jnp.sum(kinds == 0, axis=(0, 2, 3))
    full = jnp.stack([(zeros + BLK - 1) // BLK, (count - zeros + BLK - 1) // BLK], axis=1)
    blocks, blocks_other = take(full, 0, core), take(full, 0, 1 - core)
    xbit = (me_h // 2) % 2
    ybit = me_d % 2
    info = jnp.concatenate([blocks, blocks_other, jnp.stack([xbit, ybit, core])]).astype(jnp.int32)
    x_mine = mm(place, low2).astype(BF)
    x_other = near(x_mine)

    partial, kept, came = None, ([], []), ([], [])
    for call in range(CALLS):
        *partial, up_keep, up_send, down_keep, down_send = ffn(
            call, info, x_mine, x_other, g_mine, g_other, up_weight, down_weight, partial, groups
        )
        kept[0].append(up_keep)
        kept[1].append(down_keep)
        came[0].append(hflip[1](up_send))
        came[1].append(dflip[0](down_send))

    partial, early = lax.optimization_barrier((partial, [c[:-1] for c in came]))
    came = [e + c[-1:] for e, c in zip(early, came)]
    branch_mine, branch_other, dx_mine, dx_other = partial
    dx = dx_mine + near(dx_other)
    second_grad = mm_tn(place, dx)
    branch = mm_tn(place, branch_mine + near(branch_other))
    leaving = (attention + branch).astype(BF).reshape(*grid, model)

    cot32 = cot.astype(F32)
    gain2_term = by_expert(second_grad * z2, kcol)
    shift2_term = by_expert(second_grad, kcol)
    extra = norm_back(second_grad, gain2, z2, rstd2)
    attention_low = (cot32 + extra).astype(BF)
    out_term = mm_tn(ctx, attention_low)
    context_grad = mm_nt(attention_low, project_out).astype(BF)
    in_term, table1, tail, up_sum, down_sum, back, home0 = attention_backward(
        seg, qkv, context_grad.reshape(context.shape), lse, low1, project_in,
        tok, extra.reshape(*grid, model), col, first_gain,
        kept[0], came[0], kept[1], came[1], leaving, dp_bits,
    )
    output = tokens + back.reshape(row_count, length, model).astype(F32)
    att_sum, up_sum, down_sum, table, home = finish(
        dp_bits, up_sum, down_sum, in_term,
        out_term.astype(BF).reshape(groups, model // groups, model),
        (table1, gain2_term, shift2_term), tail,
    )
    home = jnp.concatenate([home0, home], axis=1)
    input_grad = cotangent + home.reshape(row_count, length, model).astype(F32)

    up_grad, down_grad = up_sum.astype(F32), down_sum.astype(F32)
    in_grad = att_sum[:, : 3 * model].astype(F32)
    out_grad = att_sum[:, 3 * model :].astype(F32)
    tables = lax.dynamic_slice_in_dim(table, me_d * (model // groups), model // groups, 1)
    tables = tables.reshape(4, EXPERTS, model // groups)
    return (
        output, input_grad, tables[0], tables[1], in_grad, out_grad, tables[2], tables[3],
        up_grad, down_grad,
    )


def solution(mesh):
    return jax.shard_map(
        functools.partial(body, dict(mesh.shape)),
        mesh=mesh,
        in_specs=(
            P("dp", "head", None),
            P("dp", None),
            P("dp", "head"),
            P(),
            P(),
            P(),
            P(),
            P(),
            P(),
            P(),
            P(),
            P("dp", "head", None),
        ),
        out_specs=(
            P("dp", "head", None),
            P("dp", "head", None),
            P(None, "dp"),
            P(None, "dp"),
            P("dp", None),
            P("dp", None),
            P(None, "dp"),
            P(None, "dp"),
            P(None, "dp", None),
            P(None, "dp", None),
        ),
        check_vma=False,
    )
```
